128 devices in a mesh: req: 16 (over z, y), mp: 8 (over x, core).
Axes of the slice: x: 4, y: 4, z: 4, core: 2. Of those that a mesh axis runs over, the one named last changes fastest.
Arguments:
- q_pre: bfloat16 [8192, 3072], P('req', 'mp'), may hold values from -64 to 64
- k_pre: bfloat16 [8192, 1024], P('req', 'mp'), may hold values from -64 to 64
- v_pre: bfloat16 [8192, 1024], P('req', 'mp'), may hold values from -12 to 12
- q_bias: float32 [3072], P('mp'), may hold values from -3 to 3
- k_bias: float32 [1024], P('mp'), may hold values from -3 to 3
- v_bias: float32 [1024], P('mp'), may hold values from -3 to 3
- segment_ids: int32 [8192], P('req'), may hold values from -1 to 63, as said below
- lengths: int32 [16, 4], replicated, may hold values from 64 to 128, as said below
- page_table: int32 [16, 4], replicated, may hold values from 0 to 63, as said below
- w_out: bfloat16 [3072, 5120], P('mp'), may hold values from -0.109375 to 0.109375
- residual: bfloat16 [8192, 5120], P('req'), may hold values from -4 to 4
- norm_gain: float32 [5120], replicated, may hold values from 0.1 to 1.9
- w_gate: bfloat16 [5120, 6912], P('req', 'mp'), may hold values from -0.078125 to 0.078125
- w_up: bfloat16 [5120, 6912], P('req', 'mp'), may hold values from -0.078125 to 0.078125
Outputs:
- hidden: bfloat16 [8192, 6912], P('req', 'mp')
- kv_cache: bfloat16 [64, 8, 128, 256], P('req', 'mp')
The draws below stay inside these ranges and needn't reach their ends.
Inputs may be any that keep to these rules, and one draw needn't show every extreme that they name: Requests of block r lie in order from the block's first token, request j taking lengths[r, j] tokens; in every block one request has exactly 128 tokens. `segment_ids`: token t of block r carries r * 4 + j inside request j's run of tokens given by lengths, and -1 after the last request of its block. `page_table`: every page is named once; page p is held by req index p // 4; the requests of one block have pages held by different req indices.
All inputs are finite; a program needn't handle non-finite values.
Results may differ from the reference program's by a relative error of at most 0.019.
Values may be sent and summed in bfloat16 or wider, within the bound.
A program may use at most 128 MiB of HBM per device.

```python
import math
import jax
import jax.numpy as jnp
from jax import lax

D = 5120
KVH = 8
HD = 128
QH = 24
FF = 6912
PAGE = 128
REQS = 4
BLOCK = 512
TOKENS = 8192
PAGES = 64
N_REQ = 16
N_MP = 8


def layout(key):
    base = jax.random.fold_in(key, 5)
    key_len = jax.random.fold_in(base, 0)
    key_long = jax.random.fold_in(base, 1)
    key_owner = jax.random.fold_in(base, 3)
    key_slot = jax.random.fold_in(base, 4)
    length_table = jax.random.randint(key_len, (N_REQ, REQS), PAGE // 2, PAGE + 1)
    longest = jax.random.randint(key_long, (N_REQ, 1), 0, REQS)
    length_table = jnp.where(jnp.arange(REQS)[None, :] == longest, PAGE, length_table).astype(jnp.int32)
    owner_order = jax.random.permutation(key_owner, N_REQ)
    owner_ids = owner_order[(jnp.arange(N_REQ)[:, None] + jnp.arange(REQS)[None, :]) % N_REQ]
    rotation = jax.random.randint(key_slot, (N_REQ,), 0, REQS)
    slot_ids = (jnp.arange(REQS)[None, :] + rotation[owner_ids]) % REQS
    page_ids = (owner_ids * REQS + slot_ids).astype(jnp.int32)
    return (length_table, page_ids)


def draw_lengths(key, part):
    return layout(key)[0]


def draw_page_table(key, part):
    return layout(key)[1]


def draw_segment_ids(key, part):
    length_table = layout(key)[0]
    starts = jnp.cumsum(length_table, axis=1) - length_table
    row_ids = jnp.arange(BLOCK)[None, :, None]
    inside = (row_ids >= starts[:, None, :]) & (row_ids < (starts + length_table)[:, None, :])
    request_ids = jnp.arange(N_REQ)[:, None, None] * REQS + jnp.arange(REQS)[None, None, :]
    segment = jnp.max(jnp.where(inside, request_ids, -1), axis=2)
    return segment.reshape(TOKENS).astype(jnp.int32)


def fields(key):
    base = jax.random.fold_in(key, 9)
    key_query, key_key = jax.random.split(base, 2)
    queries = jax.random.normal(key_query, (TOKENS, QH * HD), jnp.float32)
    keys = jax.random.normal(key_key, (TOKENS, KVH * HD), jnp.float32)
    return (queries, keys)


def draw_q_pre(key, part):
    return fields(key)[0].astype(jnp.bfloat16)


def draw_k_pre(key, part):
    return fields(key)[1].astype(jnp.bfloat16)


def steps_of(key, shape, shards, least, largest):
    def one(dim, shards_of):
        heights = jax.random.uniform(jax.random.fold_in(jax.random.fold_in(key, 6), dim), (shards_of,), jnp.float32, least / len(shards), largest / len(shards))
        return jnp.repeat(jnp.exp(heights), shape[dim] // shards_of).reshape((-1,) + (1,) * (len(shape) - dim - 1))

    gain = one(*shards[0])
    for cut in shards[1:]:
        gain = gain * one(*cut)
    return gain


def centred(rng, extent, deviation, reach, shards=(), kind=jnp.bfloat16):
    entries = deviation * jax.random.normal(rng, extent, jnp.float32)
    if shards:
        entries = entries * steps_of(rng, extent, shards, -0.22, 0.18)
    return jnp.clip(entries, -reach, reach).astype(kind)


def setup_inputs(seed: int = 0) -> dict:
    splits = jax.random.split(jax.random.key(seed), 15)
    q_pre = draw_q_pre(jax.random.fold_in(splits[14], 71), 0)
    k_pre = draw_k_pre(jax.random.fold_in(splits[14], 71), 0)
    v_pre = centred(splits[2], (TOKENS, KVH * HD), 2.0, 12.0, ((0, 16), (1, 8)))
    q_bias = centred(splits[3], (QH * HD,), 0.5, 3.0, ((0, 8),), jnp.float32)
    k_bias = centred(splits[4], (KVH * HD,), 0.5, 3.0, ((0, 8),), jnp.float32)
    v_bias = centred(splits[5], (KVH * HD,), 0.5, 3.0, ((0, 8),), jnp.float32)
    segment_ids = draw_segment_ids(jax.random.fold_in(splits[14], 71), 0)
    lengths = draw_lengths(jax.random.fold_in(splits[14], 71), 0)
    page_table = draw_page_table(jax.random.fold_in(splits[14], 71), 0)
    w_out = centred(splits[9], (QH * HD, D), (QH * HD) ** -0.5, 0.109375, ((0, 8),))
    residual = centred(splits[10], (TOKENS, D), 0.5, 4.0, ((0, 16),))
    norm_gain = jnp.clip(1.0 + 0.18 * jax.random.normal(splits[11], (D,), jnp.float32), 0.1, 1.9)
    w_gate = centred(splits[12], (D, FF), D ** -0.5, 0.078125, ((0, 16), (1, 8)))
    w_up = centred(splits[13], (D, FF), D ** -0.5, 0.078125, ((0, 16), (1, 8)))
    return {"q_pre": q_pre, "k_pre": k_pre, "v_pre": v_pre, "q_bias": q_bias, "k_bias": k_bias, "v_bias": v_bias, "segment_ids": segment_ids, "lengths": lengths, "page_table": page_table, "w_out": w_out, "residual": residual, "norm_gain": norm_gain, "w_gate": w_gate, "w_up": w_up}


THETA = 1000000.0
EPS = 1e-06

def rotate(values, positions):
    half_dim = values.shape[-1] // 2
    frequencies = THETA ** (-jnp.arange(half_dim, dtype=jnp.float32) * (2.0 / values.shape[-1]))
    angles = positions[:, None] * frequencies[None, :]
    cosine = jnp.cos(angles)[:, None, :]
    sine_part = jnp.sin(angles)[:, None, :]
    first_half = values[..., :half_dim]
    second = values[..., half_dim:]
    return jnp.concatenate([first_half * cosine - second * sine_part, second * cosine + first_half * sine_part], axis=-1)

def reference(q_pre, k_pre, v_pre, q_bias, k_bias, v_bias, segment_ids, lengths, page_table, w_out, residual, norm_gain, w_gate, w_up):
    group_size = QH // KVH
    head_cols = QH * HD // N_MP
    scale_factor = 1.0 / math.sqrt(HD)

    def one_block(inputs):
        block_idx, q_rows, k_rows, v_rows, seg_rows, lens_row, resid_rows = inputs
        starts = jnp.cumsum(lens_row) - lens_row
        alive_rows = seg_rows >= 0
        req_idx = jnp.clip(seg_rows - block_idx * REQS, 0, REQS - 1).astype(jnp.int32)
        positions = (jnp.arange(BLOCK, dtype=jnp.int32) - jnp.take(starts, req_idx)).astype(jnp.float32)
        queries = rotate((q_rows.astype(jnp.float32) + q_bias).reshape(BLOCK, QH, HD), positions)
        queries = jnp.where(alive_rows[:, None, None], queries, 0.0).astype(jnp.bfloat16)
        keyrot = rotate((k_rows.astype(jnp.float32) + k_bias).reshape(BLOCK, KVH, HD), positions)
        keyrot = jnp.where(alive_rows[:, None, None], keyrot, 0.0).astype(jnp.bfloat16)
        valrows = (v_rows.astype(jnp.float32) + v_bias).reshape(BLOCK, KVH, HD)
        valrows = jnp.where(alive_rows[:, None, None], valrows, 0.0).astype(jnp.bfloat16)
        scores = jnp.einsum('qhge,khe->hgqk', queries.reshape(BLOCK, KVH, group_size, HD).astype(jnp.float32), keyrot.astype(jnp.float32)) * scale_factor
        allowed = (seg_rows[:, None] == seg_rows[None, :]) & alive_rows[None, :] & (positions[None, :] <= positions[:, None])
        allowed = allowed[None, None]
        row_max = lax.optimization_barrier(jnp.max(jnp.where(allowed, scores, -1e+30), axis=-1, keepdims=True))
        weights = jnp.where(allowed, jnp.exp(scores - row_max), 0.0)
        row_sum = lax.optimization_barrier(jnp.sum(weights, axis=-1, keepdims=True))
        present = alive_rows[None, None, :, None]
        row_probs = jnp.where(present, weights / jnp.where(present, row_sum, 1.0), 0.0).astype(jnp.bfloat16)
        attended = jnp.einsum('hgqk,khe->qhge', row_probs.astype(jnp.float32), valrows.astype(jnp.float32)).astype(jnp.bfloat16).reshape(BLOCK, QH * HD)
        summed = jnp.zeros((BLOCK, D), jnp.float32)
        for member in range(N_MP):
            product = jnp.dot(attended[:, member * head_cols:(member + 1) * head_cols], w_out[member * head_cols:(member + 1) * head_cols], preferred_element_type=jnp.float32)
            summed = summed + lax.optimization_barrier(product.astype(jnp.bfloat16)).astype(jnp.float32)
        state = resid_rows.astype(jnp.float32) + summed
        normed = (state * lax.rsqrt(lax.optimization_barrier(jnp.mean(state * state, axis=-1, keepdims=True)) + EPS) * norm_gain).astype(jnp.bfloat16)
        gate_acc = jnp.dot(normed, w_gate, preferred_element_type=jnp.float32)
        up_acc = jnp.dot(normed, w_up, preferred_element_type=jnp.float32)
        hidden_rows = (jax.nn.silu(gate_acc) * up_acc).astype(jnp.bfloat16)
        row_index = jnp.clip(starts[:, None] + jnp.arange(PAGE, dtype=jnp.int32)[None, :], 0, BLOCK - 1).astype(jnp.int32)
        inside = (jnp.arange(PAGE, dtype=jnp.int32)[None, :] < lens_row[:, None])[:, :, None, None]
        page_keys = jnp.where(inside, keyrot[row_index], jnp.zeros((), jnp.bfloat16))
        page_vals = jnp.where(inside, valrows[row_index], jnp.zeros((), jnp.bfloat16))
        page_rows = jnp.concatenate([page_keys, page_vals], axis=-1).transpose(0, 2, 1, 3)
        return (hidden_rows, page_rows)
    hidden_all, pages_all = lax.map(one_block, (jnp.arange(N_REQ, dtype=jnp.int32), q_pre.reshape(N_REQ, BLOCK, QH * HD), k_pre.reshape(N_REQ, BLOCK, KVH * HD), v_pre.reshape(N_REQ, BLOCK, KVH * HD), segment_ids.reshape(N_REQ, BLOCK), lengths, residual.reshape(N_REQ, BLOCK, D)))
    cache_all = jnp.zeros((PAGES, KVH, PAGE, 2 * HD), jnp.bfloat16)
    cache_all = cache_all.at[page_table.reshape(-1)].set(pages_all.reshape(PAGES, KVH, PAGE, 2 * HD))
    return (hidden_all.reshape(TOKENS, FF), cache_all)
```

```python
import math

import jax
import jax.numpy as jnp
from jax import lax
from jax.sharding import PartitionSpec as P

HD = 128
PAGE = 128
REQS = 4


THETA = 1000000.0
EPS = 1e-06


def rotate(values, positions):
    half_dim = values.shape[-1] // 2
    frequencies = THETA ** (-jnp.arange(half_dim, dtype=jnp.float32) * (2.0 / values.shape[-1]))
    angles = positions[:, None] * frequencies[None, :]
    cosine = jnp.cos(angles)[:, None, :]
    sine_part = jnp.sin(angles)[:, None, :]
    first_half = values[..., :half_dim]
    second = values[..., half_dim:]
    return jnp.concatenate(
        [first_half * cosine - second * sine_part, second * cosine + first_half * sine_part],
        axis=-1,
    )


def normalize(resid_rows, summed, gain_row):
    state = resid_rows.astype(jnp.float32) + summed
    scale_row = lax.rsqrt(jnp.mean(state * state, axis=-1, keepdims=True) + EPS)
    return (state * scale_row * gain_row).astype(jnp.bfloat16)


def shards(
    q_pre,
    k_pre,
    v_pre,
    q_bias,
    k_bias,
    v_bias,
    segment_ids,
    lengths,
    page_table,
    w_out,
    residual,
    norm_gain,
    w_gate,
    w_up,
):
    me_req = lax.axis_index("req")
    groups_all = lax.axis_size("req")
    block_rows = q_pre.shape[0]
    kv_heads = k_pre.shape[1] // HD
    q_heads = q_pre.shape[1] // HD
    group_size = q_heads // kv_heads

    wg_full = lax.all_gather(w_gate, "req", axis=0, tiled=True)
    wu_full = lax.all_gather(w_up, "req", axis=0, tiled=True)

    own_lens = lax.dynamic_index_in_dim(lengths, me_req, 0, keepdims=False)
    own_pages = lax.dynamic_index_in_dim(page_table, me_req, 0, keepdims=False)
    own_owner = own_pages // REQS
    starts = jnp.cumsum(own_lens) - own_lens

    alive = segment_ids >= 0
    req_idx = jnp.clip(segment_ids - me_req * REQS, 0, REQS - 1)
    req_hit = req_idx[:, None] == jnp.arange(REQS)[None, :]
    row_start = jnp.sum(jnp.where(req_hit, starts[None, :], 0), axis=1)
    token = jnp.arange(block_rows, dtype=jnp.int32)
    positions = (token - row_start).astype(jnp.float32)
    keep = alive[:, None, None]

    queries = rotate(
        (q_pre.astype(jnp.float32) + q_bias).reshape(block_rows, q_heads, HD), positions
    )
    queries = jnp.where(keep, queries, 0.0).astype(jnp.bfloat16)
    keys = rotate((k_pre.astype(jnp.float32) + k_bias).reshape(block_rows, kv_heads, HD), positions)
    keys = jnp.where(keep, keys, 0.0).astype(jnp.bfloat16)
    values = (v_pre.astype(jnp.float32) + v_bias).reshape(block_rows, kv_heads, HD)
    values = jnp.where(keep, values, 0.0).astype(jnp.bfloat16)

    scale_factor = 1.0 / math.sqrt(HD)
    q_groups = queries.reshape(block_rows, kv_heads, group_size, HD)
    scores = (
        jnp.einsum("qhge,khe->hgqk", q_groups, keys, preferred_element_type=jnp.float32)
        * scale_factor
    )
    allowed = (
        (segment_ids[:, None] == segment_ids[None, :])
        & alive[None, :]
        & (token[None, :] <= token[:, None])
    )[None, None]
    row_max = jnp.max(jnp.where(allowed, scores, -1e30), axis=-1, keepdims=True)
    weights = jnp.where(allowed, jnp.exp(scores - row_max), 0.0)
    row_sum = jnp.sum(weights, axis=-1, keepdims=True)
    present = alive[None, None, :, None]
    probs = jnp.where(present, weights / jnp.where(present, row_sum, 1.0), 0.0).astype(
        jnp.bfloat16
    )
    attended = jnp.einsum("hgqk,khe->qhge", probs, values, preferred_element_type=jnp.float32)
    attended = attended.astype(jnp.bfloat16).reshape(block_rows, q_heads * HD)

    kv_rows = jnp.concatenate([keys, values], axis=-1)
    kv_rows = jnp.pad(kv_rows, ((0, PAGE), (0, 0), (0, 0)))
    slot = jnp.arange(PAGE, dtype=jnp.int32)
    pages = []
    for j in range(REQS):
        page = lax.dynamic_slice_in_dim(kv_rows, starts[j], PAGE, axis=0)
        page = jnp.where((slot < own_lens[j])[:, None, None], page, jnp.zeros((), jnp.bfloat16))
        pages.append(page)
    pages = jnp.stack(pages)
    to_owner = (own_owner[None, :] == jnp.arange(groups_all)[:, None]).astype(jnp.bfloat16)
    kv_send = jnp.einsum(
        "gj,jphc->gphc", to_owner, pages, preferred_element_type=jnp.float32
    ).astype(jnp.bfloat16)
    kv_in = lax.all_to_all(kv_send, "req", split_axis=0, concat_axis=0, tiled=True)
    hits = (
        page_table[None, :, :] == (me_req * REQS + jnp.arange(REQS, dtype=jnp.int32))[:, None, None]
    )
    page_select = jnp.sum(hits.astype(jnp.int32), axis=2).astype(jnp.bfloat16)
    cache_out = jnp.einsum(
        "ls,sphc->lhpc", page_select, kv_in, preferred_element_type=jnp.float32
    ).astype(jnp.bfloat16)

    summed = lax.psum(
        jnp.dot(attended, w_out, preferred_element_type=jnp.float32).astype(jnp.bfloat16), "mp"
    ).astype(jnp.float32)
    normed = normalize(residual, summed, norm_gain)
    gate_acc = jnp.dot(normed, wg_full, preferred_element_type=jnp.float32)
    up_acc = jnp.dot(normed, wu_full, preferred_element_type=jnp.float32)
    hidden = (jax.nn.silu(gate_acc) * up_acc).astype(jnp.bfloat16)
    return (hidden, cache_out)


def solution(mesh):
    in_specs = (
        P("req", "mp"),
        P("req", "mp"),
        P("req", "mp"),
        P("mp"),
        P("mp"),
        P("mp"),
        P("req"),
        P(),
        P(),
        P("mp", None),
        P("req", None),
        P(),
        P("req", "mp"),
        P("req", "mp"),
    )
    out_specs = (P("req", "mp"), P("req", "mp", None, None))
    return jax.shard_map(shards, mesh=mesh, in_specs=in_specs, out_specs=out_specs, check_vma=False)
```

```python
import math

import jax
import jax.numpy as jnp
from jax import lax
from jax.sharding import PartitionSpec as P

HD = 128
PAGE = 128
REQS = 4
RING = 4


THETA = 1000000.0
EPS = 1e-06


def rotate(values, positions):
    half_dim = values.shape[-1] // 2
    frequencies = THETA ** (-jnp.arange(half_dim, dtype=jnp.float32) * (2.0 / values.shape[-1]))
    angles = positions[:, None] * frequencies[None, :]
    cosine = jnp.cos(angles)[:, None, :]
    sine_part = jnp.sin(angles)[:, None, :]
    first_half = values[..., :half_dim]
    second = values[..., half_dim:]
    return jnp.concatenate(
        [first_half * cosine - second * sine_part, second * cosine + first_half * sine_part],
        axis=-1,
    )


def ring_gather(piece, axis_shift, n):
    from_prev = lax.ppermute(piece, "req", axis_shift(1, n))
    from_next = lax.ppermute(piece, "req", axis_shift(-1, n))
    half = piece.shape[2] // 2
    far_a = lax.ppermute(from_prev[:, :, :half], "req", axis_shift(1, n))
    far_b = lax.ppermute(from_next[:, :, half:], "req", axis_shift(-1, n))
    far = jnp.concatenate([far_a, far_b], axis=2)
    return jnp.stack([piece, from_next, far, from_prev])


def y_shift(d, n):
    return [(i, (i // RING) * RING + (i % RING + d) % RING) for i in range(n)]


def z_shift(d, n):
    return [(i, ((i // RING + d) % RING) * RING + i % RING) for i in range(n)]


def gather_weights(w_gate, w_up, me_req, n):
    rows = w_gate.shape[0]
    half = rows // 2
    both = jnp.stack([w_gate, w_up])
    part_a = both[:, :half]
    part_b = both[:, half:]
    a_y = ring_gather(part_a[None], y_shift, n)[:, 0]
    b_z = ring_gather(part_b[None], z_shift, n)[:, 0]
    a_zy = ring_gather(a_y, z_shift, n)
    b_yz = ring_gather(b_z, y_shift, n)
    my_y = me_req % RING
    my_z = me_req // RING
    a_abs = jnp.roll(a_zy, (my_z, my_y), axis=(0, 1))
    b_abs = jnp.roll(b_yz, (my_y, my_z), axis=(0, 1)).transpose(1, 0, 2, 3, 4)
    full = jnp.stack([a_abs, b_abs], axis=3)
    full = full.transpose(2, 0, 1, 3, 4, 5).reshape(2, n * rows, w_gate.shape[1])
    return full[0], full[1]


def normalize(resid_rows, summed, gain_row):
    state = resid_rows.astype(jnp.float32) + summed
    scale_row = lax.rsqrt(jnp.mean(state * state, axis=-1, keepdims=True) + EPS)
    return (state * scale_row * gain_row).astype(jnp.bfloat16)


def shards(
    q_pre,
    k_pre,
    v_pre,
    q_bias,
    k_bias,
    v_bias,
    segment_ids,
    lengths,
    page_table,
    w_out,
    residual,
    norm_gain,
    w_gate,
    w_up,
):
    me_req = lax.axis_index("req")
    groups_all = lax.axis_size("req")
    block_rows = q_pre.shape[0]
    kv_heads = k_pre.shape[1] // HD
    q_heads = q_pre.shape[1] // HD
    group_size = q_heads // kv_heads

    wg_full, wu_full = gather_weights(w_gate, w_up, me_req, groups_all)

    own_lens = lax.dynamic_index_in_dim(lengths, me_req, 0, keepdims=False)
    own_pages = lax.dynamic_index_in_dim(page_table, me_req, 0, keepdims=False)
    own_owner = own_pages // REQS
    starts = jnp.cumsum(own_lens) - own_lens

    alive = segment_ids >= 0
    req_idx = jnp.clip(segment_ids - me_req * REQS, 0, REQS - 1)
    req_hit = req_idx[:, None] == jnp.arange(REQS)[None, :]
    row_start = jnp.sum(jnp.where(req_hit, starts[None, :], 0), axis=1)
    token = jnp.arange(block_rows, dtype=jnp.int32)
    positions = (token - row_start).astype(jnp.float32)
    keep = alive[:, None, None]

    queries = rotate(
        (q_pre.astype(jnp.float32) + q_bias).reshape(block_rows, q_heads, HD), positions
    )
    queries = jnp.where(keep, queries, 0.0).astype(jnp.bfloat16)
    keys = rotate((k_pre.astype(jnp.float32) + k_bias).reshape(block_rows, kv_heads, HD), positions)
    keys = jnp.where(keep, keys, 0.0).astype(jnp.bfloat16)
    values = (v_pre.astype(jnp.float32) + v_bias).reshape(block_rows, kv_heads, HD)
    values = jnp.where(keep, values, 0.0).astype(jnp.bfloat16)

    scale_factor = 1.0 / math.sqrt(HD)
    q_groups = queries.reshape(block_rows, kv_heads, group_size, HD)
    scores = (
        jnp.einsum("qhge,khe->hgqk", q_groups, keys, preferred_element_type=jnp.float32)
        * scale_factor
    )
    allowed = (
        (segment_ids[:, None] == segment_ids[None, :])
        & alive[None, :]
        & (token[None, :] <= token[:, None])
    )[None, None]
    row_max = jnp.max(jnp.where(allowed, scores, -1e30), axis=-1, keepdims=True)
    weights = jnp.where(allowed, jnp.exp(scores - row_max), 0.0)
    row_sum = jnp.sum(weights, axis=-1, keepdims=True)
    present = alive[None, None, :, None]
    probs = jnp.where(present, weights / jnp.where(present, row_sum, 1.0), 0.0).astype(
        jnp.bfloat16
    )
    attended = jnp.einsum("hgqk,khe->qhge", probs, values, preferred_element_type=jnp.float32)
    attended = attended.astype(jnp.bfloat16).reshape(block_rows, q_heads * HD)

    kv_rows = jnp.concatenate([keys, values], axis=-1)
    kv_rows = jnp.pad(kv_rows, ((0, PAGE), (0, 0), (0, 0)))
    slot = jnp.arange(PAGE, dtype=jnp.int32)
    pages = []
    for j in range(REQS):
        page = lax.dynamic_slice_in_dim(kv_rows, starts[j], PAGE, axis=0)
        page = jnp.where((slot < own_lens[j])[:, None, None], page, jnp.zeros((), jnp.bfloat16))
        pages.append(page)
    pages = jnp.stack(pages)
    to_owner = (own_owner[None, :] == jnp.arange(groups_all)[:, None]).astype(jnp.bfloat16)
    kv_send = jnp.einsum(
        "gj,jphc->gphc", to_owner, pages, preferred_element_type=jnp.float32
    ).astype(jnp.bfloat16)
    kv_in = lax.all_to_all(kv_send, "req", split_axis=0, concat_axis=0, tiled=True)
    hits = (
        page_table[None, :, :] == (me_req * REQS + jnp.arange(REQS, dtype=jnp.int32))[:, None, None]
    )
    page_select = jnp.sum(hits.astype(jnp.int32), axis=2).astype(jnp.bfloat16)
    cache_out = jnp.einsum(
        "ls,sphc->lhpc", page_select, kv_in, preferred_element_type=jnp.float32
    ).astype(jnp.bfloat16)

    summed = lax.psum(
        jnp.dot(attended, w_out, preferred_element_type=jnp.float32).astype(jnp.bfloat16), "mp"
    ).astype(jnp.float32)
    normed = normalize(residual, summed, norm_gain)
    gate_acc = jnp.dot(normed, wg_full, preferred_element_type=jnp.float32)
    up_acc = jnp.dot(normed, wu_full, preferred_element_type=jnp.float32)
    hidden = (jax.nn.silu(gate_acc) * up_acc).astype(jnp.bfloat16)
    return (hidden, cache_out)


def solution(mesh):
    in_specs = (
        P("req", "mp"),
        P("req", "mp"),
        P("req", "mp"),
        P("mp"),
        P("mp"),
        P("mp"),
        P("req"),
        P(),
        P(),
        P("mp", None),
        P("req", None),
        P(),
        P("req", "mp"),
        P("req", "mp"),
    )
    out_specs = (P("req", "mp"), P("req", "mp", None, None))
    return jax.shard_map(shards, mesh=mesh, in_specs=in_specs, out_specs=out_specs, check_vma=False)
```

```python
import math

import jax
import jax.numpy as jnp
from jax import lax
from jax.sharding import PartitionSpec as P
from jax.experimental import pallas as pl
from jax.experimental.pallas import tpu as pltpu

HD = 128
PAGE = 128
REQS = 4
RING = 4


THETA = 1000000.0
EPS = 1e-06


def rotate(values, positions):
    half_dim = values.shape[-1] // 2
    frequencies = THETA ** (-jnp.arange(half_dim, dtype=jnp.float32) * (2.0 / values.shape[-1]))
    angles = positions[:, None] * frequencies[None, :]
    cosine = jnp.cos(angles)[:, None, :]
    sine_part = jnp.sin(angles)[:, None, :]
    first_half = values[..., :half_dim]
    second = values[..., half_dim:]
    return jnp.concatenate(
        [first_half * cosine - second * sine_part, second * cosine + first_half * sine_part],
        axis=-1,
    )


def gather_kernel(wg_ref, wu_ref, after_ref, out_ref, send_sems, recv_sems, local_sems):
    me = lax.axis_index("req")
    col = lax.axis_index("mp")
    z = me // RING
    y = me % RING
    yp = (y + 1) % RING
    ym = (y + RING - 1) % RING
    zp = (z + 1) % RING
    zm = (z + RING - 1) % RING
    rows = wg_ref.shape[0]
    half = rows // 2
    mesh_id = pl.DeviceIdType.MESH

    def to(zz, yy):
        return (zz * RING + yy, col)

    barrier = pltpu.get_barrier_semaphore()
    for peer in (to(z, yp), to(z, ym), to(zp, y), to(zm, y)):
        pl.semaphore_signal(barrier, inc=1, device_id=peer, device_id_type=mesh_id)
    pl.semaphore_wait(barrier, 4)

    def remote(k, src, dst, peer):
        return pltpu.make_async_remote_copy(
            src_ref=src,
            dst_ref=dst,
            send_sem=send_sems.at[k],
            recv_sem=recv_sems.at[k],
            device_id=peer,
            device_id_type=mesh_id,
        )

    own_g = pltpu.make_async_copy(wg_ref, out_ref.at[0, z, y], local_sems.at[0])
    own_u = pltpu.make_async_copy(wu_ref, out_ref.at[1, z, y], local_sems.at[1])
    own_g.start()
    own_u.start()

    step1 = [
        remote(0, wg_ref, out_ref.at[0, z, y], to(z, yp)),
        remote(1, wg_ref, out_ref.at[0, z, y], to(z, ym)),
        remote(2, wu_ref, out_ref.at[1, z, y], to(zp, y)),
        remote(3, wu_ref, out_ref.at[1, z, y], to(zm, y)),
    ]
    for c in step1:
        c.start()
    for c in step1:
        c.wait_recv()

    low = pl.ds(0, half)
    high = pl.ds(half, rows - half)
    step2 = [
        remote(4, out_ref.at[0, z, ym, low], out_ref.at[0, z, ym, low], to(z, yp)),
        remote(5, out_ref.at[0, z, yp, high], out_ref.at[0, z, yp, high], to(z, ym)),
        remote(6, out_ref.at[1, zm, y, low], out_ref.at[1, zm, y, low], to(zp, y)),
        remote(7, out_ref.at[1, zp, y, high], out_ref.at[1, zp, y, high], to(zm, y)),
    ]
    for c in step2:
        c.start()
    own_g.wait()
    own_u.wait()
    for c in step2:
        c.wait_recv()

    step3 = [
        remote(8, out_ref.at[0, z], out_ref.at[0, z], to(zp, y)),
        remote(9, out_ref.at[0, z], out_ref.at[0, z], to(zm, y)),
        remote(10, out_ref.at[1, :, y], out_ref.at[1, :, y], to(z, yp)),
        remote(11, out_ref.at[1, :, y], out_ref.at[1, :, y], to(z, ym)),
    ]
    for c in step3:
        c.start()
    for c in step3:
        c.wait_recv()

    first = pl.ds(0, RING // 2)
    second = pl.ds(RING // 2, RING - RING // 2)
    step4 = [
        remote(12, out_ref.at[0, zm, first], out_ref.at[0, zm, first], to(zp, y)),
        remote(13, out_ref.at[0, zp, second], out_ref.at[0, zp, second], to(zm, y)),
        remote(14, out_ref.at[1, first, ym], out_ref.at[1, first, ym], to(z, yp)),
        remote(15, out_ref.at[1, second, yp], out_ref.at[1, second, yp], to(z, ym)),
    ]
    for c in step4:
        c.start()
    for c in step4:
        c.wait_recv()
    for c in step1 + step2 + step3 + step4:
        c.wait_send()


def gather_weights(w_gate, w_up, after):
    rows, cols = w_gate.shape
    any_spec = pl.BlockSpec(memory_space=pl.ANY)
    return pl.pallas_call(
        gather_kernel,
        out_shape=jax.ShapeDtypeStruct((2, RING, RING, rows, cols), w_gate.dtype),
        in_specs=[any_spec, any_spec, any_spec],
        out_specs=any_spec,
        scratch_shapes=[
            pltpu.SemaphoreType.DMA((16,)),
            pltpu.SemaphoreType.DMA((16,)),
            pltpu.SemaphoreType.DMA((2,)),
        ],
        compiler_params=pltpu.CompilerParams(collective_id=0, has_side_effects=True),
    )(w_gate, w_up, after)


def normalize(resid_rows, summed, gain_row):
    state = resid_rows.astype(jnp.float32) + summed
    scale_row = lax.rsqrt(jnp.mean(state * state, axis=-1, keepdims=True) + EPS)
    return (state * scale_row * gain_row).astype(jnp.bfloat16)


def shards(
    q_pre,
    k_pre,
    v_pre,
    q_bias,
    k_bias,
    v_bias,
    segment_ids,
    lengths,
    page_table,
    w_out,
    residual,
    norm_gain,
    w_gate,
    w_up,
):
    me_req = lax.axis_index("req")
    groups_all = lax.axis_size("req")
    block_rows = q_pre.shape[0]
    kv_heads = k_pre.shape[1] // HD
    q_heads = q_pre.shape[1] // HD
    group_size = q_heads // kv_heads


    own_lens = lax.dynamic_index_in_dim(lengths, me_req, 0, keepdims=False)
    own_pages = lax.dynamic_index_in_dim(page_table, me_req, 0, keepdims=False)
    own_owner = own_pages // REQS
    starts = jnp.cumsum(own_lens) - own_lens

    alive = segment_ids >= 0
    req_idx = jnp.clip(segment_ids - me_req * REQS, 0, REQS - 1)
    req_hit = req_idx[:, None] == jnp.arange(REQS)[None, :]
    row_start = jnp.sum(jnp.where(req_hit, starts[None, :], 0), axis=1)
    token = jnp.arange(block_rows, dtype=jnp.int32)
    positions = (token - row_start).astype(jnp.float32)
    keep = alive[:, None, None]

    queries = rotate(
        (q_pre.astype(jnp.float32) + q_bias).reshape(block_rows, q_heads, HD), positions
    )
    queries = jnp.where(keep, queries, 0.0).astype(jnp.bfloat16)
    keys = rotate((k_pre.astype(jnp.float32) + k_bias).reshape(block_rows, kv_heads, HD), positions)
    keys = jnp.where(keep, keys, 0.0).astype(jnp.bfloat16)
    values = (v_pre.astype(jnp.float32) + v_bias).reshape(block_rows, kv_heads, HD)
    values = jnp.where(keep, values, 0.0).astype(jnp.bfloat16)

    scale_factor = 1.0 / math.sqrt(HD)
    q_groups = queries.reshape(block_rows, kv_heads, group_size, HD)
    scores = (
        jnp.einsum("qhge,khe->hgqk", q_groups, keys, preferred_element_type=jnp.float32)
        * scale_factor
    )
    allowed = (
        (segment_ids[:, None] == segment_ids[None, :])
        & alive[None, :]
        & (token[None, :] <= token[:, None])
    )[None, None]
    row_max = jnp.max(jnp.where(allowed, scores, -1e30), axis=-1, keepdims=True)
    weights = jnp.where(allowed, jnp.exp(scores - row_max), 0.0)
    row_sum = jnp.sum(weights, axis=-1, keepdims=True)
    present = alive[None, None, :, None]
    probs = jnp.where(present, weights / jnp.where(present, row_sum, 1.0), 0.0).astype(
        jnp.bfloat16
    )
    attended = jnp.einsum("hgqk,khe->qhge", probs, values, preferred_element_type=jnp.float32)
    attended = attended.astype(jnp.bfloat16).reshape(block_rows, q_heads * HD)

    kv_rows = jnp.concatenate([keys, values], axis=-1)
    kv_rows = jnp.pad(kv_rows, ((0, PAGE), (0, 0), (0, 0)))
    slot = jnp.arange(PAGE, dtype=jnp.int32)
    pages = []
    for j in range(REQS):
        page = lax.dynamic_slice_in_dim(kv_rows, starts[j], PAGE, axis=0)
        page = jnp.where((slot < own_lens[j])[:, None, None], page, jnp.zeros((), jnp.bfloat16))
        pages.append(page)
    pages = jnp.stack(pages)
    to_owner = (own_owner[None, :] == jnp.arange(groups_all)[:, None]).astype(jnp.bfloat16)
    kv_send = jnp.einsum(
        "gj,jphc->gphc", to_owner, pages, preferred_element_type=jnp.float32
    ).astype(jnp.bfloat16)
    kv_in = lax.all_to_all(kv_send, "req", split_axis=0, concat_axis=0, tiled=True)
    hits = (
        page_table[None, :, :] == (me_req * REQS + jnp.arange(REQS, dtype=jnp.int32))[:, None, None]
    )
    page_select = jnp.sum(hits.astype(jnp.int32), axis=2).astype(jnp.bfloat16)
    cache_out = jnp.einsum(
        "ls,sphc->lhpc", page_select, kv_in, preferred_element_type=jnp.float32
    ).astype(jnp.bfloat16)

    product = jnp.dot(attended, w_out, preferred_element_type=jnp.float32).astype(jnp.bfloat16)
    summed = lax.psum(product, "mp").astype(jnp.float32)
    normed = normalize(residual, summed, norm_gain)
    gathered = gather_weights(w_gate, w_up, product[:8, :128])
    wg_full = gathered[0].reshape(-1, w_gate.shape[1])
    wu_full = gathered[1].reshape(-1, w_up.shape[1])
    gate_acc = jnp.dot(normed, wg_full, preferred_element_type=jnp.float32)
    up_acc = jnp.dot(normed, wu_full, preferred_element_type=jnp.float32)
    hidden = (jax.nn.silu(gate_acc) * up_acc).astype(jnp.bfloat16)
    return (hidden, cache_out)


def solution(mesh):
    in_specs = (
        P("req", "mp"),
        P("req", "mp"),
        P("req", "mp"),
        P("mp"),
        P("mp"),
        P("mp"),
        P("req"),
        P(),
        P(),
        P("mp", None),
        P("req", None),
        P(),
        P("req", "mp"),
        P("req", "mp"),
    )
    out_specs = (P("req", "mp"), P("req", "mp", None, None))
    return jax.shard_map(shards, mesh=mesh, in_specs=in_specs, out_specs=out_specs, check_vma=False)
```

```python
import math

import jax
import jax.numpy as jnp
from jax import lax
from jax.sharding import PartitionSpec as P
from jax.experimental import pallas as pl
from jax.experimental.pallas import tpu as pltpu

HD = 128
PAGE = 128
REQS = 4
RING = 4


THETA = 1000000.0
EPS = 1e-06


def rotate(values, positions):
    half_dim = values.shape[-1] // 2
    frequencies = THETA ** (-jnp.arange(half_dim, dtype=jnp.float32) * (2.0 / values.shape[-1]))
    angles = positions[:, None] * frequencies[None, :]
    cosine = jnp.cos(angles)[:, None, :]
    sine_part = jnp.sin(angles)[:, None, :]
    first_half = values[..., :half_dim]
    second = values[..., half_dim:]
    return jnp.concatenate(
        [first_half * cosine - second * sine_part, second * cosine + first_half * sine_part],
        axis=-1,
    )


def gather_kernel(wg_ref, wu_ref, after_ref, g_ref, u_ref, send_sems, recv_sems, local_sems):
    me = lax.axis_index("req")
    col = lax.axis_index("mp")
    z = me // RING
    y = me % RING
    yp = (y + 1) % RING
    ym = (y + RING - 1) % RING
    y2 = (y + 2) % RING
    zp = (z + 1) % RING
    zm = (z + RING - 1) % RING
    z2 = (z + 2) % RING
    rows = wg_ref.shape[0]
    low = pl.ds(0, rows // 2)
    high = pl.ds(rows // 2, rows - rows // 2)
    mesh_id = pl.DeviceIdType.MESH

    def to(zz, yy):
        return (zz * RING + yy, col)

    barrier = pltpu.get_barrier_semaphore()
    for peer in (to(z, yp), to(z, ym), to(zp, y), to(zm, y)):
        pl.semaphore_signal(barrier, inc=1, device_id=peer, device_id_type=mesh_id)
    pl.semaphore_wait(barrier, 4)

    copies = []

    def send(src, dst, peer):
        k = len(copies)
        c = pltpu.make_async_remote_copy(
            src_ref=src,
            dst_ref=dst,
            send_sem=send_sems.at[k],
            recv_sem=recv_sems.at[k],
            device_id=peer,
            device_id_type=mesh_id,
        )
        c.start()
        copies.append(c)
        return c

    own_g = pltpu.make_async_copy(wg_ref, g_ref.at[z, y], local_sems.at[0])
    own_u = pltpu.make_async_copy(wu_ref, u_ref.at[z, y], local_sems.at[1])
    own_g.start()
    own_u.start()

    g_from_ym = send(wg_ref, g_ref.at[z, y], to(z, yp))
    g_from_yp = send(wg_ref, g_ref.at[z, y], to(z, ym))
    u_from_zm = send(wu_ref, u_ref.at[z, y], to(zp, y))
    u_from_zp = send(wu_ref, u_ref.at[z, y], to(zm, y))
    gz = {"y": (send(wg_ref, g_ref.at[z, y], to(zp, y)), send(wg_ref, g_ref.at[z, y], to(zm, y)))}
    uy = {"z": (send(wu_ref, u_ref.at[z, y], to(z, yp)), send(wu_ref, u_ref.at[z, y], to(z, ym)))}

    g_from_ym.wait_recv()
    g_far_a = send(g_ref.at[z, ym, low], g_ref.at[z, ym, low], to(z, yp))
    gz["ym"] = (send(g_ref.at[z, ym], g_ref.at[z, ym], to(zp, y)), send(g_ref.at[z, ym], g_ref.at[z, ym], to(zm, y)))
    u_from_zm.wait_recv()
    u_far_a = send(u_ref.at[zm, y, low], u_ref.at[zm, y, low], to(zp, y))
    uy["zm"] = (send(u_ref.at[zm, y], u_ref.at[zm, y], to(z, yp)), send(u_ref.at[zm, y], u_ref.at[zm, y], to(z, ym)))
    g_from_yp.wait_recv()
    g_far_b = send(g_ref.at[z, yp, high], g_ref.at[z, yp, high], to(z, ym))
    gz["yp"] = (send(g_ref.at[z, yp], g_ref.at[z, yp], to(zp, y)), send(g_ref.at[z, yp], g_ref.at[z, yp], to(zm, y)))
    u_from_zp.wait_recv()
    u_far_b = send(u_ref.at[zp, y, high], u_ref.at[zp, y, high], to(zm, y))
    uy["zp"] = (send(u_ref.at[zp, y], u_ref.at[zp, y], to(z, yp)), send(u_ref.at[zp, y], u_ref.at[zp, y], to(z, ym)))

    g_far_a.wait_recv()
    g_far_b.wait_recv()
    gz["y2"] = (send(g_ref.at[z, y2], g_ref.at[z, y2], to(zp, y)), send(g_ref.at[z, y2], g_ref.at[z, y2], to(zm, y)))
    u_far_a.wait_recv()
    u_far_b.wait_recv()
    uy["z2"] = (send(u_ref.at[z2, y], u_ref.at[z2, y], to(z, yp)), send(u_ref.at[z2, y], u_ref.at[z2, y], to(z, ym)))

    for key, yy in (("y", y), ("ym", ym), ("yp", yp), ("y2", y2)):
        from_zm, from_zp = gz[key]
        from_zm.wait_recv()
        send(g_ref.at[zm, yy, low], g_ref.at[zm, yy, low], to(zp, y))
        from_zp.wait_recv()
        send(g_ref.at[zp, yy, high], g_ref.at[zp, yy, high], to(zm, y))
    for key, zz in (("z", z), ("zm", zm), ("zp", zp), ("z2", z2)):
        from_ym, from_yp = uy[key]
        from_ym.wait_recv()
        send(u_ref.at[zz, ym, low], u_ref.at[zz, ym, low], to(z, yp))
        from_yp.wait_recv()
        send(u_ref.at[zz, yp, high], u_ref.at[zz, yp, high], to(z, ym))

    waited = [g_from_ym, g_from_yp, u_from_zm, u_from_zp, g_far_a, g_far_b, u_far_a, u_far_b]
    waited += list(gz["y"]) + list(gz["ym"]) + list(gz["yp"]) + list(gz["y2"])
    waited += list(uy["z"]) + list(uy["zm"]) + list(uy["zp"]) + list(uy["z2"])
    for c in copies:
        if not any(c is w for w in waited):
            c.wait_recv()
    for c in copies:
        c.wait_send()
    own_g.wait()
    own_u.wait()


def gather_weights(w_gate, w_up, after):
    rows, cols = w_gate.shape
    any_spec = pl.BlockSpec(memory_space=pl.ANY)
    piece = jax.ShapeDtypeStruct((RING, RING, rows, cols), w_gate.dtype)
    return pl.pallas_call(
        gather_kernel,
        out_shape=(piece, piece),
        in_specs=[any_spec, any_spec, any_spec],
        out_specs=(any_spec, any_spec),
        scratch_shapes=[
            pltpu.SemaphoreType.DMA((40,)),
            pltpu.SemaphoreType.DMA((40,)),
            pltpu.SemaphoreType.DMA((2,)),
        ],
        compiler_params=pltpu.CompilerParams(collective_id=0, has_side_effects=True),
    )(w_gate, w_up, after)

def normalize(resid_rows, summed, gain_row):
    state = resid_rows.astype(jnp.float32) + summed
    scale_row = lax.rsqrt(jnp.mean(state * state, axis=-1, keepdims=True) + EPS)
    return (state * scale_row * gain_row).astype(jnp.bfloat16)


def shards(
    q_pre,
    k_pre,
    v_pre,
    q_bias,
    k_bias,
    v_bias,
    segment_ids,
    lengths,
    page_table,
    w_out,
    residual,
    norm_gain,
    w_gate,
    w_up,
):
    me_req = lax.axis_index("req")
    groups_all = lax.axis_size("req")
    block_rows = q_pre.shape[0]
    kv_heads = k_pre.shape[1] // HD
    q_heads = q_pre.shape[1] // HD
    group_size = q_heads // kv_heads


    own_lens = lax.dynamic_index_in_dim(lengths, me_req, 0, keepdims=False)
    own_pages = lax.dynamic_index_in_dim(page_table, me_req, 0, keepdims=False)
    own_owner = own_pages // REQS
    starts = jnp.cumsum(own_lens) - own_lens

    alive = segment_ids >= 0
    req_idx = jnp.clip(segment_ids - me_req * REQS, 0, REQS - 1)
    req_hit = req_idx[:, None] == jnp.arange(REQS)[None, :]
    row_start = jnp.sum(jnp.where(req_hit, starts[None, :], 0), axis=1)
    token = jnp.arange(block_rows, dtype=jnp.int32)
    positions = (token - row_start).astype(jnp.float32)
    keep = alive[:, None, None]

    queries = rotate(
        (q_pre.astype(jnp.float32) + q_bias).reshape(block_rows, q_heads, HD), positions
    )
    queries = jnp.where(keep, queries, 0.0).astype(jnp.bfloat16)
    keys = rotate((k_pre.astype(jnp.float32) + k_bias).reshape(block_rows, kv_heads, HD), positions)
    keys = jnp.where(keep, keys, 0.0).astype(jnp.bfloat16)
    values = (v_pre.astype(jnp.float32) + v_bias).reshape(block_rows, kv_heads, HD)
    values = jnp.where(keep, values, 0.0).astype(jnp.bfloat16)

    scale_factor = 1.0 / math.sqrt(HD)
    q_groups = queries.reshape(block_rows, kv_heads, group_size, HD)
    scores = (
        jnp.einsum("qhge,khe->hgqk", q_groups, keys, preferred_element_type=jnp.float32)
        * scale_factor
    )
    allowed = (
        (segment_ids[:, None] == segment_ids[None, :])
        & alive[None, :]
        & (token[None, :] <= token[:, None])
    )[None, None]
    row_max = jnp.max(jnp.where(allowed, scores, -1e30), axis=-1, keepdims=True)
    weights = jnp.where(allowed, jnp.exp(scores - row_max), 0.0)
    row_sum = jnp.sum(weights, axis=-1, keepdims=True)
    present = alive[None, None, :, None]
    probs = jnp.where(present, weights / jnp.where(present, row_sum, 1.0), 0.0).astype(
        jnp.bfloat16
    )
    attended = jnp.einsum("hgqk,khe->qhge", probs, values, preferred_element_type=jnp.float32)
    attended = attended.astype(jnp.bfloat16).reshape(block_rows, q_heads * HD)

    kv_rows = jnp.concatenate([keys, values], axis=-1)
    kv_rows = jnp.pad(kv_rows, ((0, PAGE), (0, 0), (0, 0)))
    slot = jnp.arange(PAGE, dtype=jnp.int32)
    pages = []
    for j in range(REQS):
        page = lax.dynamic_slice_in_dim(kv_rows, starts[j], PAGE, axis=0)
        page = jnp.where((slot < own_lens[j])[:, None, None], page, jnp.zeros((), jnp.bfloat16))
        pages.append(page)
    pages = jnp.stack(pages)
    to_owner = (own_owner[None, :] == jnp.arange(groups_all)[:, None]).astype(jnp.bfloat16)
    kv_send = jnp.einsum(
        "gj,jphc->gphc", to_owner, pages, preferred_element_type=jnp.float32
    ).astype(jnp.bfloat16)
    kv_in = lax.all_to_all(kv_send, "req", split_axis=0, concat_axis=0, tiled=True)
    hits = (
        page_table[None, :, :] == (me_req * REQS + jnp.arange(REQS, dtype=jnp.int32))[:, None, None]
    )
    page_select = jnp.sum(hits.astype(jnp.int32), axis=2).astype(jnp.bfloat16)
    cache_out = jnp.einsum(
        "ls,sphc->lhpc", page_select, kv_in, preferred_element_type=jnp.float32
    ).astype(jnp.bfloat16)

    product = jnp.dot(attended, w_out, preferred_element_type=jnp.float32).astype(jnp.bfloat16)
    summed = lax.psum(product, "mp").astype(jnp.float32)
    normed = normalize(residual, summed, norm_gain)
    g_full, u_full = gather_weights(w_gate, w_up, product[:8, :128])
    wg_full = g_full.reshape(-1, w_gate.shape[1])
    wu_full = u_full.reshape(-1, w_up.shape[1])
    gate_acc = jnp.dot(normed, wg_full, preferred_element_type=jnp.float32)
    up_acc = jnp.dot(normed, wu_full, preferred_element_type=jnp.float32)
    hidden = (jax.nn.silu(gate_acc) * up_acc).astype(jnp.bfloat16)
    return (hidden, cache_out)


def solution(mesh):
    in_specs = (
        P("req", "mp"),
        P("req", "mp"),
        P("req", "mp"),
        P("mp"),
        P("mp"),
        P("mp"),
        P("req"),
        P(),
        P(),
        P("mp", None),
        P("req", None),
        P(),
        P("req", "mp"),
        P("req", "mp"),
    )
    out_specs = (P("req", "mp"), P("req", "mp", None, None))
    return jax.shard_map(shards, mesh=mesh, in_specs=in_specs, out_specs=out_specs, check_vma=False)
```

```python
import math

import jax
import jax.numpy as jnp
from jax import lax
from jax.sharding import PartitionSpec as P
from jax.experimental import pallas as pl
from jax.experimental.pallas import tpu as pltpu

HD = 128
PAGE = 128
REQS = 4
RING = 4


THETA = 1000000.0
EPS = 1e-06


def rotate(values, positions):
    half_dim = values.shape[-1] // 2
    frequencies = THETA ** (-jnp.arange(half_dim, dtype=jnp.float32) * (2.0 / values.shape[-1]))
    angles = positions[:, None] * frequencies[None, :]
    cosine = jnp.cos(angles)[:, None, :]
    sine_part = jnp.sin(angles)[:, None, :]
    first_half = values[..., :half_dim]
    second = values[..., half_dim:]
    return jnp.concatenate(
        [first_half * cosine - second * sine_part, second * cosine + first_half * sine_part],
        axis=-1,
    )


def gather_kernel(wg_ref, wu_ref, after_ref, g_ref, u_ref, send_sems, recv_sems, local_sems):
    me = lax.axis_index("req")
    col = lax.axis_index("mp")
    z = me // RING
    y = me % RING
    yp = (y + 1) % RING
    ym = (y + RING - 1) % RING
    y2 = (y + 2) % RING
    zp = (z + 1) % RING
    zm = (z + RING - 1) % RING
    z2 = (z + 2) % RING
    rows = wg_ref.shape[0]
    low = pl.ds(0, rows // 2)
    high = pl.ds(rows // 2, rows - rows // 2)
    mesh_id = pl.DeviceIdType.MESH

    def to(zz, yy):
        return (zz * RING + yy, col)

    barrier = pltpu.get_barrier_semaphore()
    for peer in (to(z, yp), to(z, ym), to(zp, y), to(zm, y)):
        pl.semaphore_signal(barrier, inc=1, device_id=peer, device_id_type=mesh_id)
    pl.semaphore_wait(barrier, 4)

    copies = []

    def send(src, dst, peer):
        k = len(copies)
        c = pltpu.make_async_remote_copy(
            src_ref=src,
            dst_ref=dst,
            send_sem=send_sems.at[k],
            recv_sem=recv_sems.at[k],
            device_id=peer,
            device_id_type=mesh_id,
        )
        c.start()
        copies.append(c)
        return c

    own_g = pltpu.make_async_copy(wg_ref, g_ref.at[z, y], local_sems.at[0])
    own_u = pltpu.make_async_copy(wu_ref, u_ref.at[z, y], local_sems.at[1])
    own_g.start()
    own_u.start()

    g_from_ym = send(wg_ref, g_ref.at[z, y], to(z, yp))
    g_from_yp = send(wg_ref, g_ref.at[z, y], to(z, ym))
    u_from_zm = send(wu_ref, u_ref.at[z, y], to(zp, y))
    u_from_zp = send(wu_ref, u_ref.at[z, y], to(zm, y))
    gz = {"y": (send(wg_ref, g_ref.at[z, y], to(zp, y)), send(wg_ref, g_ref.at[z, y], to(zm, y)))}
    uy = {"z": (send(wu_ref, u_ref.at[z, y], to(z, yp)), send(wu_ref, u_ref.at[z, y], to(z, ym)))}

    g_from_ym.wait_recv()
    g_far_a = send(g_ref.at[z, ym, low], g_ref.at[z, ym, low], to(z, yp))
    gz["ym"] = (send(g_ref.at[z, ym], g_ref.at[z, ym], to(zp, y)), send(g_ref.at[z, ym], g_ref.at[z, ym], to(zm, y)))
    u_from_zm.wait_recv()
    u_far_a = send(u_ref.at[zm, y, low], u_ref.at[zm, y, low], to(zp, y))
    uy["zm"] = (send(u_ref.at[zm, y], u_ref.at[zm, y], to(z, yp)), send(u_ref.at[zm, y], u_ref.at[zm, y], to(z, ym)))
    g_from_yp.wait_recv()
    g_far_b = send(g_ref.at[z, yp, high], g_ref.at[z, yp, high], to(z, ym))
    gz["yp"] = (send(g_ref.at[z, yp], g_ref.at[z, yp], to(zp, y)), send(g_ref.at[z, yp], g_ref.at[z, yp], to(zm, y)))
    u_from_zp.wait_recv()
    u_far_b = send(u_ref.at[zp, y, high], u_ref.at[zp, y, high], to(zm, y))
    uy["zp"] = (send(u_ref.at[zp, y], u_ref.at[zp, y], to(z, yp)), send(u_ref.at[zp, y], u_ref.at[zp, y], to(z, ym)))

    g_far_a.wait_recv()
    g_far_b.wait_recv()
    gz["y2"] = (send(g_ref.at[z, y2], g_ref.at[z, y2], to(zp, y)), send(g_ref.at[z, y2], g_ref.at[z, y2], to(zm, y)))
    u_far_a.wait_recv()
    u_far_b.wait_recv()
    uy["z2"] = (send(u_ref.at[z2, y], u_ref.at[z2, y], to(z, yp)), send(u_ref.at[z2, y], u_ref.at[z2, y], to(z, ym)))

    for key, yy in (("y", y), ("ym", ym), ("yp", yp), ("y2", y2)):
        from_zm, from_zp = gz[key]
        from_zm.wait_recv()
        send(g_ref.at[zm, yy, low], g_ref.at[zm, yy, low], to(zp, y))
        from_zp.wait_recv()
        send(g_ref.at[zp, yy, high], g_ref.at[zp, yy, high], to(zm, y))
    for key, zz in (("z", z), ("zm", zm), ("zp", zp), ("z2", z2)):
        from_ym, from_yp = uy[key]
        from_ym.wait_recv()
        send(u_ref.at[zz, ym, low], u_ref.at[zz, ym, low], to(z, yp))
        from_yp.wait_recv()
        send(u_ref.at[zz, yp, high], u_ref.at[zz, yp, high], to(z, ym))

    waited = [g_from_ym, g_from_yp, u_from_zm, u_from_zp, g_far_a, g_far_b, u_far_a, u_far_b]
    waited += list(gz["y"]) + list(gz["ym"]) + list(gz["yp"]) + list(gz["y2"])
    waited += list(uy["z"]) + list(uy["zm"]) + list(uy["zp"]) + list(uy["z2"])
    for c in copies:
        if not any(c is w for w in waited):
            c.wait_recv()
    for c in copies:
        c.wait_send()
    own_g.wait()
    own_u.wait()


def gather_weights(w_gate, w_up, after):
    rows, cols = w_gate.shape
    any_spec = pl.BlockSpec(memory_space=pl.ANY)
    piece = jax.ShapeDtypeStruct((RING, RING, rows, cols), w_gate.dtype)
    return pl.pallas_call(
        gather_kernel,
        out_shape=(piece, piece),
        in_specs=[any_spec, any_spec, any_spec],
        out_specs=(any_spec, any_spec),
        scratch_shapes=[
            pltpu.SemaphoreType.DMA((40,)),
            pltpu.SemaphoreType.DMA((40,)),
            pltpu.SemaphoreType.DMA((2,)),
        ],
        compiler_params=pltpu.CompilerParams(collective_id=0, has_side_effects=True),
    )(w_gate, w_up, after)

def normalize(resid_rows, summed, gain_row):
    state = resid_rows.astype(jnp.float32) + summed
    scale_row = lax.rsqrt(jnp.mean(state * state, axis=-1, keepdims=True) + EPS)
    return (state * scale_row * gain_row).astype(jnp.bfloat16)


def shards(
    q_pre,
    k_pre,
    v_pre,
    q_bias,
    k_bias,
    v_bias,
    segment_ids,
    lengths,
    page_table,
    w_out,
    residual,
    norm_gain,
    w_gate,
    w_up,
):
    me_req = lax.axis_index("req")
    groups_all = lax.axis_size("req")
    block_rows = q_pre.shape[0]
    kv_heads = k_pre.shape[1] // HD
    q_heads = q_pre.shape[1] // HD
    group_size = q_heads // kv_heads


    own_lens = lax.dynamic_index_in_dim(lengths, me_req, 0, keepdims=False)
    own_pages = lax.dynamic_index_in_dim(page_table, me_req, 0, keepdims=False)
    own_owner = own_pages // REQS
    starts = jnp.cumsum(own_lens) - own_lens

    alive = segment_ids >= 0
    req_idx = jnp.clip(segment_ids - me_req * REQS, 0, REQS - 1)
    req_hit = req_idx[:, None] == jnp.arange(REQS)[None, :]
    row_start = jnp.sum(jnp.where(req_hit, starts[None, :], 0), axis=1)
    token = jnp.arange(block_rows, dtype=jnp.int32)
    positions = (token - row_start).astype(jnp.float32)
    keep = alive[:, None, None]

    queries = rotate(
        (q_pre.astype(jnp.float32) + q_bias).reshape(block_rows, q_heads, HD), positions
    )
    queries = jnp.where(keep, queries, 0.0).astype(jnp.bfloat16)
    keys = rotate((k_pre.astype(jnp.float32) + k_bias).reshape(block_rows, kv_heads, HD), positions)
    keys = jnp.where(keep, keys, 0.0).astype(jnp.bfloat16)
    values = (v_pre.astype(jnp.float32) + v_bias).reshape(block_rows, kv_heads, HD)
    values = jnp.where(keep, values, 0.0).astype(jnp.bfloat16)

    scale_factor = 1.0 / math.sqrt(HD)
    q_groups = queries.reshape(block_rows, kv_heads, group_size, HD)
    scores = (
        jnp.einsum("qhge,khe->hgqk", q_groups, keys, preferred_element_type=jnp.float32)
        * scale_factor
    )
    allowed = (
        (segment_ids[:, None] == segment_ids[None, :])
        & alive[None, :]
        & (token[None, :] <= token[:, None])
    )[None, None]
    row_max = jnp.max(jnp.where(allowed, scores, -1e30), axis=-1, keepdims=True)
    weights = jnp.where(allowed, jnp.exp(scores - row_max), 0.0)
    row_sum = jnp.sum(weights, axis=-1, keepdims=True)
    present = alive[None, None, :, None]
    probs = jnp.where(present, weights / jnp.where(present, row_sum, 1.0), 0.0).astype(
        jnp.bfloat16
    )
    attended = jnp.einsum("hgqk,khe->qhge", probs, values, preferred_element_type=jnp.float32)
    attended = attended.astype(jnp.bfloat16).reshape(block_rows, q_heads * HD)

    kv_rows = jnp.concatenate([keys, values], axis=-1)
    kv_rows = jnp.pad(kv_rows, ((0, PAGE), (0, 0), (0, 0)))
    slot = jnp.arange(PAGE, dtype=jnp.int32)
    pages = []
    for j in range(REQS):
        page = lax.dynamic_slice_in_dim(kv_rows, starts[j], PAGE, axis=0)
        page = jnp.where((slot < own_lens[j])[:, None, None], page, jnp.zeros((), jnp.bfloat16))
        pages.append(page)
    pages = jnp.stack(pages)
    to_owner = (own_owner[None, :] == jnp.arange(groups_all)[:, None]).astype(jnp.bfloat16)
    kv_send = jnp.einsum(
        "gj,jphc->gphc", to_owner, pages, preferred_element_type=jnp.float32
    ).astype(jnp.bfloat16)
    kv_in = lax.all_to_all(kv_send, "req", split_axis=0, concat_axis=0, tiled=True)
    hits = (
        page_table[None, :, :] == (me_req * REQS + jnp.arange(REQS, dtype=jnp.int32))[:, None, None]
    )
    page_select = jnp.sum(hits.astype(jnp.int32), axis=2).astype(jnp.bfloat16)
    cache_out = jnp.einsum(
        "ls,sphc->lhpc", page_select, kv_in, preferred_element_type=jnp.float32
    ).astype(jnp.bfloat16)

    product = jnp.dot(attended, w_out, preferred_element_type=jnp.float32).astype(jnp.bfloat16)
    summed = lax.psum(product, "mp").astype(jnp.float32)
    normed = normalize(residual, summed, norm_gain)
    half = w_gate.shape[0] // 2
    g_low, g_high = gather_weights(w_gate[:half], w_gate[half:], product[:8, :128])
    wu_full = lax.all_gather(w_up, "req", axis=0, tiled=True)
    cols = g_low.shape[-1]
    split = normed.reshape(block_rows, -1, 2, half)
    gate_acc = jnp.dot(
        split[:, :, 0].reshape(block_rows, -1),
        g_low.reshape(-1, cols),
        preferred_element_type=jnp.float32,
    ) + jnp.dot(
        split[:, :, 1].reshape(block_rows, -1),
        g_high.reshape(-1, cols),
        preferred_element_type=jnp.float32,
    )
    up_acc = jnp.dot(normed, wu_full, preferred_element_type=jnp.float32)
    hidden = (jax.nn.silu(gate_acc) * up_acc).astype(jnp.bfloat16)
    return (hidden, cache_out)


def solution(mesh):
    in_specs = (
        P("req", "mp"),
        P("req", "mp"),
        P("req", "mp"),
        P("mp"),
        P("mp"),
        P("mp"),
        P("req"),
        P(),
        P(),
        P("mp", None),
        P("req", None),
        P(),
        P("req", "mp"),
        P("req", "mp"),
    )
    out_specs = (P("req", "mp"), P("req", "mp", None, None))
    return jax.shard_map(shards, mesh=mesh, in_specs=in_specs, out_specs=out_specs, check_vma=False)
```

```python
import math

import jax
import jax.numpy as jnp
from jax import lax
from jax.sharding import PartitionSpec as P
from jax.experimental import pallas as pl
from jax.experimental.pallas import tpu as pltpu

HD = 128
PAGE = 128
REQS = 4
RING = 4


THETA = 1000000.0
EPS = 1e-06


def rotate(values, positions):
    half_dim = values.shape[-1] // 2
    frequencies = THETA ** (-jnp.arange(half_dim, dtype=jnp.float32) * (2.0 / values.shape[-1]))
    angles = positions[:, None] * frequencies[None, :]
    cosine = jnp.cos(angles)[:, None, :]
    sine_part = jnp.sin(angles)[:, None, :]
    first_half = values[..., :half_dim]
    second = values[..., half_dim:]
    return jnp.concatenate(
        [first_half * cosine - second * sine_part, second * cosine + first_half * sine_part],
        axis=-1,
    )


def gather_kernel(wg_ref, wu_ref, after_ref, g_ref, u_ref, send_sems, recv_sems, local_sems):
    me = lax.axis_index("req")
    col = lax.axis_index("mp")
    z = me // RING
    y = me % RING
    yp = (y + 1) % RING
    ym = (y + RING - 1) % RING
    y2 = (y + 2) % RING
    zp = (z + 1) % RING
    zm = (z + RING - 1) % RING
    z2 = (z + 2) % RING
    rows = wg_ref.shape[0]
    low = pl.ds(0, rows // 2)
    high = pl.ds(rows // 2, rows - rows // 2)
    mesh_id = pl.DeviceIdType.MESH

    def to(zz, yy):
        return (zz * RING + yy, col)

    barrier = pltpu.get_barrier_semaphore()
    for peer in (to(z, yp), to(z, ym), to(zp, y), to(zm, y)):
        pl.semaphore_signal(barrier, inc=1, device_id=peer, device_id_type=mesh_id)
    pl.semaphore_wait(barrier, 4)

    copies = []

    def send(src, dst, peer):
        k = len(copies)
        c = pltpu.make_async_remote_copy(
            src_ref=src,
            dst_ref=dst,
            send_sem=send_sems.at[k],
            recv_sem=recv_sems.at[k],
            device_id=peer,
            device_id_type=mesh_id,
        )
        c.start()
        copies.append(c)
        return c

    own_g = pltpu.make_async_copy(wg_ref, g_ref.at[z, y], local_sems.at[0])
    own_u = pltpu.make_async_copy(wu_ref, u_ref.at[z, y], local_sems.at[1])
    own_g.start()
    own_u.start()

    g_from_ym = send(wg_ref, g_ref.at[z, y], to(z, yp))
    g_from_yp = send(wg_ref, g_ref.at[z, y], to(z, ym))
    u_from_zm = send(wu_ref, u_ref.at[z, y], to(zp, y))
    u_from_zp = send(wu_ref, u_ref.at[z, y], to(zm, y))
    gz = {"y": (send(wg_ref, g_ref.at[z, y], to(zp, y)), send(wg_ref, g_ref.at[z, y], to(zm, y)))}
    uy = {"z": (send(wu_ref, u_ref.at[z, y], to(z, yp)), send(wu_ref, u_ref.at[z, y], to(z, ym)))}

    g_from_ym.wait_recv()
    g_far_a = send(g_ref.at[z, ym, low], g_ref.at[z, ym, low], to(z, yp))
    gz["ym"] = (send(g_ref.at[z, ym], g_ref.at[z, ym], to(zp, y)), send(g_ref.at[z, ym], g_ref.at[z, ym], to(zm, y)))
    u_from_zm.wait_recv()
    u_far_a = send(u_ref.at[zm, y, low], u_ref.at[zm, y, low], to(zp, y))
    uy["zm"] = (send(u_ref.at[zm, y], u_ref.at[zm, y], to(z, yp)), send(u_ref.at[zm, y], u_ref.at[zm, y], to(z, ym)))
    g_from_yp.wait_recv()
    g_far_b = send(g_ref.at[z, yp, high], g_ref.at[z, yp, high], to(z, ym))
    gz["yp"] = (send(g_ref.at[z, yp], g_ref.at[z, yp], to(zp, y)), send(g_ref.at[z, yp], g_ref.at[z, yp], to(zm, y)))
    u_from_zp.wait_recv()
    u_far_b = send(u_ref.at[zp, y, high], u_ref.at[zp, y, high], to(zm, y))
    uy["zp"] = (send(u_ref.at[zp, y], u_ref.at[zp, y], to(z, yp)), send(u_ref.at[zp, y], u_ref.at[zp, y], to(z, ym)))

    g_far_a.wait_recv()
    g_far_b.wait_recv()
    gz["y2"] = (send(g_ref.at[z, y2], g_ref.at[z, y2], to(zp, y)), send(g_ref.at[z, y2], g_ref.at[z, y2], to(zm, y)))
    u_far_a.wait_recv()
    u_far_b.wait_recv()
    uy["z2"] = (send(u_ref.at[z2, y], u_ref.at[z2, y], to(z, yp)), send(u_ref.at[z2, y], u_ref.at[z2, y], to(z, ym)))

    for key, yy in (("y", y), ("ym", ym), ("yp", yp), ("y2", y2)):
        from_zm, from_zp = gz[key]
        from_zm.wait_recv()
        send(g_ref.at[zm, yy, low], g_ref.at[zm, yy, low], to(zp, y))
        from_zp.wait_recv()
        send(g_ref.at[zp, yy, high], g_ref.at[zp, yy, high], to(zm, y))
    for key, zz in (("z", z), ("zm", zm), ("zp", zp), ("z2", z2)):
        from_ym, from_yp = uy[key]
        from_ym.wait_recv()
        send(u_ref.at[zz, ym, low], u_ref.at[zz, ym, low], to(z, yp))
        from_yp.wait_recv()
        send(u_ref.at[zz, yp, high], u_ref.at[zz, yp, high], to(z, ym))

    waited = [g_from_ym, g_from_yp, u_from_zm, u_from_zp, g_far_a, g_far_b, u_far_a, u_far_b]
    waited += list(gz["y"]) + list(gz["ym"]) + list(gz["yp"]) + list(gz["y2"])
    waited += list(uy["z"]) + list(uy["zm"]) + list(uy["zp"]) + list(uy["z2"])
    for c in copies:
        if not any(c is w for w in waited):
            c.wait_recv()
    for c in copies:
        c.wait_send()
    own_g.wait()
    own_u.wait()


def gather_weights(w_gate, w_up, after):
    rows, cols = w_gate.shape
    any_spec = pl.BlockSpec(memory_space=pl.ANY)
    piece = jax.ShapeDtypeStruct((RING, RING, rows, cols), w_gate.dtype)
    return pl.pallas_call(
        gather_kernel,
        out_shape=(piece, piece),
        in_specs=[any_spec, any_spec, any_spec],
        out_specs=(any_spec, any_spec),
        scratch_shapes=[
            pltpu.SemaphoreType.DMA((40,)),
            pltpu.SemaphoreType.DMA((40,)),
            pltpu.SemaphoreType.DMA((2,)),
        ],
        compiler_params=pltpu.CompilerParams(collective_id=0, has_side_effects=True),
    )(w_gate, w_up, after)

def normalize(resid_rows, summed, gain_row):
    state = resid_rows.astype(jnp.float32) + summed
    scale_row = lax.rsqrt(jnp.mean(state * state, axis=-1, keepdims=True) + EPS)
    return (state * scale_row * gain_row).astype(jnp.bfloat16)


def shards(
    q_pre,
    k_pre,
    v_pre,
    q_bias,
    k_bias,
    v_bias,
    segment_ids,
    lengths,
    page_table,
    w_out,
    residual,
    norm_gain,
    w_gate,
    w_up,
):
    me_req = lax.axis_index("req")
    groups_all = lax.axis_size("req")
    block_rows = q_pre.shape[0]
    kv_heads = k_pre.shape[1] // HD
    q_heads = q_pre.shape[1] // HD
    group_size = q_heads // kv_heads


    own_lens = lax.dynamic_index_in_dim(lengths, me_req, 0, keepdims=False)
    own_pages = lax.dynamic_index_in_dim(page_table, me_req, 0, keepdims=False)
    own_owner = own_pages // REQS
    starts = jnp.cumsum(own_lens) - own_lens

    alive = segment_ids >= 0
    req_idx = jnp.clip(segment_ids - me_req * REQS, 0, REQS - 1)
    req_hit = req_idx[:, None] == jnp.arange(REQS)[None, :]
    row_start = jnp.sum(jnp.where(req_hit, starts[None, :], 0), axis=1)
    token = jnp.arange(block_rows, dtype=jnp.int32)
    positions = (token - row_start).astype(jnp.float32)
    keep = alive[:, None, None]

    queries = rotate(
        (q_pre.astype(jnp.float32) + q_bias).reshape(block_rows, q_heads, HD), positions
    )
    queries = jnp.where(keep, queries, 0.0).astype(jnp.bfloat16)
    keys = rotate((k_pre.astype(jnp.float32) + k_bias).reshape(block_rows, kv_heads, HD), positions)
    keys = jnp.where(keep, keys, 0.0).astype(jnp.bfloat16)
    values = (v_pre.astype(jnp.float32) + v_bias).reshape(block_rows, kv_heads, HD)
    values = jnp.where(keep, values, 0.0).astype(jnp.bfloat16)

    scale_factor = 1.0 / math.sqrt(HD)
    q_groups = queries.reshape(block_rows, kv_heads, group_size, HD)
    scores = (
        jnp.einsum("qhge,khe->hgqk", q_groups, keys, preferred_element_type=jnp.float32)
        * scale_factor
    )
    allowed = (
        (segment_ids[:, None] == segment_ids[None, :])
        & alive[None, :]
        & (token[None, :] <= token[:, None])
    )[None, None]
    row_max = jnp.max(jnp.where(allowed, scores, -1e30), axis=-1, keepdims=True)
    weights = jnp.where(allowed, jnp.exp(scores - row_max), 0.0)
    row_sum = jnp.sum(weights, axis=-1, keepdims=True)
    present = alive[None, None, :, None]
    probs = jnp.where(present, weights / jnp.where(present, row_sum, 1.0), 0.0).astype(
        jnp.bfloat16
    )
    attended = jnp.einsum("hgqk,khe->qhge", probs, values, preferred_element_type=jnp.float32)
    attended = attended.astype(jnp.bfloat16).reshape(block_rows, q_heads * HD)

    kv_rows = jnp.concatenate([keys, values], axis=-1).reshape(block_rows, -1)
    slot = jnp.arange(PAGE, dtype=jnp.int32)
    source = starts[:, None] + slot[None, :]
    live_slot = slot[None, :] < own_lens[:, None]
    owner_hit = own_owner[None, :] == jnp.arange(groups_all)[:, None]
    picks = (
        owner_hit[:, :, None, None]
        & live_slot[None, :, :, None]
        & (source[None, :, :, None] == token[None, None, None, :])
    )
    select = jnp.sum(picks.astype(jnp.int32), axis=1).astype(jnp.bfloat16)
    kv_send = jnp.einsum(
        "gst,tc->gsc", select, kv_rows, preferred_element_type=jnp.float32
    ).astype(jnp.bfloat16).reshape(groups_all, PAGE, kv_heads, 2 * HD)
    kv_in = lax.all_to_all(kv_send, "req", split_axis=0, concat_axis=0, tiled=True)
    hits = (
        page_table[None, :, :] == (me_req * REQS + jnp.arange(REQS, dtype=jnp.int32))[:, None, None]
    )
    page_select = jnp.sum(hits.astype(jnp.int32), axis=2).astype(jnp.bfloat16)
    cache_out = jnp.einsum(
        "ls,sphc->lhpc", page_select, kv_in, preferred_element_type=jnp.float32
    ).astype(jnp.bfloat16)

    product = jnp.dot(attended, w_out, preferred_element_type=jnp.float32).astype(jnp.bfloat16)
    summed = lax.psum(product, "mp").astype(jnp.float32)
    normed = normalize(residual, summed, norm_gain)
    g_full, u_full = gather_weights(w_gate, w_up, product[:8, :128])
    wg_full = g_full.reshape(-1, w_gate.shape[1])
    wu_full = u_full.reshape(-1, w_up.shape[1])
    gate_acc = jnp.dot(normed, wg_full, preferred_element_type=jnp.float32)
    up_acc = jnp.dot(normed, wu_full, preferred_element_type=jnp.float32)
    hidden = (jax.nn.silu(gate_acc) * up_acc).astype(jnp.bfloat16)
    return (hidden, cache_out)


def solution(mesh):
    in_specs = (
        P("req", "mp"),
        P("req", "mp"),
        P("req", "mp"),
        P("mp"),
        P("mp"),
        P("mp"),
        P("req"),
        P(),
        P(),
        P("mp", None),
        P("req", None),
        P(),
        P("req", "mp"),
        P("req", "mp"),
    )
    out_specs = (P("req", "mp"), P("req", "mp", None, None))
    return jax.shard_map(shards, mesh=mesh, in_specs=in_specs, out_specs=out_specs, check_vma=False)
```

```python
import math

import jax
import jax.numpy as jnp
from jax import lax
from jax.sharding import PartitionSpec as P
from jax.experimental import pallas as pl
from jax.experimental.pallas import tpu as pltpu

HD = 128
PAGE = 128
REQS = 4
RING = 4
KV_SEMS = 40


THETA = 1000000.0
EPS = 1e-06


def rotate(values, positions):
    half_dim = values.shape[-1] // 2
    frequencies = THETA ** (-jnp.arange(half_dim, dtype=jnp.float32) * (2.0 / values.shape[-1]))
    angles = positions[:, None] * frequencies[None, :]
    cosine = jnp.cos(angles)[:, None, :]
    sine_part = jnp.sin(angles)[:, None, :]
    first_half = values[..., :half_dim]
    second = values[..., half_dim:]
    return jnp.concatenate(
        [first_half * cosine - second * sine_part, second * cosine + first_half * sine_part],
        axis=-1,
    )


def gather_kernel(wg_ref, wu_ref, kv_ref, after_ref, g_ref, u_ref, kv_out, send_sems, recv_sems, local_sems):
    me = lax.axis_index("req")
    col = lax.axis_index("mp")
    z = me // RING
    y = me % RING
    yp = (y + 1) % RING
    ym = (y + RING - 1) % RING
    y2 = (y + 2) % RING
    zp = (z + 1) % RING
    zm = (z + RING - 1) % RING
    z2 = (z + 2) % RING
    rows = wg_ref.shape[0]
    low = pl.ds(0, rows // 2)
    high = pl.ds(rows // 2, rows - rows // 2)
    mesh_id = pl.DeviceIdType.MESH

    def to(zz, yy):
        return (zz * RING + yy, col)

    groups = kv_ref.shape[0]
    barrier = pltpu.get_barrier_semaphore()
    for d in range(1, groups):
        peer = ((me + d) % groups, col)
        pl.semaphore_signal(barrier, inc=1, device_id=peer, device_id_type=mesh_id)
    pl.semaphore_wait(barrier, groups - 1)

    copies = []
    own_kv = pltpu.make_async_copy(kv_ref.at[me], kv_out.at[me], local_sems.at[2])
    own_kv.start()
    for d in range(1, groups):
        dest = (me + d) % groups
        c = pltpu.make_async_remote_copy(
            src_ref=kv_ref.at[dest],
            dst_ref=kv_out.at[me],
            send_sem=send_sems.at[KV_SEMS + d - 1],
            recv_sem=recv_sems.at[KV_SEMS + d - 1],
            device_id=(dest, col),
            device_id_type=mesh_id,
        )
        c.start()
        copies.append(c)
    kv_copies = list(copies)
    copies.clear()

    def send(src, dst, peer):
        k = len(copies)
        c = pltpu.make_async_remote_copy(
            src_ref=src,
            dst_ref=dst,
            send_sem=send_sems.at[k],
            recv_sem=recv_sems.at[k],
            device_id=peer,
            device_id_type=mesh_id,
        )
        c.start()
        copies.append(c)
        return c

    own_g = pltpu.make_async_copy(wg_ref, g_ref.at[z, y], local_sems.at[0])
    own_u = pltpu.make_async_copy(wu_ref, u_ref.at[z, y], local_sems.at[1])
    own_g.start()
    own_u.start()

    g_from_ym = send(wg_ref, g_ref.at[z, y], to(z, yp))
    g_from_yp = send(wg_ref, g_ref.at[z, y], to(z, ym))
    u_from_zm = send(wu_ref, u_ref.at[z, y], to(zp, y))
    u_from_zp = send(wu_ref, u_ref.at[z, y], to(zm, y))
    gz = {"y": (send(wg_ref, g_ref.at[z, y], to(zp, y)), send(wg_ref, g_ref.at[z, y], to(zm, y)))}
    uy = {"z": (send(wu_ref, u_ref.at[z, y], to(z, yp)), send(wu_ref, u_ref.at[z, y], to(z, ym)))}

    g_from_ym.wait_recv()
    g_far_a = send(g_ref.at[z, ym, low], g_ref.at[z, ym, low], to(z, yp))
    gz["ym"] = (send(g_ref.at[z, ym], g_ref.at[z, ym], to(zp, y)), send(g_ref.at[z, ym], g_ref.at[z, ym], to(zm, y)))
    u_from_zm.wait_recv()
    u_far_a = send(u_ref.at[zm, y, low], u_ref.at[zm, y, low], to(zp, y))
    uy["zm"] = (send(u_ref.at[zm, y], u_ref.at[zm, y], to(z, yp)), send(u_ref.at[zm, y], u_ref.at[zm, y], to(z, ym)))
    g_from_yp.wait_recv()
    g_far_b = send(g_ref.at[z, yp, high], g_ref.at[z, yp, high], to(z, ym))
    gz["yp"] = (send(g_ref.at[z, yp], g_ref.at[z, yp], to(zp, y)), send(g_ref.at[z, yp], g_ref.at[z, yp], to(zm, y)))
    u_from_zp.wait_recv()
    u_far_b = send(u_ref.at[zp, y, high], u_ref.at[zp, y, high], to(zm, y))
    uy["zp"] = (send(u_ref.at[zp, y], u_ref.at[zp, y], to(z, yp)), send(u_ref.at[zp, y], u_ref.at[zp, y], to(z, ym)))

    g_far_a.wait_recv()
    g_far_b.wait_recv()
    gz["y2"] = (send(g_ref.at[z, y2], g_ref.at[z, y2], to(zp, y)), send(g_ref.at[z, y2], g_ref.at[z, y2], to(zm, y)))
    u_far_a.wait_recv()
    u_far_b.wait_recv()
    uy["z2"] = (send(u_ref.at[z2, y], u_ref.at[z2, y], to(z, yp)), send(u_ref.at[z2, y], u_ref.at[z2, y], to(z, ym)))

    for key, yy in (("y", y), ("ym", ym), ("yp", yp), ("y2", y2)):
        from_zm, from_zp = gz[key]
        from_zm.wait_recv()
        send(g_ref.at[zm, yy, low], g_ref.at[zm, yy, low], to(zp, y))
        from_zp.wait_recv()
        send(g_ref.at[zp, yy, high], g_ref.at[zp, yy, high], to(zm, y))
    for key, zz in (("z", z), ("zm", zm), ("zp", zp), ("z2", z2)):
        from_ym, from_yp = uy[key]
        from_ym.wait_recv()
        send(u_ref.at[zz, ym, low], u_ref.at[zz, ym, low], to(z, yp))
        from_yp.wait_recv()
        send(u_ref.at[zz, yp, high], u_ref.at[zz, yp, high], to(z, ym))

    waited = [g_from_ym, g_from_yp, u_from_zm, u_from_zp, g_far_a, g_far_b, u_far_a, u_far_b]
    waited += list(gz["y"]) + list(gz["ym"]) + list(gz["yp"]) + list(gz["y2"])
    waited += list(uy["z"]) + list(uy["zm"]) + list(uy["zp"]) + list(uy["z2"])
    for c in copies:
        if not any(c is w for w in waited):
            c.wait_recv()
    for c in copies:
        c.wait_send()
    for c in kv_copies:
        c.wait_recv()
        c.wait_send()
    own_g.wait()
    own_u.wait()
    own_kv.wait()


def gather_weights(w_gate, w_up, kv_send, after):
    rows, cols = w_gate.shape
    any_spec = pl.BlockSpec(memory_space=pl.ANY)
    piece = jax.ShapeDtypeStruct((RING, RING, rows, cols), w_gate.dtype)
    slots = jax.ShapeDtypeStruct(kv_send.shape, kv_send.dtype)
    sems = KV_SEMS + kv_send.shape[0] - 1
    return pl.pallas_call(
        gather_kernel,
        out_shape=(piece, piece, slots),
        in_specs=[any_spec, any_spec, any_spec, any_spec],
        out_specs=(any_spec, any_spec, any_spec),
        scratch_shapes=[
            pltpu.SemaphoreType.DMA((sems,)),
            pltpu.SemaphoreType.DMA((sems,)),
            pltpu.SemaphoreType.DMA((3,)),
        ],
        compiler_params=pltpu.CompilerParams(collective_id=0, has_side_effects=True),
    )(w_gate, w_up, kv_send, after)

def normalize(resid_rows, summed, gain_row):
    state = resid_rows.astype(jnp.float32) + summed
    scale_row = lax.rsqrt(jnp.mean(state * state, axis=-1, keepdims=True) + EPS)
    return (state * scale_row * gain_row).astype(jnp.bfloat16)


def shards(
    q_pre,
    k_pre,
    v_pre,
    q_bias,
    k_bias,
    v_bias,
    segment_ids,
    lengths,
    page_table,
    w_out,
    residual,
    norm_gain,
    w_gate,
    w_up,
):
    me_req = lax.axis_index("req")
    groups_all = lax.axis_size("req")
    block_rows = q_pre.shape[0]
    kv_heads = k_pre.shape[1] // HD
    q_heads = q_pre.shape[1] // HD
    group_size = q_heads // kv_heads


    own_lens = lax.dynamic_index_in_dim(lengths, me_req, 0, keepdims=False)
    own_pages = lax.dynamic_index_in_dim(page_table, me_req, 0, keepdims=False)
    own_owner = own_pages // REQS
    starts = jnp.cumsum(own_lens) - own_lens

    alive = segment_ids >= 0
    req_idx = jnp.clip(segment_ids - me_req * REQS, 0, REQS - 1)
    req_hit = req_idx[:, None] == jnp.arange(REQS)[None, :]
    row_start = jnp.sum(jnp.where(req_hit, starts[None, :], 0), axis=1)
    token = jnp.arange(block_rows, dtype=jnp.int32)
    positions = (token - row_start).astype(jnp.float32)
    keep = alive[:, None, None]

    queries = rotate(
        (q_pre.astype(jnp.float32) + q_bias).reshape(block_rows, q_heads, HD), positions
    )
    queries = jnp.where(keep, queries, 0.0).astype(jnp.bfloat16)
    keys = rotate((k_pre.astype(jnp.float32) + k_bias).reshape(block_rows, kv_heads, HD), positions)
    keys = jnp.where(keep, keys, 0.0).astype(jnp.bfloat16)
    values = (v_pre.astype(jnp.float32) + v_bias).reshape(block_rows, kv_heads, HD)
    values = jnp.where(keep, values, 0.0).astype(jnp.bfloat16)

    scale_factor = 1.0 / math.sqrt(HD)
    q_groups = queries.reshape(block_rows, kv_heads, group_size, HD)
    scores = (
        jnp.einsum("qhge,khe->hgqk", q_groups, keys, preferred_element_type=jnp.float32)
        * scale_factor
    )
    allowed = (
        (segment_ids[:, None] == segment_ids[None, :])
        & alive[None, :]
        & (token[None, :] <= token[:, None])
    )[None, None]
    row_max = jnp.max(jnp.where(allowed, scores, -1e30), axis=-1, keepdims=True)
    weights = jnp.where(allowed, jnp.exp(scores - row_max), 0.0)
    row_sum = jnp.sum(weights, axis=-1, keepdims=True)
    present = alive[None, None, :, None]
    probs = jnp.where(present, weights / jnp.where(present, row_sum, 1.0), 0.0).astype(
        jnp.bfloat16
    )
    attended = jnp.einsum("hgqk,khe->qhge", probs, values, preferred_element_type=jnp.float32)
    attended = attended.astype(jnp.bfloat16).reshape(block_rows, q_heads * HD)

    kv_rows = jnp.concatenate([keys, values], axis=-1).reshape(block_rows, -1)
    slot = jnp.arange(PAGE, dtype=jnp.int32)
    source = starts[:, None] + slot[None, :]
    live_slot = slot[None, :] < own_lens[:, None]
    owner_hit = own_owner[None, :] == jnp.arange(groups_all)[:, None]
    picks = (
        owner_hit[:, :, None, None]
        & live_slot[None, :, :, None]
        & (source[None, :, :, None] == token[None, None, None, :])
    )
    select = jnp.sum(picks.astype(jnp.int32), axis=1).astype(jnp.bfloat16)
    kv_send = jnp.einsum(
        "gst,tc->gsc", select, kv_rows, preferred_element_type=jnp.float32
    ).astype(jnp.bfloat16)
    hits = (
        page_table[None, :, :] == (me_req * REQS + jnp.arange(REQS, dtype=jnp.int32))[:, None, None]
    )
    page_select = jnp.sum(hits.astype(jnp.int32), axis=2).astype(jnp.bfloat16)

    product = jnp.dot(attended, w_out, preferred_element_type=jnp.float32).astype(jnp.bfloat16)
    summed = lax.psum(product, "mp").astype(jnp.float32)
    normed = normalize(residual, summed, norm_gain)
    g_full, u_full, kv_in = gather_weights(w_gate, w_up, kv_send, product[:8, :128])
    kv_in = kv_in.reshape(groups_all, PAGE, kv_heads, 2 * HD)
    cache_out = jnp.einsum(
        "ls,sphc->lhpc", page_select, kv_in, preferred_element_type=jnp.float32
    ).astype(jnp.bfloat16)
    wg_full = g_full.reshape(-1, w_gate.shape[1])
    wu_full = u_full.reshape(-1, w_up.shape[1])
    gate_acc = jnp.dot(normed, wg_full, preferred_element_type=jnp.float32)
    up_acc = jnp.dot(normed, wu_full, preferred_element_type=jnp.float32)
    hidden = (jax.nn.silu(gate_acc) * up_acc).astype(jnp.bfloat16)
    return (hidden, cache_out)


def solution(mesh):
    in_specs = (
        P("req", "mp"),
        P("req", "mp"),
        P("req", "mp"),
        P("mp"),
        P("mp"),
        P("mp"),
        P("req"),
        P(),
        P(),
        P("mp", None),
        P("req", None),
        P(),
        P("req", "mp"),
        P("req", "mp"),
    )
    out_specs = (P("req", "mp"), P("req", "mp", None, None))
    return jax.shard_map(shards, mesh=mesh, in_specs=in_specs, out_specs=out_specs, check_vma=False)
```

```python
import math

import jax
import jax.numpy as jnp
from jax import lax
from jax.sharding import PartitionSpec as P
from jax.experimental import pallas as pl
from jax.experimental.pallas import tpu as pltpu

HD = 128
PAGE = 128
REQS = 4
RING = 4
KV_SEMS = 36


THETA = 1000000.0
EPS = 1e-06


def rotate(values, positions):
    half_dim = values.shape[-1] // 2
    frequencies = THETA ** (-jnp.arange(half_dim, dtype=jnp.float32) * (2.0 / values.shape[-1]))
    angles = positions[:, None] * frequencies[None, :]
    cosine = jnp.cos(angles)[:, None, :]
    sine_part = jnp.sin(angles)[:, None, :]
    first_half = values[..., :half_dim]
    second = values[..., half_dim:]
    return jnp.concatenate(
        [first_half * cosine - second * sine_part, second * cosine + first_half * sine_part],
        axis=-1,
    )


def gather_kernel(
    wg_ref, wu_ref, gm_ref, gp_ref, um_ref, up_ref, kv_ref, after_ref,
    g_ref, u_ref, kv_out, send_sems, recv_sems, local_sems,
):
    me = lax.axis_index("req")
    col = lax.axis_index("mp")
    z = me // RING
    y = me % RING
    yp = (y + 1) % RING
    ym = (y + RING - 1) % RING
    y2 = (y + 2) % RING
    zp = (z + 1) % RING
    zm = (z + RING - 1) % RING
    z2 = (z + 2) % RING
    rows = wg_ref.shape[0]
    low = pl.ds(0, rows // 2)
    high = pl.ds(rows // 2, rows - rows // 2)
    mesh_id = pl.DeviceIdType.MESH

    def to(zz, yy):
        return (zz * RING + yy, col)

    groups = kv_ref.shape[0]
    barrier = pltpu.get_barrier_semaphore()
    for d in range(1, groups):
        peer = ((me + d) % groups, col)
        pl.semaphore_signal(barrier, inc=1, device_id=peer, device_id_type=mesh_id)
    pl.semaphore_wait(barrier, groups - 1)

    copies = []
    own_kv = pltpu.make_async_copy(kv_ref.at[me], kv_out.at[me], local_sems.at[6])
    own_kv.start()
    for d in range(1, groups):
        dest = (me + d) % groups
        c = pltpu.make_async_remote_copy(
            src_ref=kv_ref.at[dest],
            dst_ref=kv_out.at[me],
            send_sem=send_sems.at[KV_SEMS + d - 1],
            recv_sem=recv_sems.at[KV_SEMS + d - 1],
            device_id=(dest, col),
            device_id_type=mesh_id,
        )
        c.start()
        copies.append(c)
    kv_copies = list(copies)
    copies.clear()

    def send(src, dst, peer):
        k = len(copies)
        c = pltpu.make_async_remote_copy(
            src_ref=src,
            dst_ref=dst,
            send_sem=send_sems.at[k],
            recv_sem=recv_sems.at[k],
            device_id=peer,
            device_id_type=mesh_id,
        )
        c.start()
        copies.append(c)
        return c

    placed = []
    for k, (src_ref, dst_ref) in enumerate((
        (wg_ref, g_ref.at[z, y]),
        (wu_ref, u_ref.at[z, y]),
        (gm_ref, g_ref.at[z, ym]),
        (gp_ref, g_ref.at[z, yp]),
        (um_ref, u_ref.at[zm, y]),
        (up_ref, u_ref.at[zp, y]),
    )):
        c = pltpu.make_async_copy(src_ref, dst_ref, local_sems.at[k])
        c.start()
        placed.append(c)

    g_far_a = send(gm_ref.at[low], g_ref.at[z, ym, low], to(z, yp))
    g_far_b = send(gp_ref.at[high], g_ref.at[z, yp, high], to(z, ym))
    u_far_a = send(um_ref.at[low], u_ref.at[zm, y, low], to(zp, y))
    u_far_b = send(up_ref.at[high], u_ref.at[zp, y, high], to(zm, y))
    gz = {"y": (send(wg_ref, g_ref.at[z, y], to(zp, y)), send(wg_ref, g_ref.at[z, y], to(zm, y)))}
    uy = {"z": (send(wu_ref, u_ref.at[z, y], to(z, yp)), send(wu_ref, u_ref.at[z, y], to(z, ym)))}
    gz["ym"] = (send(gm_ref, g_ref.at[z, ym], to(zp, y)), send(gm_ref, g_ref.at[z, ym], to(zm, y)))
    uy["zm"] = (send(um_ref, u_ref.at[zm, y], to(z, yp)), send(um_ref, u_ref.at[zm, y], to(z, ym)))
    gz["yp"] = (send(gp_ref, g_ref.at[z, yp], to(zp, y)), send(gp_ref, g_ref.at[z, yp], to(zm, y)))
    uy["zp"] = (send(up_ref, u_ref.at[zp, y], to(z, yp)), send(up_ref, u_ref.at[zp, y], to(z, ym)))

    g_far_a.wait_recv()
    g_far_b.wait_recv()
    gz["y2"] = (send(g_ref.at[z, y2], g_ref.at[z, y2], to(zp, y)), send(g_ref.at[z, y2], g_ref.at[z, y2], to(zm, y)))
    u_far_a.wait_recv()
    u_far_b.wait_recv()
    uy["z2"] = (send(u_ref.at[z2, y], u_ref.at[z2, y], to(z, yp)), send(u_ref.at[z2, y], u_ref.at[z2, y], to(z, ym)))

    for key, yy in (("y", y), ("ym", ym), ("yp", yp), ("y2", y2)):
        from_zm, from_zp = gz[key]
        from_zm.wait_recv()
        send(g_ref.at[zm, yy, low], g_ref.at[zm, yy, low], to(zp, y))
        from_zp.wait_recv()
        send(g_ref.at[zp, yy, high], g_ref.at[zp, yy, high], to(zm, y))
    for key, zz in (("z", z), ("zm", zm), ("zp", zp), ("z2", z2)):
        from_ym, from_yp = uy[key]
        from_ym.wait_recv()
        send(u_ref.at[zz, ym, low], u_ref.at[zz, ym, low], to(z, yp))
        from_yp.wait_recv()
        send(u_ref.at[zz, yp, high], u_ref.at[zz, yp, high], to(z, ym))

    assert len(copies) <= KV_SEMS
    waited = [g_far_a, g_far_b, u_far_a, u_far_b]
    waited += list(gz["y"]) + list(gz["ym"]) + list(gz["yp"]) + list(gz["y2"])
    waited += list(uy["z"]) + list(uy["zm"]) + list(uy["zp"]) + list(uy["z2"])
    for c in copies:
        if not any(c is w for w in waited):
            c.wait_recv()
    for c in copies:
        c.wait_send()
    for c in kv_copies:
        c.wait_recv()
        c.wait_send()
    for c in placed:
        c.wait()
    own_kv.wait()


def y_shift(d, n):
    return [(i, (i // RING) * RING + (i % RING + d) % RING) for i in range(n)]


def z_shift(d, n):
    return [(i, ((i // RING + d) % RING) * RING + i % RING) for i in range(n)]


def first_hops(w_gate, w_up, n):
    return (
        lax.ppermute(w_gate, "req", y_shift(1, n)),
        lax.ppermute(w_gate, "req", y_shift(-1, n)),
        lax.ppermute(w_up, "req", z_shift(1, n)),
        lax.ppermute(w_up, "req", z_shift(-1, n)),
    )


def gather_weights(w_gate, w_up, hops, kv_send, after):
    rows, cols = w_gate.shape
    any_spec = pl.BlockSpec(memory_space=pl.ANY)
    piece = jax.ShapeDtypeStruct((RING, RING, rows, cols), w_gate.dtype)
    slots = jax.ShapeDtypeStruct(kv_send.shape, kv_send.dtype)
    sems = KV_SEMS + kv_send.shape[0] - 1
    return pl.pallas_call(
        gather_kernel,
        out_shape=(piece, piece, slots),
        in_specs=[any_spec] * 8,
        out_specs=(any_spec, any_spec, any_spec),
        scratch_shapes=[
            pltpu.SemaphoreType.DMA((sems,)),
            pltpu.SemaphoreType.DMA((sems,)),
            pltpu.SemaphoreType.DMA((7,)),
        ],
        compiler_params=pltpu.CompilerParams(collective_id=0, has_side_effects=True),
    )(w_gate, w_up, *hops, kv_send, after)

def normalize(resid_rows, summed, gain_row):
    state = resid_rows.astype(jnp.float32) + summed
    scale_row = lax.rsqrt(jnp.mean(state * state, axis=-1, keepdims=True) + EPS)
    return (state * scale_row * gain_row).astype(jnp.bfloat16)


def shards(
    q_pre,
    k_pre,
    v_pre,
    q_bias,
    k_bias,
    v_bias,
    segment_ids,
    lengths,
    page_table,
    w_out,
    residual,
    norm_gain,
    w_gate,
    w_up,
):
    me_req = lax.axis_index("req")
    groups_all = lax.axis_size("req")
    block_rows = q_pre.shape[0]
    kv_heads = k_pre.shape[1] // HD
    q_heads = q_pre.shape[1] // HD
    group_size = q_heads // kv_heads


    hops = first_hops(w_gate, w_up, groups_all)

    own_lens = lax.dynamic_index_in_dim(lengths, me_req, 0, keepdims=False)
    own_pages = lax.dynamic_index_in_dim(page_table, me_req, 0, keepdims=False)
    own_owner = own_pages // REQS
    starts = jnp.cumsum(own_lens) - own_lens

    alive = segment_ids >= 0
    req_idx = jnp.clip(segment_ids - me_req * REQS, 0, REQS - 1)
    req_hit = req_idx[:, None] == jnp.arange(REQS)[None, :]
    row_start = jnp.sum(jnp.where(req_hit, starts[None, :], 0), axis=1)
    token = jnp.arange(block_rows, dtype=jnp.int32)
    positions = (token - row_start).astype(jnp.float32)
    keep = alive[:, None, None]

    queries = rotate(
        (q_pre.astype(jnp.float32) + q_bias).reshape(block_rows, q_heads, HD), positions
    )
    queries = jnp.where(keep, queries, 0.0).astype(jnp.bfloat16)
    keys = rotate((k_pre.astype(jnp.float32) + k_bias).reshape(block_rows, kv_heads, HD), positions)
    keys = jnp.where(keep, keys, 0.0).astype(jnp.bfloat16)
    values = (v_pre.astype(jnp.float32) + v_bias).reshape(block_rows, kv_heads, HD)
    values = jnp.where(keep, values, 0.0).astype(jnp.bfloat16)

    scale_factor = 1.0 / math.sqrt(HD)
    q_groups = queries.reshape(block_rows, kv_heads, group_size, HD)
    scores = (
        jnp.einsum("qhge,khe->hgqk", q_groups, keys, preferred_element_type=jnp.float32)
        * scale_factor
    )
    allowed = (
        (segment_ids[:, None] == segment_ids[None, :])
        & alive[None, :]
        & (token[None, :] <= token[:, None])
    )[None, None]
    row_max = jnp.max(jnp.where(allowed, scores, -1e30), axis=-1, keepdims=True)
    weights = jnp.where(allowed, jnp.exp(scores - row_max), 0.0)
    row_sum = jnp.sum(weights, axis=-1, keepdims=True)
    present = alive[None, None, :, None]
    probs = jnp.where(present, weights / jnp.where(present, row_sum, 1.0), 0.0).astype(
        jnp.bfloat16
    )
    attended = jnp.einsum("hgqk,khe->qhge", probs, values, preferred_element_type=jnp.float32)
    attended = attended.astype(jnp.bfloat16).reshape(block_rows, q_heads * HD)

    kv_rows = jnp.concatenate([keys, values], axis=-1).reshape(block_rows, -1)
    slot = jnp.arange(PAGE, dtype=jnp.int32)
    source = starts[:, None] + slot[None, :]
    live_slot = slot[None, :] < own_lens[:, None]
    owner_hit = own_owner[None, :] == jnp.arange(groups_all)[:, None]
    picks = (
        owner_hit[:, :, None, None]
        & live_slot[None, :, :, None]
        & (source[None, :, :, None] == token[None, None, None, :])
    )
    select = jnp.sum(picks.astype(jnp.int32), axis=1).astype(jnp.bfloat16)
    kv_send = jnp.einsum(
        "gst,tc->gsc", select, kv_rows, preferred_element_type=jnp.float32
    ).astype(jnp.bfloat16)
    hits = (
        page_table[None, :, :] == (me_req * REQS + jnp.arange(REQS, dtype=jnp.int32))[:, None, None]
    )
    page_select = jnp.sum(hits.astype(jnp.int32), axis=2).astype(jnp.bfloat16)

    product = jnp.dot(attended, w_out, preferred_element_type=jnp.float32).astype(jnp.bfloat16)
    summed = lax.psum(product, "mp").astype(jnp.float32)
    normed = normalize(residual, summed, norm_gain)
    g_full, u_full, kv_in = gather_weights(w_gate, w_up, hops, kv_send, product[:8, :128])
    kv_in = kv_in.reshape(groups_all, PAGE, kv_heads, 2 * HD)
    cache_out = jnp.einsum(
        "ls,sphc->lhpc", page_select, kv_in, preferred_element_type=jnp.float32
    ).astype(jnp.bfloat16)
    wg_full = g_full.reshape(-1, w_gate.shape[1])
    wu_full = u_full.reshape(-1, w_up.shape[1])
    gate_acc = jnp.dot(normed, wg_full, preferred_element_type=jnp.float32)
    up_acc = jnp.dot(normed, wu_full, preferred_element_type=jnp.float32)
    hidden = (jax.nn.silu(gate_acc) * up_acc).astype(jnp.bfloat16)
    return (hidden, cache_out)


def solution(mesh):
    in_specs = (
        P("req", "mp"),
        P("req", "mp"),
        P("req", "mp"),
        P("mp"),
        P("mp"),
        P("mp"),
        P("req"),
        P(),
        P(),
        P("mp", None),
        P("req", None),
        P(),
        P("req", "mp"),
        P("req", "mp"),
    )
    out_specs = (P("req", "mp"), P("req", "mp", None, None))
    return jax.shard_map(shards, mesh=mesh, in_specs=in_specs, out_specs=out_specs, check_vma=False)
```

```python
import math

import jax
import jax.numpy as jnp
from jax import lax
from jax.sharding import PartitionSpec as P
from jax.experimental import pallas as pl
from jax.experimental.pallas import tpu as pltpu

HD = 128
PAGE = 128
REQS = 4
RING = 4
KV_SEMS = 40
AR_TILE = 512


THETA = 1000000.0
EPS = 1e-06


def rotate(values, positions):
    half_dim = values.shape[-1] // 2
    frequencies = THETA ** (-jnp.arange(half_dim, dtype=jnp.float32) * (2.0 / values.shape[-1]))
    angles = positions[:, None] * frequencies[None, :]
    cosine = jnp.cos(angles)[:, None, :]
    sine_part = jnp.sin(angles)[:, None, :]
    first_half = values[..., :half_dim]
    second = values[..., half_dim:]
    return jnp.concatenate(
        [first_half * cosine - second * sine_part, second * cosine + first_half * sine_part],
        axis=-1,
    )


def gather_kernel(
    wg_ref, wu_ref, kv_ref, prod_ref, g_ref, u_ref, kv_out, sum_ref,
    send_sems, recv_sems, local_sems, ar_send, ar_recv, a_buf, p_buf, b_src, b_buf, m_buf,
):
    me = lax.axis_index("req")
    col = lax.axis_index("mp")
    z = me // RING
    y = me % RING
    yp = (y + 1) % RING
    ym = (y + RING - 1) % RING
    y2 = (y + 2) % RING
    zp = (z + 1) % RING
    zm = (z + RING - 1) % RING
    z2 = (z + 2) % RING
    rows = wg_ref.shape[0]
    low = pl.ds(0, rows // 2)
    high = pl.ds(rows // 2, rows - rows // 2)
    mesh_id = pl.DeviceIdType.MESH

    def to(zz, yy):
        return (zz * RING + yy, col)

    groups = kv_ref.shape[0]
    xs = prod_ref.shape[0]
    cx = col // 2
    cc = col % 2
    core_peer = (me, cx * 2 + 1 - cc)
    x_peers = [(me, ((cx + d) % xs) * 2 + cc) for d in range(1, xs)]

    barrier = pltpu.get_barrier_semaphore()
    for d in range(1, groups):
        peer = ((me + d) % groups, col)
        pl.semaphore_signal(barrier, inc=1, device_id=peer, device_id_type=mesh_id)
    for peer in [core_peer] + x_peers:
        pl.semaphore_signal(barrier, inc=1, device_id=peer, device_id_type=mesh_id)
    pl.semaphore_wait(barrier, groups - 1 + xs)

    def ar_copy(k, src, dst, peer):
        c = pltpu.make_async_remote_copy(
            src_ref=src,
            dst_ref=dst,
            send_sem=ar_send.at[k],
            recv_sem=ar_recv.at[k],
            device_id=peer,
            device_id_type=mesh_id,
        )
        c.start()
        return c

    ar_a = ar_copy(0, prod_ref.at[:, 1 - cc], a_buf, core_peer)
    p_load = pltpu.make_async_copy(prod_ref.at[:, cc], p_buf, local_sems.at[3])
    p_load.start()
    width = AR_TILE
    tiles = a_buf.shape[-1] // width

    copies = []
    own_kv = pltpu.make_async_copy(kv_ref.at[me], kv_out.at[me], local_sems.at[2])
    own_kv.start()
    for d in range(1, groups):
        dest = (me + d) % groups
        c = pltpu.make_async_remote_copy(
            src_ref=kv_ref.at[dest],
            dst_ref=kv_out.at[me],
            send_sem=send_sems.at[KV_SEMS + d - 1],
            recv_sem=recv_sems.at[KV_SEMS + d - 1],
            device_id=(dest, col),
            device_id_type=mesh_id,
        )
        c.start()
        copies.append(c)
    kv_copies = list(copies)
    copies.clear()

    def send(src, dst, peer):
        k = len(copies)
        c = pltpu.make_async_remote_copy(
            src_ref=src,
            dst_ref=dst,
            send_sem=send_sems.at[k],
            recv_sem=recv_sems.at[k],
            device_id=peer,
            device_id_type=mesh_id,
        )
        c.start()
        copies.append(c)
        return c

    own_g = pltpu.make_async_copy(wg_ref, g_ref.at[z, y], local_sems.at[0])
    own_u = pltpu.make_async_copy(wu_ref, u_ref.at[z, y], local_sems.at[1])
    own_g.start()
    own_u.start()

    g_from_ym = send(wg_ref, g_ref.at[z, y], to(z, yp))
    g_from_yp = send(wg_ref, g_ref.at[z, y], to(z, ym))
    u_from_zm = send(wu_ref, u_ref.at[z, y], to(zp, y))
    u_from_zp = send(wu_ref, u_ref.at[z, y], to(zm, y))
    gz = {"y": (send(wg_ref, g_ref.at[z, y], to(zp, y)), send(wg_ref, g_ref.at[z, y], to(zm, y)))}
    uy = {"z": (send(wu_ref, u_ref.at[z, y], to(z, yp)), send(wu_ref, u_ref.at[z, y], to(z, ym)))}

    ar_a.wait_recv()
    p_load.wait()

    def add_pair(i, carry):
        xi = i // tiles
        cols = pl.ds(pl.multiple_of((i % tiles) * width, width), width)
        b_src[xi, :, cols] = p_buf[xi, :, cols].astype(jnp.float32) + a_buf[xi, :, cols].astype(
            jnp.float32
        )
        return carry

    lax.fori_loop(0, xs * tiles, add_pair, 0)
    ar_b = [
        ar_copy(d, b_src.at[(cx + d) % xs], b_buf.at[cx], x_peers[d - 1]) for d in range(1, xs)
    ]

    g_from_ym.wait_recv()
    g_far_a = send(g_ref.at[z, ym, low], g_ref.at[z, ym, low], to(z, yp))
    gz["ym"] = (send(g_ref.at[z, ym], g_ref.at[z, ym], to(zp, y)), send(g_ref.at[z, ym], g_ref.at[z, ym], to(zm, y)))
    u_from_zm.wait_recv()
    u_far_a = send(u_ref.at[zm, y, low], u_ref.at[zm, y, low], to(zp, y))
    uy["zm"] = (send(u_ref.at[zm, y], u_ref.at[zm, y], to(z, yp)), send(u_ref.at[zm, y], u_ref.at[zm, y], to(z, ym)))
    g_from_yp.wait_recv()
    g_far_b = send(g_ref.at[z, yp, high], g_ref.at[z, yp, high], to(z, ym))
    gz["yp"] = (send(g_ref.at[z, yp], g_ref.at[z, yp], to(zp, y)), send(g_ref.at[z, yp], g_ref.at[z, yp], to(zm, y)))
    u_from_zp.wait_recv()
    u_far_b = send(u_ref.at[zp, y, high], u_ref.at[zp, y, high], to(zm, y))
    uy["zp"] = (send(u_ref.at[zp, y], u_ref.at[zp, y], to(z, yp)), send(u_ref.at[zp, y], u_ref.at[zp, y], to(z, ym)))

    g_far_a.wait_recv()
    g_far_b.wait_recv()
    gz["y2"] = (send(g_ref.at[z, y2], g_ref.at[z, y2], to(zp, y)), send(g_ref.at[z, y2], g_ref.at[z, y2], to(zm, y)))
    u_far_a.wait_recv()
    u_far_b.wait_recv()
    uy["z2"] = (send(u_ref.at[z2, y], u_ref.at[z2, y], to(z, yp)), send(u_ref.at[z2, y], u_ref.at[z2, y], to(z, ym)))

    for c in ar_b:
        c.wait_recv()

    def add_chips(t, carry):
        cols = pl.ds(pl.multiple_of(t * width, width), width)
        acc = b_src[cx, :, cols]
        for d in range(1, xs):
            acc = acc + b_buf[(cx + d) % xs, :, cols]
        m_buf[:, cols] = acc.astype(m_buf.dtype)
        return carry

    lax.fori_loop(0, tiles, add_chips, 0)
    own_sum = pltpu.make_async_copy(m_buf, sum_ref.at[cx, cc], local_sems.at[4])
    own_sum.start()
    own_sum.wait()
    ar_c = [
        ar_copy(xs - 1 + d, sum_ref.at[cx, cc], sum_ref.at[cx, cc], x_peers[d - 1])
        for d in range(1, xs)
    ]

    for key, yy in (("y", y), ("ym", ym), ("yp", yp), ("y2", y2)):
        from_zm, from_zp = gz[key]
        from_zm.wait_recv()
        send(g_ref.at[zm, yy, low], g_ref.at[zm, yy, low], to(zp, y))
        from_zp.wait_recv()
        send(g_ref.at[zp, yy, high], g_ref.at[zp, yy, high], to(zm, y))
    for key, zz in (("z", z), ("zm", zm), ("zp", zp), ("z2", z2)):
        from_ym, from_yp = uy[key]
        from_ym.wait_recv()
        send(u_ref.at[zz, ym, low], u_ref.at[zz, ym, low], to(z, yp))
        from_yp.wait_recv()
        send(u_ref.at[zz, yp, high], u_ref.at[zz, yp, high], to(z, ym))

    for c in ar_c:
        c.wait_recv()
    ar_d = ar_copy(2 * xs - 1, sum_ref.at[:, cc], sum_ref.at[:, cc], core_peer)
    ar_d.wait_recv()
    for c in [ar_a] + ar_b + ar_c + [ar_d]:
        c.wait_send()

    waited = [g_from_ym, g_from_yp, u_from_zm, u_from_zp, g_far_a, g_far_b, u_far_a, u_far_b]
    waited += list(gz["y"]) + list(gz["ym"]) + list(gz["yp"]) + list(gz["y2"])
    waited += list(uy["z"]) + list(uy["zm"]) + list(uy["zp"]) + list(uy["z2"])
    for c in copies:
        if not any(c is w for w in waited):
            c.wait_recv()
    for c in copies:
        c.wait_send()
    for c in kv_copies:
        c.wait_recv()
        c.wait_send()
    own_g.wait()
    own_u.wait()
    own_kv.wait()


def gather_weights(w_gate, w_up, kv_send, product):
    rows, cols = w_gate.shape
    xs, _, chunk, width = product.shape
    any_spec = pl.BlockSpec(memory_space=pl.ANY)
    piece = jax.ShapeDtypeStruct((RING, RING, rows, cols), w_gate.dtype)
    slots = jax.ShapeDtypeStruct(kv_send.shape, kv_send.dtype)
    sums = jax.ShapeDtypeStruct(product.shape, product.dtype)
    sems = KV_SEMS + kv_send.shape[0] - 1
    return pl.pallas_call(
        gather_kernel,
        out_shape=(piece, piece, slots, sums),
        in_specs=[any_spec, any_spec, any_spec, any_spec],
        out_specs=(any_spec, any_spec, any_spec, any_spec),
        scratch_shapes=[
            pltpu.SemaphoreType.DMA((sems,)),
            pltpu.SemaphoreType.DMA((sems,)),
            pltpu.SemaphoreType.DMA((5,)),
            pltpu.SemaphoreType.DMA((2 * xs,)),
            pltpu.SemaphoreType.DMA((2 * xs,)),
            pltpu.VMEM((xs, chunk, width), product.dtype),
            pltpu.VMEM((xs, chunk, width), product.dtype),
            pltpu.VMEM((xs, chunk, width), jnp.float32),
            pltpu.VMEM((xs, chunk, width), jnp.float32),
            pltpu.VMEM((chunk, width), product.dtype),
        ],
        compiler_params=pltpu.CompilerParams(
            collective_id=0, has_side_effects=True, vmem_limit_bytes=48 * 1024 * 1024
        ),
    )(w_gate, w_up, kv_send, product)

def normalize(resid_rows, summed, gain_row):
    state = resid_rows.astype(jnp.float32) + summed
    scale_row = lax.rsqrt(jnp.mean(state * state, axis=-1, keepdims=True) + EPS)
    return (state * scale_row * gain_row).astype(jnp.bfloat16)


def shards(
    q_pre,
    k_pre,
    v_pre,
    q_bias,
    k_bias,
    v_bias,
    segment_ids,
    lengths,
    page_table,
    w_out,
    residual,
    norm_gain,
    w_gate,
    w_up,
):
    me_req = lax.axis_index("req")
    groups_all = lax.axis_size("req")
    block_rows = q_pre.shape[0]
    kv_heads = k_pre.shape[1] // HD
    q_heads = q_pre.shape[1] // HD
    group_size = q_heads // kv_heads


    own_lens = lax.dynamic_index_in_dim(lengths, me_req, 0, keepdims=False)
    own_pages = lax.dynamic_index_in_dim(page_table, me_req, 0, keepdims=False)
    own_owner = own_pages // REQS
    starts = jnp.cumsum(own_lens) - own_lens

    alive = segment_ids >= 0
    req_idx = jnp.clip(segment_ids - me_req * REQS, 0, REQS - 1)
    req_hit = req_idx[:, None] == jnp.arange(REQS)[None, :]
    row_start = jnp.sum(jnp.where(req_hit, starts[None, :], 0), axis=1)
    token = jnp.arange(block_rows, dtype=jnp.int32)
    positions = (token - row_start).astype(jnp.float32)
    keep = alive[:, None, None]

    queries = rotate(
        (q_pre.astype(jnp.float32) + q_bias).reshape(block_rows, q_heads, HD), positions
    )
    queries = jnp.where(keep, queries, 0.0).astype(jnp.bfloat16)
    keys = rotate((k_pre.astype(jnp.float32) + k_bias).reshape(block_rows, kv_heads, HD), positions)
    keys = jnp.where(keep, keys, 0.0).astype(jnp.bfloat16)
    values = (v_pre.astype(jnp.float32) + v_bias).reshape(block_rows, kv_heads, HD)
    values = jnp.where(keep, values, 0.0).astype(jnp.bfloat16)

    scale_factor = 1.0 / math.sqrt(HD)
    q_groups = queries.reshape(block_rows, kv_heads, group_size, HD)
    scores = (
        jnp.einsum("qhge,khe->hgqk", q_groups, keys, preferred_element_type=jnp.float32)
        * scale_factor
    )
    allowed = (
        (segment_ids[:, None] == segment_ids[None, :])
        & alive[None, :]
        & (token[None, :] <= token[:, None])
    )[None, None]
    row_max = jnp.max(jnp.where(allowed, scores, -1e30), axis=-1, keepdims=True)
    weights = jnp.where(allowed, jnp.exp(scores - row_max), 0.0)
    row_sum = jnp.sum(weights, axis=-1, keepdims=True)
    present = alive[None, None, :, None]
    probs = jnp.where(present, weights / jnp.where(present, row_sum, 1.0), 0.0).astype(
        jnp.bfloat16
    )
    attended = jnp.einsum("hgqk,khe->qhge", probs, values, preferred_element_type=jnp.float32)
    attended = attended.astype(jnp.bfloat16).reshape(block_rows, q_heads * HD)

    kv_rows = jnp.concatenate([keys, values], axis=-1).reshape(block_rows, -1)
    slot = jnp.arange(PAGE, dtype=jnp.int32)
    source = starts[:, None] + slot[None, :]
    live_slot = slot[None, :] < own_lens[:, None]
    owner_hit = own_owner[None, :] == jnp.arange(groups_all)[:, None]
    picks = (
        owner_hit[:, :, None, None]
        & live_slot[None, :, :, None]
        & (source[None, :, :, None] == token[None, None, None, :])
    )
    select = jnp.sum(picks.astype(jnp.int32), axis=1).astype(jnp.bfloat16)
    kv_send = jnp.einsum(
        "gst,tc->gsc", select, kv_rows, preferred_element_type=jnp.float32
    ).astype(jnp.bfloat16)
    hits = (
        page_table[None, :, :] == (me_req * REQS + jnp.arange(REQS, dtype=jnp.int32))[:, None, None]
    )
    page_select = jnp.sum(hits.astype(jnp.int32), axis=2).astype(jnp.bfloat16)

    product = jnp.dot(attended, w_out, preferred_element_type=jnp.float32).astype(jnp.bfloat16)
    n_mp = lax.axis_size("mp")
    product = product.reshape(n_mp // 2, 2, block_rows // n_mp, product.shape[-1])
    g_full, u_full, kv_in, summed = gather_weights(w_gate, w_up, kv_send, product)
    summed = summed.reshape(block_rows, -1).astype(jnp.float32)
    normed = normalize(residual, summed, norm_gain)
    kv_in = kv_in.reshape(groups_all, PAGE, kv_heads, 2 * HD)
    cache_out = jnp.einsum(
        "ls,sphc->lhpc", page_select, kv_in, preferred_element_type=jnp.float32
    ).astype(jnp.bfloat16)
    wg_full = g_full.reshape(-1, w_gate.shape[1])
    wu_full = u_full.reshape(-1, w_up.shape[1])
    gate_acc = jnp.dot(normed, wg_full, preferred_element_type=jnp.float32)
    up_acc = jnp.dot(normed, wu_full, preferred_element_type=jnp.float32)
    hidden = (jax.nn.silu(gate_acc) * up_acc).astype(jnp.bfloat16)
    return (hidden, cache_out)


def solution(mesh):
    in_specs = (
        P("req", "mp"),
        P("req", "mp"),
        P("req", "mp"),
        P("mp"),
        P("mp"),
        P("mp"),
        P("req"),
        P(),
        P(),
        P("mp", None),
        P("req", None),
        P(),
        P("req", "mp"),
        P("req", "mp"),
    )
    out_specs = (P("req", "mp"), P("req", "mp", None, None))
    return jax.shard_map(shards, mesh=mesh, in_specs=in_specs, out_specs=out_specs, check_vma=False)
```

```python
import math

import jax
import jax.numpy as jnp
from jax import lax
from jax.sharding import PartitionSpec as P
from jax.experimental import pallas as pl
from jax.experimental.pallas import tpu as pltpu

HD = 128
PAGE = 128
REQS = 4
RING = 4
KV_SEMS = 40
AR_TILE = 512


THETA = 1000000.0
EPS = 1e-06


def rotate(values, positions):
    half_dim = values.shape[-1] // 2
    frequencies = THETA ** (-jnp.arange(half_dim, dtype=jnp.float32) * (2.0 / values.shape[-1]))
    angles = positions[:, None] * frequencies[None, :]
    cosine = jnp.cos(angles)[:, None, :]
    sine_part = jnp.sin(angles)[:, None, :]
    first_half = values[..., :half_dim]
    second = values[..., half_dim:]
    return jnp.concatenate(
        [first_half * cosine - second * sine_part, second * cosine + first_half * sine_part],
        axis=-1,
    )


def gather_kernel(
    wg_ref, wu_ref, kv_ref, prod_ref, res_ref, gain_ref, g_ref, u_ref, kv_out, sum_ref,
    send_sems, recv_sems, local_sems, ar_send, ar_recv, a_buf, p_buf, b_src, b_buf, m_buf,
    r_buf, gain_buf,
):
    me = lax.axis_index("req")
    col = lax.axis_index("mp")
    z = me // RING
    y = me % RING
    yp = (y + 1) % RING
    ym = (y + RING - 1) % RING
    y2 = (y + 2) % RING
    zp = (z + 1) % RING
    zm = (z + RING - 1) % RING
    z2 = (z + 2) % RING
    rows = wg_ref.shape[0]
    low = pl.ds(0, rows // 2)
    high = pl.ds(rows // 2, rows - rows // 2)
    mesh_id = pl.DeviceIdType.MESH

    def to(zz, yy):
        return (zz * RING + yy, col)

    groups = kv_ref.shape[0]
    xs = prod_ref.shape[0]
    cx = col // 2
    cc = col % 2
    core_peer = (me, cx * 2 + 1 - cc)
    x_peers = [(me, ((cx + d) % xs) * 2 + cc) for d in range(1, xs)]

    barrier = pltpu.get_barrier_semaphore()
    for d in range(1, groups):
        peer = ((me + d) % groups, col)
        pl.semaphore_signal(barrier, inc=1, device_id=peer, device_id_type=mesh_id)
    for peer in [core_peer] + x_peers:
        pl.semaphore_signal(barrier, inc=1, device_id=peer, device_id_type=mesh_id)
    pl.semaphore_wait(barrier, groups - 1 + xs)

    def ar_copy(k, src, dst, peer):
        c = pltpu.make_async_remote_copy(
            src_ref=src,
            dst_ref=dst,
            send_sem=ar_send.at[k],
            recv_sem=ar_recv.at[k],
            device_id=peer,
            device_id_type=mesh_id,
        )
        c.start()
        return c

    ar_a = ar_copy(0, prod_ref.at[:, 1 - cc], a_buf, core_peer)
    p_load = pltpu.make_async_copy(prod_ref.at[:, cc], p_buf, local_sems.at[3])
    p_load.start()
    r_load = pltpu.make_async_copy(res_ref.at[cx, cc], r_buf, local_sems.at[5])
    r_load.start()
    g_load = pltpu.make_async_copy(gain_ref, gain_buf, local_sems.at[6])
    g_load.start()
    width = AR_TILE
    tiles = a_buf.shape[-1] // width

    copies = []
    own_kv = pltpu.make_async_copy(kv_ref.at[me], kv_out.at[me], local_sems.at[2])
    own_kv.start()
    for d in range(1, groups):
        dest = (me + d) % groups
        c = pltpu.make_async_remote_copy(
            src_ref=kv_ref.at[dest],
            dst_ref=kv_out.at[me],
            send_sem=send_sems.at[KV_SEMS + d - 1],
            recv_sem=recv_sems.at[KV_SEMS + d - 1],
            device_id=(dest, col),
            device_id_type=mesh_id,
        )
        c.start()
        copies.append(c)
    kv_copies = list(copies)
    copies.clear()

    def send(src, dst, peer):
        k = len(copies)
        c = pltpu.make_async_remote_copy(
            src_ref=src,
            dst_ref=dst,
            send_sem=send_sems.at[k],
            recv_sem=recv_sems.at[k],
            device_id=peer,
            device_id_type=mesh_id,
        )
        c.start()
        copies.append(c)
        return c

    own_g = pltpu.make_async_copy(wg_ref, g_ref.at[z, y], local_sems.at[0])
    own_u = pltpu.make_async_copy(wu_ref, u_ref.at[z, y], local_sems.at[1])
    own_g.start()
    own_u.start()

    g_from_ym = send(wg_ref, g_ref.at[z, y], to(z, yp))
    g_from_yp = send(wg_ref, g_ref.at[z, y], to(z, ym))
    u_from_zm = send(wu_ref, u_ref.at[z, y], to(zp, y))
    u_from_zp = send(wu_ref, u_ref.at[z, y], to(zm, y))
    gz = {"y": (send(wg_ref, g_ref.at[z, y], to(zp, y)), send(wg_ref, g_ref.at[z, y], to(zm, y)))}
    uy = {"z": (send(wu_ref, u_ref.at[z, y], to(z, yp)), send(wu_ref, u_ref.at[z, y], to(z, ym)))}

    ar_a.wait_recv()
    p_load.wait()

    def add_pair(i, carry):
        xi = i // tiles
        cols = pl.ds(pl.multiple_of((i % tiles) * width, width), width)
        b_src[xi, :, cols] = p_buf[xi, :, cols].astype(jnp.float32) + a_buf[xi, :, cols].astype(
            jnp.float32
        )
        return carry

    lax.fori_loop(0, xs * tiles, add_pair, 0)
    ar_b = [
        ar_copy(d, b_src.at[(cx + d) % xs], b_buf.at[cx], x_peers[d - 1]) for d in range(1, xs)
    ]

    g_from_ym.wait_recv()
    g_far_a = send(g_ref.at[z, ym, low], g_ref.at[z, ym, low], to(z, yp))
    gz["ym"] = (send(g_ref.at[z, ym], g_ref.at[z, ym], to(zp, y)), send(g_ref.at[z, ym], g_ref.at[z, ym], to(zm, y)))
    u_from_zm.wait_recv()
    u_far_a = send(u_ref.at[zm, y, low], u_ref.at[zm, y, low], to(zp, y))
    uy["zm"] = (send(u_ref.at[zm, y], u_ref.at[zm, y], to(z, yp)), send(u_ref.at[zm, y], u_ref.at[zm, y], to(z, ym)))
    g_from_yp.wait_recv()
    g_far_b = send(g_ref.at[z, yp, high], g_ref.at[z, yp, high], to(z, ym))
    gz["yp"] = (send(g_ref.at[z, yp], g_ref.at[z, yp], to(zp, y)), send(g_ref.at[z, yp], g_ref.at[z, yp], to(zm, y)))
    u_from_zp.wait_recv()
    u_far_b = send(u_ref.at[zp, y, high], u_ref.at[zp, y, high], to(zm, y))
    uy["zp"] = (send(u_ref.at[zp, y], u_ref.at[zp, y], to(z, yp)), send(u_ref.at[zp, y], u_ref.at[zp, y], to(z, ym)))

    g_far_a.wait_recv()
    g_far_b.wait_recv()
    gz["y2"] = (send(g_ref.at[z, y2], g_ref.at[z, y2], to(zp, y)), send(g_ref.at[z, y2], g_ref.at[z, y2], to(zm, y)))
    u_far_a.wait_recv()
    u_far_b.wait_recv()
    uy["z2"] = (send(u_ref.at[z2, y], u_ref.at[z2, y], to(z, yp)), send(u_ref.at[z2, y], u_ref.at[z2, y], to(z, ym)))

    for c in ar_b:
        c.wait_recv()

    r_load.wait()
    g_load.wait()

    def add_chips(t, squares):
        cols = pl.ds(pl.multiple_of(t * width, width), width)
        acc = b_src[cx, :, cols]
        for d in range(1, xs):
            acc = acc + b_buf[(cx + d) % xs, :, cols]
        state = acc + r_buf[:, cols].astype(jnp.float32)
        b_src[cx, :, cols] = state
        return squares + jnp.sum(state * state, axis=1, keepdims=True)

    squares = lax.fori_loop(0, tiles, add_chips, jnp.zeros((m_buf.shape[0], 1), jnp.float32))
    scale = lax.rsqrt(squares / m_buf.shape[1] + EPS)

    def scale_rows(t, carry):
        cols = pl.ds(pl.multiple_of(t * width, width), width)
        normed = b_src[cx, :, cols] * scale * gain_buf[:, cols]
        m_buf[:, cols] = normed.astype(m_buf.dtype)
        return carry

    lax.fori_loop(0, tiles, scale_rows, 0)
    own_sum = pltpu.make_async_copy(m_buf, sum_ref.at[cx, cc], local_sems.at[4])
    own_sum.start()
    own_sum.wait()
    ar_c = [
        ar_copy(xs - 1 + d, sum_ref.at[cx, cc], sum_ref.at[cx, cc], x_peers[d - 1])
        for d in range(1, xs)
    ]

    for key, yy in (("y", y), ("ym", ym), ("yp", yp), ("y2", y2)):
        from_zm, from_zp = gz[key]
        from_zm.wait_recv()
        send(g_ref.at[zm, yy, low], g_ref.at[zm, yy, low], to(zp, y))
        from_zp.wait_recv()
        send(g_ref.at[zp, yy, high], g_ref.at[zp, yy, high], to(zm, y))
    for key, zz in (("z", z), ("zm", zm), ("zp", zp), ("z2", z2)):
        from_ym, from_yp = uy[key]
        from_ym.wait_recv()
        send(u_ref.at[zz, ym, low], u_ref.at[zz, ym, low], to(z, yp))
        from_yp.wait_recv()
        send(u_ref.at[zz, yp, high], u_ref.at[zz, yp, high], to(z, ym))

    for c in ar_c:
        c.wait_recv()
    ar_d = ar_copy(2 * xs - 1, sum_ref.at[:, cc], sum_ref.at[:, cc], core_peer)
    ar_d.wait_recv()
    for c in [ar_a] + ar_b + ar_c + [ar_d]:
        c.wait_send()

    waited = [g_from_ym, g_from_yp, u_from_zm, u_from_zp, g_far_a, g_far_b, u_far_a, u_far_b]
    waited += list(gz["y"]) + list(gz["ym"]) + list(gz["yp"]) + list(gz["y2"])
    waited += list(uy["z"]) + list(uy["zm"]) + list(uy["zp"]) + list(uy["z2"])
    for c in copies:
        if not any(c is w for w in waited):
            c.wait_recv()
    for c in copies:
        c.wait_send()
    for c in kv_copies:
        c.wait_recv()
        c.wait_send()
    own_g.wait()
    own_u.wait()
    own_kv.wait()


def gather_weights(w_gate, w_up, kv_send, product, residual, gain):
    rows, cols = w_gate.shape
    xs, _, chunk, width = product.shape
    any_spec = pl.BlockSpec(memory_space=pl.ANY)
    piece = jax.ShapeDtypeStruct((RING, RING, rows, cols), w_gate.dtype)
    slots = jax.ShapeDtypeStruct(kv_send.shape, kv_send.dtype)
    sums = jax.ShapeDtypeStruct(product.shape, product.dtype)
    sems = KV_SEMS + kv_send.shape[0] - 1
    return pl.pallas_call(
        gather_kernel,
        out_shape=(piece, piece, slots, sums),
        in_specs=[any_spec] * 6,
        out_specs=(any_spec, any_spec, any_spec, any_spec),
        scratch_shapes=[
            pltpu.SemaphoreType.DMA((sems,)),
            pltpu.SemaphoreType.DMA((sems,)),
            pltpu.SemaphoreType.DMA((7,)),
            pltpu.SemaphoreType.DMA((2 * xs,)),
            pltpu.SemaphoreType.DMA((2 * xs,)),
            pltpu.VMEM((xs, chunk, width), product.dtype),
            pltpu.VMEM((xs, chunk, width), product.dtype),
            pltpu.VMEM((xs, chunk, width), jnp.float32),
            pltpu.VMEM((xs, chunk, width), jnp.float32),
            pltpu.VMEM((chunk, width), product.dtype),
            pltpu.VMEM((chunk, width), residual.dtype),
            pltpu.VMEM((1, width), jnp.float32),
        ],
        compiler_params=pltpu.CompilerParams(
            collective_id=0, has_side_effects=True, vmem_limit_bytes=48 * 1024 * 1024
        ),
    )(w_gate, w_up, kv_send, product, residual, gain)

def normalize(resid_rows, summed, gain_row):
    state = resid_rows.astype(jnp.float32) + summed
    scale_row = lax.rsqrt(jnp.mean(state * state, axis=-1, keepdims=True) + EPS)
    return (state * scale_row * gain_row).astype(jnp.bfloat16)


def shards(
    q_pre,
    k_pre,
    v_pre,
    q_bias,
    k_bias,
    v_bias,
    segment_ids,
    lengths,
    page_table,
    w_out,
    residual,
    norm_gain,
    w_gate,
    w_up,
):
    me_req = lax.axis_index("req")
    groups_all = lax.axis_size("req")
    block_rows = q_pre.shape[0]
    kv_heads = k_pre.shape[1] // HD
    q_heads = q_pre.shape[1] // HD
    group_size = q_heads // kv_heads


    own_lens = lax.dynamic_index_in_dim(lengths, me_req, 0, keepdims=False)
    own_pages = lax.dynamic_index_in_dim(page_table, me_req, 0, keepdims=False)
    own_owner = own_pages // REQS
    starts = jnp.cumsum(own_lens) - own_lens

    alive = segment_ids >= 0
    req_idx = jnp.clip(segment_ids - me_req * REQS, 0, REQS - 1)
    req_hit = req_idx[:, None] == jnp.arange(REQS)[None, :]
    row_start = jnp.sum(jnp.where(req_hit, starts[None, :], 0), axis=1)
    token = jnp.arange(block_rows, dtype=jnp.int32)
    positions = (token - row_start).astype(jnp.float32)
    keep = alive[:, None, None]

    queries = rotate(
        (q_pre.astype(jnp.float32) + q_bias).reshape(block_rows, q_heads, HD), positions
    )
    queries = jnp.where(keep, queries, 0.0).astype(jnp.bfloat16)
    keys = rotate((k_pre.astype(jnp.float32) + k_bias).reshape(block_rows, kv_heads, HD), positions)
    keys = jnp.where(keep, keys, 0.0).astype(jnp.bfloat16)
    values = (v_pre.astype(jnp.float32) + v_bias).reshape(block_rows, kv_heads, HD)
    values = jnp.where(keep, values, 0.0).astype(jnp.bfloat16)

    scale_factor = 1.0 / math.sqrt(HD)
    q_groups = queries.reshape(block_rows, kv_heads, group_size, HD)
    scores = (
        jnp.einsum("qhge,khe->hgqk", q_groups, keys, preferred_element_type=jnp.float32)
        * scale_factor
    )
    allowed = (
        (segment_ids[:, None] == segment_ids[None, :])
        & alive[None, :]
        & (token[None, :] <= token[:, None])
    )[None, None]
    row_max = jnp.max(jnp.where(allowed, scores, -1e30), axis=-1, keepdims=True)
    weights = jnp.where(allowed, jnp.exp(scores - row_max), 0.0)
    row_sum = jnp.sum(weights, axis=-1, keepdims=True)
    present = alive[None, None, :, None]
    probs = jnp.where(present, weights / jnp.where(present, row_sum, 1.0), 0.0).astype(
        jnp.bfloat16
    )
    attended = jnp.einsum("hgqk,khe->qhge", probs, values, preferred_element_type=jnp.float32)
    attended = attended.astype(jnp.bfloat16).reshape(block_rows, q_heads * HD)

    kv_rows = jnp.concatenate([keys, values], axis=-1).reshape(block_rows, -1)
    slot = jnp.arange(PAGE, dtype=jnp.int32)
    source = starts[:, None] + slot[None, :]
    live_slot = slot[None, :] < own_lens[:, None]
    owner_hit = own_owner[None, :] == jnp.arange(groups_all)[:, None]
    picks = (
        owner_hit[:, :, None, None]
        & live_slot[None, :, :, None]
        & (source[None, :, :, None] == token[None, None, None, :])
    )
    select = jnp.sum(picks.astype(jnp.int32), axis=1).astype(jnp.bfloat16)
    kv_send = jnp.einsum(
        "gst,tc->gsc", select, kv_rows, preferred_element_type=jnp.float32
    ).astype(jnp.bfloat16)
    hits = (
        page_table[None, :, :] == (me_req * REQS + jnp.arange(REQS, dtype=jnp.int32))[:, None, None]
    )
    page_select = jnp.sum(hits.astype(jnp.int32), axis=2).astype(jnp.bfloat16)

    product = jnp.dot(attended, w_out, preferred_element_type=jnp.float32).astype(jnp.bfloat16)
    n_mp = lax.axis_size("mp")
    product = product.reshape(n_mp // 2, 2, block_rows // n_mp, product.shape[-1])
    g_full, u_full, kv_in, normed = gather_weights(
        w_gate,
        w_up,
        kv_send,
        product,
        residual.reshape(product.shape),
        norm_gain.reshape(1, -1).astype(jnp.float32),
    )
    normed = normed.reshape(block_rows, -1)
    kv_in = kv_in.reshape(groups_all, PAGE, kv_heads, 2 * HD)
    cache_out = jnp.einsum(
        "ls,sphc->lhpc", page_select, kv_in, preferred_element_type=jnp.float32
    ).astype(jnp.bfloat16)
    wg_full = g_full.reshape(-1, w_gate.shape[1])
    wu_full = u_full.reshape(-1, w_up.shape[1])
    gate_acc = jnp.dot(normed, wg_full, preferred_element_type=jnp.float32)
    up_acc = jnp.dot(normed, wu_full, preferred_element_type=jnp.float32)
    hidden = (jax.nn.silu(gate_acc) * up_acc).astype(jnp.bfloat16)
    return (hidden, cache_out)


def solution(mesh):
    in_specs = (
        P("req", "mp"),
        P("req", "mp"),
        P("req", "mp"),
        P("mp"),
        P("mp"),
        P("mp"),
        P("req"),
        P(),
        P(),
        P("mp", None),
        P("req", None),
        P(),
        P("req", "mp"),
        P("req", "mp"),
    )
    out_specs = (P("req", "mp"), P("req", "mp", None, None))
    return jax.shard_map(shards, mesh=mesh, in_specs=in_specs, out_specs=out_specs, check_vma=False)
```

```python
import math

import jax
import jax.numpy as jnp
from jax import lax
from jax.sharding import PartitionSpec as P
from jax.experimental import pallas as pl
from jax.experimental.pallas import tpu as pltpu

HD = 128
PAGE = 128
REQS = 4
RING = 4
KV_SEMS = 40
AR_TILE = 512


THETA = 1000000.0
EPS = 1e-06


def rotate(values, positions):
    half_dim = values.shape[-1] // 2
    frequencies = THETA ** (-jnp.arange(half_dim, dtype=jnp.float32) * (2.0 / values.shape[-1]))
    angles = positions[:, None] * frequencies[None, :]
    cosine = jnp.cos(angles)[:, None, :]
    sine_part = jnp.sin(angles)[:, None, :]
    first_half = values[..., :half_dim]
    second = values[..., half_dim:]
    return jnp.concatenate(
        [first_half * cosine - second * sine_part, second * cosine + first_half * sine_part],
        axis=-1,
    )


def gather_kernel(
    wg_ref, wu_ref, kv_ref, prod_ref, res_ref, gain_ref, g_ref, u_ref, kv_out, sum_ref,
    send_sems, recv_sems, local_sems, ar_send, ar_recv, a_buf, p_buf, b_src, b_buf, m_buf,
    r_buf, gain_buf,
):
    me = lax.axis_index("req")
    col = lax.axis_index("mp")
    z = me // RING
    y = me % RING
    yp = (y + 1) % RING
    ym = (y + RING - 1) % RING
    y2 = (y + 2) % RING
    zp = (z + 1) % RING
    zm = (z + RING - 1) % RING
    z2 = (z + 2) % RING
    rows = wg_ref.shape[0]
    low = pl.ds(0, rows // 2)
    high = pl.ds(rows // 2, rows - rows // 2)
    mesh_id = pl.DeviceIdType.MESH

    def to(zz, yy):
        return (zz * RING + yy, col)

    groups = kv_ref.shape[0]
    xs = prod_ref.shape[0]
    cx = col // 2
    cc = col % 2
    core_peer = (me, cx * 2 + 1 - cc)
    x_peers = [(me, ((cx + d) % xs) * 2 + cc) for d in range(1, xs)]

    barrier = pltpu.get_barrier_semaphore()
    for d in range(1, groups):
        peer = ((me + d) % groups, col)
        pl.semaphore_signal(barrier, inc=1, device_id=peer, device_id_type=mesh_id)
    for peer in [core_peer] + x_peers:
        pl.semaphore_signal(barrier, inc=1, device_id=peer, device_id_type=mesh_id)
    pl.semaphore_wait(barrier, groups - 1 + xs)

    def ar_copy(k, src, dst, peer):
        c = pltpu.make_async_remote_copy(
            src_ref=src,
            dst_ref=dst,
            send_sem=ar_send.at[k],
            recv_sem=ar_recv.at[k],
            device_id=peer,
            device_id_type=mesh_id,
        )
        c.start()
        return c

    ar_a = ar_copy(0, prod_ref.at[:, 1 - cc], a_buf, core_peer)
    p_load = pltpu.make_async_copy(prod_ref.at[:, cc], p_buf, local_sems.at[3])
    p_load.start()
    r_load = pltpu.make_async_copy(res_ref.at[cx, cc], r_buf, local_sems.at[5])
    r_load.start()
    g_load = pltpu.make_async_copy(gain_ref, gain_buf, local_sems.at[6])
    g_load.start()
    width = AR_TILE
    tiles = a_buf.shape[-1] // width

    copies = []

    def send(src, dst, peer):
        k = len(copies)
        c = pltpu.make_async_remote_copy(
            src_ref=src,
            dst_ref=dst,
            send_sem=send_sems.at[k],
            recv_sem=recv_sems.at[k],
            device_id=peer,
            device_id_type=mesh_id,
        )
        c.start()
        copies.append(c)
        return c

    own_g = pltpu.make_async_copy(wg_ref, g_ref.at[z, y], local_sems.at[0])
    own_u = pltpu.make_async_copy(wu_ref, u_ref.at[z, y], local_sems.at[1])
    own_g.start()
    own_u.start()

    g_from_ym = send(wg_ref, g_ref.at[z, y], to(z, yp))
    g_from_yp = send(wg_ref, g_ref.at[z, y], to(z, ym))
    u_from_zm = send(wu_ref, u_ref.at[z, y], to(zp, y))
    u_from_zp = send(wu_ref, u_ref.at[z, y], to(zm, y))
    gz = {"y": (send(wg_ref, g_ref.at[z, y], to(zp, y)), send(wg_ref, g_ref.at[z, y], to(zm, y)))}
    uy = {"z": (send(wu_ref, u_ref.at[z, y], to(z, yp)), send(wu_ref, u_ref.at[z, y], to(z, ym)))}
    kv_copies = []
    own_kv = pltpu.make_async_copy(kv_ref.at[me], kv_out.at[me], local_sems.at[2])
    own_kv.start()
    for d in range(1, groups):
        dest = (me + d) % groups
        c = pltpu.make_async_remote_copy(
            src_ref=kv_ref.at[dest],
            dst_ref=kv_out.at[me],
            send_sem=send_sems.at[KV_SEMS + d - 1],
            recv_sem=recv_sems.at[KV_SEMS + d - 1],
            device_id=(dest, col),
            device_id_type=mesh_id,
        )
        c.start()
        kv_copies.append(c)

    ar_a.wait_recv()
    p_load.wait()

    def add_pair(i, carry):
        xi = i // tiles
        cols = pl.ds(pl.multiple_of((i % tiles) * width, width), width)
        b_src[xi, :, cols] = p_buf[xi, :, cols].astype(jnp.float32) + a_buf[xi, :, cols].astype(
            jnp.float32
        )
        return carry

    lax.fori_loop(0, xs * tiles, add_pair, 0)
    ar_b = [
        ar_copy(d, b_src.at[(cx + d) % xs], b_buf.at[cx], x_peers[d - 1]) for d in range(1, xs)
    ]

    g_from_ym.wait_recv()
    g_far_a = send(g_ref.at[z, ym, low], g_ref.at[z, ym, low], to(z, yp))
    gz["ym"] = (send(g_ref.at[z, ym], g_ref.at[z, ym], to(zp, y)), send(g_ref.at[z, ym], g_ref.at[z, ym], to(zm, y)))
    u_from_zm.wait_recv()
    u_far_a = send(u_ref.at[zm, y, low], u_ref.at[zm, y, low], to(zp, y))
    uy["zm"] = (send(u_ref.at[zm, y], u_ref.at[zm, y], to(z, yp)), send(u_ref.at[zm, y], u_ref.at[zm, y], to(z, ym)))
    g_from_yp.wait_recv()
    g_far_b = send(g_ref.at[z, yp, high], g_ref.at[z, yp, high], to(z, ym))
    gz["yp"] = (send(g_ref.at[z, yp], g_ref.at[z, yp], to(zp, y)), send(g_ref.at[z, yp], g_ref.at[z, yp], to(zm, y)))
    u_from_zp.wait_recv()
    u_far_b = send(u_ref.at[zp, y, high], u_ref.at[zp, y, high], to(zm, y))
    uy["zp"] = (send(u_ref.at[zp, y], u_ref.at[zp, y], to(z, yp)), send(u_ref.at[zp, y], u_ref.at[zp, y], to(z, ym)))

    g_far_a.wait_recv()
    g_far_b.wait_recv()
    gz["y2"] = (send(g_ref.at[z, y2], g_ref.at[z, y2], to(zp, y)), send(g_ref.at[z, y2], g_ref.at[z, y2], to(zm, y)))
    u_far_a.wait_recv()
    u_far_b.wait_recv()
    uy["z2"] = (send(u_ref.at[z2, y], u_ref.at[z2, y], to(z, yp)), send(u_ref.at[z2, y], u_ref.at[z2, y], to(z, ym)))

    for c in ar_b:
        c.wait_recv()

    r_load.wait()
    g_load.wait()

    def add_chips(t, squares):
        cols = pl.ds(pl.multiple_of(t * width, width), width)
        acc = b_src[cx, :, cols]
        for d in range(1, xs):
            acc = acc + b_buf[(cx + d) % xs, :, cols]
        state = acc + r_buf[:, cols].astype(jnp.float32)
        b_src[cx, :, cols] = state
        return squares + jnp.sum(state * state, axis=1, keepdims=True)

    squares = lax.fori_loop(0, tiles, add_chips, jnp.zeros((m_buf.shape[0], 1), jnp.float32))
    scale = lax.rsqrt(squares / m_buf.shape[1] + EPS)

    def scale_rows(t, carry):
        cols = pl.ds(pl.multiple_of(t * width, width), width)
        normed = b_src[cx, :, cols] * scale * gain_buf[:, cols]
        m_buf[:, cols] = normed.astype(m_buf.dtype)
        return carry

    lax.fori_loop(0, tiles, scale_rows, 0)
    own_sum = pltpu.make_async_copy(m_buf, sum_ref.at[cx, cc], local_sems.at[4])
    own_sum.start()
    own_sum.wait()
    ar_c = [
        ar_copy(xs - 1 + d, sum_ref.at[cx, cc], sum_ref.at[cx, cc], x_peers[d - 1])
        for d in range(1, xs)
    ]

    for key, yy in (("y", y), ("ym", ym), ("yp", yp), ("y2", y2)):
        from_zm, from_zp = gz[key]
        from_zm.wait_recv()
        send(g_ref.at[zm, yy, low], g_ref.at[zm, yy, low], to(zp, y))
        from_zp.wait_recv()
        send(g_ref.at[zp, yy, high], g_ref.at[zp, yy, high], to(zm, y))
    for key, zz in (("z", z), ("zm", zm), ("zp", zp), ("z2", z2)):
        from_ym, from_yp = uy[key]
        from_ym.wait_recv()
        send(u_ref.at[zz, ym, low], u_ref.at[zz, ym, low], to(z, yp))
        from_yp.wait_recv()
        send(u_ref.at[zz, yp, high], u_ref.at[zz, yp, high], to(z, ym))

    for c in ar_c:
        c.wait_recv()
    ar_d = ar_copy(2 * xs - 1, sum_ref.at[:, cc], sum_ref.at[:, cc], core_peer)
    ar_d.wait_recv()
    for c in [ar_a] + ar_b + ar_c + [ar_d]:
        c.wait_send()

    waited = [g_from_ym, g_from_yp, u_from_zm, u_from_zp, g_far_a, g_far_b, u_far_a, u_far_b]
    waited += list(gz["y"]) + list(gz["ym"]) + list(gz["yp"]) + list(gz["y2"])
    waited += list(uy["z"]) + list(uy["zm"]) + list(uy["zp"]) + list(uy["z2"])
    for c in copies:
        if not any(c is w for w in waited):
            c.wait_recv()
    for c in copies:
        c.wait_send()
    for c in kv_copies:
        c.wait_recv()
        c.wait_send()
    own_g.wait()
    own_u.wait()
    own_kv.wait()


def gather_weights(w_gate, w_up, kv_send, product, residual, gain):
    rows, cols = w_gate.shape
    xs, _, chunk, width = product.shape
    any_spec = pl.BlockSpec(memory_space=pl.ANY)
    piece = jax.ShapeDtypeStruct((RING, RING, rows, cols), w_gate.dtype)
    slots = jax.ShapeDtypeStruct(kv_send.shape, kv_send.dtype)
    sums = jax.ShapeDtypeStruct(product.shape, product.dtype)
    sems = KV_SEMS + kv_send.shape[0] - 1
    return pl.pallas_call(
        gather_kernel,
        out_shape=(piece, piece, slots, sums),
        in_specs=[any_spec] * 6,
        out_specs=(any_spec, any_spec, any_spec, any_spec),
        scratch_shapes=[
            pltpu.SemaphoreType.DMA((sems,)),
            pltpu.SemaphoreType.DMA((sems,)),
            pltpu.SemaphoreType.DMA((7,)),
            pltpu.SemaphoreType.DMA((2 * xs,)),
            pltpu.SemaphoreType.DMA((2 * xs,)),
            pltpu.VMEM((xs, chunk, width), product.dtype),
            pltpu.VMEM((xs, chunk, width), product.dtype),
            pltpu.VMEM((xs, chunk, width), jnp.float32),
            pltpu.VMEM((xs, chunk, width), jnp.float32),
            pltpu.VMEM((chunk, width), product.dtype),
            pltpu.VMEM((chunk, width), residual.dtype),
            pltpu.VMEM((1, width), jnp.float32),
        ],
        compiler_params=pltpu.CompilerParams(
            collective_id=0, has_side_effects=True, vmem_limit_bytes=48 * 1024 * 1024
        ),
    )(w_gate, w_up, kv_send, product, residual, gain)

def normalize(resid_rows, summed, gain_row):
    state = resid_rows.astype(jnp.float32) + summed
    scale_row = lax.rsqrt(jnp.mean(state * state, axis=-1, keepdims=True) + EPS)
    return (state * scale_row * gain_row).astype(jnp.bfloat16)


def shards(
    q_pre,
    k_pre,
    v_pre,
    q_bias,
    k_bias,
    v_bias,
    segment_ids,
    lengths,
    page_table,
    w_out,
    residual,
    norm_gain,
    w_gate,
    w_up,
):
    me_req = lax.axis_index("req")
    groups_all = lax.axis_size("req")
    block_rows = q_pre.shape[0]
    kv_heads = k_pre.shape[1] // HD
    q_heads = q_pre.shape[1] // HD
    group_size = q_heads // kv_heads


    own_lens = lax.dynamic_index_in_dim(lengths, me_req, 0, keepdims=False)
    own_pages = lax.dynamic_index_in_dim(page_table, me_req, 0, keepdims=False)
    own_owner = own_pages // REQS
    starts = jnp.cumsum(own_lens) - own_lens

    alive = segment_ids >= 0
    req_idx = jnp.clip(segment_ids - me_req * REQS, 0, REQS - 1)
    req_hit = req_idx[:, None] == jnp.arange(REQS)[None, :]
    row_start = jnp.sum(jnp.where(req_hit, starts[None, :], 0), axis=1)
    token = jnp.arange(block_rows, dtype=jnp.int32)
    positions = (token - row_start).astype(jnp.float32)
    keep = alive[:, None, None]

    queries = rotate(
        (q_pre.astype(jnp.float32) + q_bias).reshape(block_rows, q_heads, HD), positions
    )
    queries = jnp.where(keep, queries, 0.0).astype(jnp.bfloat16)
    keys = rotate((k_pre.astype(jnp.float32) + k_bias).reshape(block_rows, kv_heads, HD), positions)
    keys = jnp.where(keep, keys, 0.0).astype(jnp.bfloat16)
    values = (v_pre.astype(jnp.float32) + v_bias).reshape(block_rows, kv_heads, HD)
    values = jnp.where(keep, values, 0.0).astype(jnp.bfloat16)

    scale_factor = 1.0 / math.sqrt(HD)
    q_groups = queries.reshape(block_rows, kv_heads, group_size, HD)
    scores = (
        jnp.einsum("qhge,khe->hgqk", q_groups, keys, preferred_element_type=jnp.float32)
        * scale_factor
    )
    allowed = (
        (segment_ids[:, None] == segment_ids[None, :])
        & alive[None, :]
        & (token[None, :] <= token[:, None])
    )[None, None]
    row_max = jnp.max(jnp.where(allowed, scores, -1e30), axis=-1, keepdims=True)
    weights = jnp.where(allowed, jnp.exp(scores - row_max), 0.0)
    row_sum = jnp.sum(weights, axis=-1, keepdims=True)
    present = alive[None, None, :, None]
    probs = jnp.where(present, weights / jnp.where(present, row_sum, 1.0), 0.0).astype(
        jnp.bfloat16
    )
    attended = jnp.einsum("hgqk,khe->qhge", probs, values, preferred_element_type=jnp.float32)
    attended = attended.astype(jnp.bfloat16).reshape(block_rows, q_heads * HD)

    kv_rows = jnp.concatenate([keys, values], axis=-1).reshape(block_rows, -1)
    slot = jnp.arange(PAGE, dtype=jnp.int32)
    source = starts[:, None] + slot[None, :]
    live_slot = slot[None, :] < own_lens[:, None]
    select = (live_slot[:, :, None] & (source[:, :, None] == token[None, None, :])).astype(
        jnp.bfloat16
    )
    pages = jnp.einsum("jst,tc->jsc", select, kv_rows, preferred_element_type=jnp.float32)
    to_owner = (own_owner[None, :] == jnp.arange(groups_all)[:, None]).astype(jnp.bfloat16)
    kv_send = jnp.einsum(
        "gj,jsc->gsc", to_owner, pages.astype(jnp.bfloat16), preferred_element_type=jnp.float32
    ).astype(jnp.bfloat16)
    hits = (
        page_table[None, :, :] == (me_req * REQS + jnp.arange(REQS, dtype=jnp.int32))[:, None, None]
    )
    page_select = jnp.sum(hits.astype(jnp.int32), axis=2).astype(jnp.bfloat16)

    product = jnp.dot(attended, w_out, preferred_element_type=jnp.float32).astype(jnp.bfloat16)
    n_mp = lax.axis_size("mp")
    product = product.reshape(n_mp // 2, 2, block_rows // n_mp, product.shape[-1])
    g_full, u_full, kv_in, normed = gather_weights(
        w_gate,
        w_up,
        kv_send,
        product,
        residual.reshape(product.shape),
        norm_gain.reshape(1, -1).astype(jnp.float32),
    )
    normed = normed.reshape(block_rows, -1)
    kv_in = kv_in.reshape(groups_all, PAGE, kv_heads, 2 * HD)
    cache_out = jnp.einsum(
        "ls,sphc->lhpc", page_select, kv_in, preferred_element_type=jnp.float32
    ).astype(jnp.bfloat16)
    wg_full = g_full.reshape(-1, w_gate.shape[1])
    wu_full = u_full.reshape(-1, w_up.shape[1])
    gate_acc = jnp.dot(normed, wg_full, preferred_element_type=jnp.float32)
    up_acc = jnp.dot(normed, wu_full, preferred_element_type=jnp.float32)
    hidden = (jax.nn.silu(gate_acc) * up_acc).astype(jnp.bfloat16)
    return (hidden, cache_out)


def solution(mesh):
    in_specs = (
        P("req", "mp"),
        P("req", "mp"),
        P("req", "mp"),
        P("mp"),
        P("mp"),
        P("mp"),
        P("req"),
        P(),
        P(),
        P("mp", None),
        P("req", None),
        P(),
        P("req", "mp"),
        P("req", "mp"),
    )
    out_specs = (P("req", "mp"), P("req", "mp", None, None))
    return jax.shard_map(shards, mesh=mesh, in_specs=in_specs, out_specs=out_specs, check_vma=False)
```

```python
import math

import jax
import jax.numpy as jnp
from jax import lax
from jax.sharding import PartitionSpec as P
from jax.experimental import pallas as pl
from jax.experimental.pallas import tpu as pltpu

HD = 128
PAGE = 128
REQS = 4
RING = 4
KV_SEMS = 40
AR_TILE = 512


THETA = 1000000.0
EPS = 1e-06


def rotate(values, positions):
    half_dim = values.shape[-1] // 2
    frequencies = THETA ** (-jnp.arange(half_dim, dtype=jnp.float32) * (2.0 / values.shape[-1]))
    angles = positions[:, None] * frequencies[None, :]
    cosine = jnp.cos(angles)[:, None, :]
    sine_part = jnp.sin(angles)[:, None, :]
    first_half = values[..., :half_dim]
    second = values[..., half_dim:]
    return jnp.concatenate(
        [first_half * cosine - second * sine_part, second * cosine + first_half * sine_part],
        axis=-1,
    )


def gather_kernel(
    wg_ref, wu_ref, kv_ref, prod_ref, res_ref, gain_ref, g_ref, u_ref, kv_out, sum_ref,
    send_sems, recv_sems, local_sems, ar_send, ar_recv, a_buf, p_buf, b_src, b_buf, m_buf,
    r_buf, gain_buf,
):
    me = lax.axis_index("req")
    col = lax.axis_index("mp")
    z = me // RING
    y = me % RING
    yp = (y + 1) % RING
    ym = (y + RING - 1) % RING
    y2 = (y + 2) % RING
    zp = (z + 1) % RING
    zm = (z + RING - 1) % RING
    z2 = (z + 2) % RING
    rows = wg_ref.shape[0]
    low = pl.ds(0, rows // 2)
    high = pl.ds(rows // 2, rows - rows // 2)
    mesh_id = pl.DeviceIdType.MESH

    def to(zz, yy):
        return (zz * RING + yy, col)

    groups = kv_ref.shape[0]
    xs = prod_ref.shape[0]
    cx = col // 2
    cc = col % 2
    core_peer = (me, cx * 2 + 1 - cc)
    x_peers = [(me, ((cx + d) % xs) * 2 + cc) for d in range(1, xs)]

    barrier = pltpu.get_barrier_semaphore()
    for d in range(1, groups):
        peer = ((me + d) % groups, col)
        pl.semaphore_signal(barrier, inc=1, device_id=peer, device_id_type=mesh_id)
    for peer in [core_peer] + x_peers:
        pl.semaphore_signal(barrier, inc=1, device_id=peer, device_id_type=mesh_id)
    pl.semaphore_wait(barrier, groups - 1 + xs)

    def ar_copy(k, src, dst, peer):
        c = pltpu.make_async_remote_copy(
            src_ref=src,
            dst_ref=dst,
            send_sem=ar_send.at[k],
            recv_sem=ar_recv.at[k],
            device_id=peer,
            device_id_type=mesh_id,
        )
        c.start()
        return c

    ar_a = ar_copy(0, prod_ref.at[:, 1 - cc], a_buf, core_peer)
    p_load = pltpu.make_async_copy(prod_ref.at[:, cc], p_buf, local_sems.at[3])
    p_load.start()
    r_load = pltpu.make_async_copy(res_ref.at[cx, cc], r_buf, local_sems.at[5])
    r_load.start()
    g_load = pltpu.make_async_copy(gain_ref, gain_buf, local_sems.at[6])
    g_load.start()
    width = AR_TILE
    tiles = a_buf.shape[-1] // width

    copies = []

    def send(src, dst, peer):
        k = len(copies)
        c = pltpu.make_async_remote_copy(
            src_ref=src,
            dst_ref=dst,
            send_sem=send_sems.at[k],
            recv_sem=recv_sems.at[k],
            device_id=peer,
            device_id_type=mesh_id,
        )
        c.start()
        copies.append(c)
        return c

    own_g = pltpu.make_async_copy(wg_ref, g_ref.at[z, y], local_sems.at[0])
    own_u = pltpu.make_async_copy(wu_ref, u_ref.at[z, y], local_sems.at[1])
    own_g.start()
    own_u.start()

    g_from_ym = send(wg_ref, g_ref.at[z, y], to(z, yp))
    g_from_yp = send(wg_ref, g_ref.at[z, y], to(z, ym))
    u_from_zm = send(wu_ref, u_ref.at[z, y], to(zp, y))
    u_from_zp = send(wu_ref, u_ref.at[z, y], to(zm, y))
    gz = {"y": (send(wg_ref, g_ref.at[z, y], to(zp, y)), send(wg_ref, g_ref.at[z, y], to(zm, y)))}
    uy = {"z": (send(wu_ref, u_ref.at[z, y], to(z, yp)), send(wu_ref, u_ref.at[z, y], to(z, ym)))}
    kv_copies = []
    own_kv = pltpu.make_async_copy(kv_ref.at[me], kv_out.at[me], local_sems.at[2])
    own_kv.start()
    for d in range(1, groups):
        dest = (me + d) % groups
        c = pltpu.make_async_remote_copy(
            src_ref=kv_ref.at[dest],
            dst_ref=kv_out.at[me],
            send_sem=send_sems.at[KV_SEMS + d - 1],
            recv_sem=recv_sems.at[KV_SEMS + d - 1],
            device_id=(dest, col),
            device_id_type=mesh_id,
        )
        c.start()
        kv_copies.append(c)

    ar_a.wait_recv()
    p_load.wait()

    def add_pair(i, carry):
        xi = i // tiles
        cols = pl.ds(pl.multiple_of((i % tiles) * width, width), width)
        b_src[xi, :, cols] = p_buf[xi, :, cols].astype(jnp.float32) + a_buf[xi, :, cols].astype(
            jnp.float32
        )
        return carry

    lax.fori_loop(0, xs * tiles, add_pair, 0)
    ar_b = [
        ar_copy(d, b_src.at[(cx + d) % xs], b_buf.at[cx], x_peers[d - 1]) for d in range(1, xs)
    ]

    g_from_ym.wait_recv()
    g_far_a = send(g_ref.at[z, ym, low], g_ref.at[z, ym, low], to(z, yp))
    gz["ym"] = (send(g_ref.at[z, ym], g_ref.at[z, ym], to(zp, y)), send(g_ref.at[z, ym], g_ref.at[z, ym], to(zm, y)))
    u_from_zm.wait_recv()
    u_far_a = send(u_ref.at[zm, y, low], u_ref.at[zm, y, low], to(zp, y))
    uy["zm"] = (send(u_ref.at[zm, y], u_ref.at[zm, y], to(z, yp)), send(u_ref.at[zm, y], u_ref.at[zm, y], to(z, ym)))
    g_from_yp.wait_recv()
    g_far_b = send(g_ref.at[z, yp, high], g_ref.at[z, yp, high], to(z, ym))
    gz["yp"] = (send(g_ref.at[z, yp], g_ref.at[z, yp], to(zp, y)), send(g_ref.at[z, yp], g_ref.at[z, yp], to(zm, y)))
    u_from_zp.wait_recv()
    u_far_b = send(u_ref.at[zp, y, high], u_ref.at[zp, y, high], to(zm, y))
    uy["zp"] = (send(u_ref.at[zp, y], u_ref.at[zp, y], to(z, yp)), send(u_ref.at[zp, y], u_ref.at[zp, y], to(z, ym)))

    g_far_a.wait_recv()
    g_far_b.wait_recv()
    gz["y2"] = (send(g_ref.at[z, y2], g_ref.at[z, y2], to(zp, y)), send(g_ref.at[z, y2], g_ref.at[z, y2], to(zm, y)))
    u_far_a.wait_recv()
    u_far_b.wait_recv()
    uy["z2"] = (send(u_ref.at[z2, y], u_ref.at[z2, y], to(z, yp)), send(u_ref.at[z2, y], u_ref.at[z2, y], to(z, ym)))

    for c in ar_b:
        c.wait_recv()

    r_load.wait()
    g_load.wait()

    def add_chips(t, squares):
        cols = pl.ds(pl.multiple_of(t * width, width), width)
        acc = b_src[cx, :, cols]
        for d in range(1, xs):
            acc = acc + b_buf[(cx + d) % xs, :, cols]
        state = acc + r_buf[:, cols].astype(jnp.float32)
        b_src[cx, :, cols] = state
        return squares + jnp.sum(state * state, axis=1, keepdims=True)

    squares = lax.fori_loop(0, tiles, add_chips, jnp.zeros((m_buf.shape[0], 1), jnp.float32))
    scale = lax.rsqrt(squares / m_buf.shape[1] + EPS)

    def scale_rows(t, carry):
        cols = pl.ds(pl.multiple_of(t * width, width), width)
        normed = b_src[cx, :, cols] * scale * gain_buf[:, cols]
        m_buf[:, cols] = normed.astype(m_buf.dtype)
        return carry

    lax.fori_loop(0, tiles, scale_rows, 0)
    own_sum = pltpu.make_async_copy(m_buf, sum_ref.at[cx, cc], local_sems.at[4])
    own_sum.start()
    own_sum.wait()
    ar_c = [
        ar_copy(xs - 1 + d, sum_ref.at[cx, cc], sum_ref.at[cx, cc], x_peers[d - 1])
        for d in range(1, xs)
    ]

    for (gkey, yy), (ukey, zz) in zip(
        (("y", y), ("ym", ym), ("yp", yp), ("y2", y2)),
        (("z", z), ("zm", zm), ("zp", zp), ("z2", z2)),
    ):
        from_zm, from_zp = gz[gkey]
        from_ym, from_yp = uy[ukey]
        from_zm.wait_recv()
        send(g_ref.at[zm, yy, low], g_ref.at[zm, yy, low], to(zp, y))
        from_ym.wait_recv()
        send(u_ref.at[zz, ym, low], u_ref.at[zz, ym, low], to(z, yp))
        from_zp.wait_recv()
        send(g_ref.at[zp, yy, high], g_ref.at[zp, yy, high], to(zm, y))
        from_yp.wait_recv()
        send(u_ref.at[zz, yp, high], u_ref.at[zz, yp, high], to(z, ym))

    for c in ar_c:
        c.wait_recv()
    ar_d = ar_copy(2 * xs - 1, sum_ref.at[:, cc], sum_ref.at[:, cc], core_peer)
    ar_d.wait_recv()
    for c in [ar_a] + ar_b + ar_c + [ar_d]:
        c.wait_send()

    waited = [g_from_ym, g_from_yp, u_from_zm, u_from_zp, g_far_a, g_far_b, u_far_a, u_far_b]
    waited += list(gz["y"]) + list(gz["ym"]) + list(gz["yp"]) + list(gz["y2"])
    waited += list(uy["z"]) + list(uy["zm"]) + list(uy["zp"]) + list(uy["z2"])
    for c in copies:
        if not any(c is w for w in waited):
            c.wait_recv()
    for c in copies:
        c.wait_send()
    for c in kv_copies:
        c.wait_recv()
        c.wait_send()
    own_g.wait()
    own_u.wait()
    own_kv.wait()


def gather_weights(w_gate, w_up, kv_send, product, residual, gain):
    rows, cols = w_gate.shape
    xs, _, chunk, width = product.shape
    any_spec = pl.BlockSpec(memory_space=pl.ANY)
    piece = jax.ShapeDtypeStruct((RING, RING, rows, cols), w_gate.dtype)
    slots = jax.ShapeDtypeStruct(kv_send.shape, kv_send.dtype)
    sums = jax.ShapeDtypeStruct(product.shape, product.dtype)
    sems = KV_SEMS + kv_send.shape[0] - 1
    return pl.pallas_call(
        gather_kernel,
        out_shape=(piece, piece, slots, sums),
        in_specs=[any_spec] * 6,
        out_specs=(any_spec, any_spec, any_spec, any_spec),
        scratch_shapes=[
            pltpu.SemaphoreType.DMA((sems,)),
            pltpu.SemaphoreType.DMA((sems,)),
            pltpu.SemaphoreType.DMA((7,)),
            pltpu.SemaphoreType.DMA((2 * xs,)),
            pltpu.SemaphoreType.DMA((2 * xs,)),
            pltpu.VMEM((xs, chunk, width), product.dtype),
            pltpu.VMEM((xs, chunk, width), product.dtype),
            pltpu.VMEM((xs, chunk, width), jnp.float32),
            pltpu.VMEM((xs, chunk, width), jnp.float32),
            pltpu.VMEM((chunk, width), product.dtype),
            pltpu.VMEM((chunk, width), residual.dtype),
            pltpu.VMEM((1, width), jnp.float32),
        ],
        compiler_params=pltpu.CompilerParams(
            collective_id=0, has_side_effects=True, vmem_limit_bytes=48 * 1024 * 1024
        ),
    )(w_gate, w_up, kv_send, product, residual, gain)

def normalize(resid_rows, summed, gain_row):
    state = resid_rows.astype(jnp.float32) + summed
    scale_row = lax.rsqrt(jnp.mean(state * state, axis=-1, keepdims=True) + EPS)
    return (state * scale_row * gain_row).astype(jnp.bfloat16)


def shards(
    q_pre,
    k_pre,
    v_pre,
    q_bias,
    k_bias,
    v_bias,
    segment_ids,
    lengths,
    page_table,
    w_out,
    residual,
    norm_gain,
    w_gate,
    w_up,
):
    me_req = lax.axis_index("req")
    groups_all = lax.axis_size("req")
    block_rows = q_pre.shape[0]
    kv_heads = k_pre.shape[1] // HD
    q_heads = q_pre.shape[1] // HD
    group_size = q_heads // kv_heads


    own_lens = lax.dynamic_index_in_dim(lengths, me_req, 0, keepdims=False)
    own_pages = lax.dynamic_index_in_dim(page_table, me_req, 0, keepdims=False)
    own_owner = own_pages // REQS
    starts = jnp.cumsum(own_lens) - own_lens

    alive = segment_ids >= 0
    req_idx = jnp.clip(segment_ids - me_req * REQS, 0, REQS - 1)
    req_hit = req_idx[:, None] == jnp.arange(REQS)[None, :]
    row_start = jnp.sum(jnp.where(req_hit, starts[None, :], 0), axis=1)
    token = jnp.arange(block_rows, dtype=jnp.int32)
    positions = (token - row_start).astype(jnp.float32)
    keep = alive[:, None, None]

    queries = rotate(
        (q_pre.astype(jnp.float32) + q_bias).reshape(block_rows, q_heads, HD), positions
    )
    queries = jnp.where(keep, queries, 0.0).astype(jnp.bfloat16)
    keys = rotate((k_pre.astype(jnp.float32) + k_bias).reshape(block_rows, kv_heads, HD), positions)
    keys = jnp.where(keep, keys, 0.0).astype(jnp.bfloat16)
    values = (v_pre.astype(jnp.float32) + v_bias).reshape(block_rows, kv_heads, HD)
    values = jnp.where(keep, values, 0.0).astype(jnp.bfloat16)

    scale_factor = 1.0 / math.sqrt(HD)
    q_groups = queries.reshape(block_rows, kv_heads, group_size, HD)
    scores = (
        jnp.einsum("qhge,khe->hgqk", q_groups, keys, preferred_element_type=jnp.float32)
        * scale_factor
    )
    allowed = (
        (segment_ids[:, None] == segment_ids[None, :])
        & alive[None, :]
        & (token[None, :] <= token[:, None])
    )[None, None]
    row_max = jnp.max(jnp.where(allowed, scores, -1e30), axis=-1, keepdims=True)
    weights = jnp.where(allowed, jnp.exp(scores - row_max), 0.0)
    row_sum = jnp.sum(weights, axis=-1, keepdims=True)
    present = alive[None, None, :, None]
    probs = jnp.where(present, weights / jnp.where(present, row_sum, 1.0), 0.0).astype(
        jnp.bfloat16
    )
    attended = jnp.einsum("hgqk,khe->qhge", probs, values, preferred_element_type=jnp.float32)
    attended = attended.astype(jnp.bfloat16).reshape(block_rows, q_heads * HD)

    kv_rows = jnp.concatenate([keys, values], axis=-1).reshape(block_rows, -1)
    slot = jnp.arange(PAGE, dtype=jnp.int32)
    source = starts[:, None] + slot[None, :]
    live_slot = slot[None, :] < own_lens[:, None]
    select = (live_slot[:, :, None] & (source[:, :, None] == token[None, None, :])).astype(
        jnp.bfloat16
    )
    pages = jnp.einsum("jst,tc->jsc", select, kv_rows, preferred_element_type=jnp.float32)
    to_owner = (own_owner[None, :] == jnp.arange(groups_all)[:, None]).astype(jnp.bfloat16)
    kv_send = jnp.einsum(
        "gj,jsc->gsc", to_owner, pages.astype(jnp.bfloat16), preferred_element_type=jnp.float32
    ).astype(jnp.bfloat16)
    hits = (
        page_table[None, :, :] == (me_req * REQS + jnp.arange(REQS, dtype=jnp.int32))[:, None, None]
    )
    page_select = jnp.sum(hits.astype(jnp.int32), axis=2).astype(jnp.bfloat16)

    product = jnp.dot(attended, w_out, preferred_element_type=jnp.float32).astype(jnp.bfloat16)
    n_mp = lax.axis_size("mp")
    product = product.reshape(n_mp // 2, 2, block_rows // n_mp, product.shape[-1])
    g_full, u_full, kv_in, normed = gather_weights(
        w_gate,
        w_up,
        kv_send,
        product,
        residual.reshape(product.shape),
        norm_gain.reshape(1, -1).astype(jnp.float32),
    )
    normed = normed.reshape(block_rows, -1)
    kv_in = kv_in.reshape(groups_all, PAGE, kv_heads, 2 * HD)
    cache_out = jnp.einsum(
        "ls,sphc->lhpc", page_select, kv_in, preferred_element_type=jnp.float32
    ).astype(jnp.bfloat16)
    wg_full = g_full.reshape(-1, w_gate.shape[1])
    wu_full = u_full.reshape(-1, w_up.shape[1])
    gate_acc = jnp.dot(normed, wg_full, preferred_element_type=jnp.float32)
    up_acc = jnp.dot(normed, wu_full, preferred_element_type=jnp.float32)
    hidden = (jax.nn.silu(gate_acc) * up_acc).astype(jnp.bfloat16)
    return (hidden, cache_out)


def solution(mesh):
    in_specs = (
        P("req", "mp"),
        P("req", "mp"),
        P("req", "mp"),
        P("mp"),
        P("mp"),
        P("mp"),
        P("req"),
        P(),
        P(),
        P("mp", None),
        P("req", None),
        P(),
        P("req", "mp"),
        P("req", "mp"),
    )
    out_specs = (P("req", "mp"), P("req", "mp", None, None))
    return jax.shard_map(shards, mesh=mesh, in_specs=in_specs, out_specs=out_specs, check_vma=False)
```

```python
import math

import jax
import jax.numpy as jnp
from jax import lax
from jax.sharding import PartitionSpec as P
from jax.experimental import pallas as pl
from jax.experimental.pallas import tpu as pltpu

HD = 128
PAGE = 128
REQS = 4
RING = 4
KV_SEMS = 40
AR_TILE = 512


THETA = 1000000.0
EPS = 1e-06


def rotate(values, positions):
    half_dim = values.shape[-1] // 2
    frequencies = THETA ** (-jnp.arange(half_dim, dtype=jnp.float32) * (2.0 / values.shape[-1]))
    angles = positions[:, None] * frequencies[None, :]
    cosine = jnp.cos(angles)[:, None, :]
    sine_part = jnp.sin(angles)[:, None, :]
    first_half = values[..., :half_dim]
    second = values[..., half_dim:]
    return jnp.concatenate(
        [first_half * cosine - second * sine_part, second * cosine + first_half * sine_part],
        axis=-1,
    )


def gather_kernel(
    wg_ref, wu_ref, kv_ref, att_ref, wout_ref, res_ref, gain_ref, g_ref, u_ref, kv_out, sum_ref,
    send_sems, recv_sems, local_sems, ar_send, ar_recv, a_buf, prod_v, b_src, b_buf, m_buf,
    r_buf, gain_buf,
):
    me = lax.axis_index("req")
    col = lax.axis_index("mp")
    z = me // RING
    y = me % RING
    yp = (y + 1) % RING
    ym = (y + RING - 1) % RING
    y2 = (y + 2) % RING
    zp = (z + 1) % RING
    zm = (z + RING - 1) % RING
    z2 = (z + 2) % RING
    rows = wg_ref.shape[0]
    low = pl.ds(0, rows // 2)
    high = pl.ds(rows // 2, rows - rows // 2)
    mesh_id = pl.DeviceIdType.MESH

    def to(zz, yy):
        return (zz * RING + yy, col)

    groups = kv_ref.shape[0]
    xs = prod_v.shape[0]
    cx = col // 2
    cc = col % 2
    core_peer = (me, cx * 2 + 1 - cc)
    x_peers = [(me, ((cx + d) % xs) * 2 + cc) for d in range(1, xs)]

    barrier = pltpu.get_barrier_semaphore()
    for d in range(1, groups):
        peer = ((me + d) % groups, col)
        pl.semaphore_signal(barrier, inc=1, device_id=peer, device_id_type=mesh_id)
    for peer in [core_peer] + x_peers:
        pl.semaphore_signal(barrier, inc=1, device_id=peer, device_id_type=mesh_id)
    pl.semaphore_wait(barrier, groups - 1 + xs)

    def ar_copy(k, src, dst, peer):
        c = pltpu.make_async_remote_copy(
            src_ref=src,
            dst_ref=dst,
            send_sem=ar_send.at[k],
            recv_sem=ar_recv.at[k],
            device_id=peer,
            device_id_type=mesh_id,
        )
        c.start()
        return c

    r_load = pltpu.make_async_copy(res_ref.at[cx, cc], r_buf, local_sems.at[5])
    r_load.start()
    g_load = pltpu.make_async_copy(gain_ref, gain_buf, local_sems.at[6])
    g_load.start()
    width = AR_TILE
    tiles = a_buf.shape[-1] // width

    copies = []

    def send(src, dst, peer):
        k = len(copies)
        c = pltpu.make_async_remote_copy(
            src_ref=src,
            dst_ref=dst,
            send_sem=send_sems.at[k],
            recv_sem=recv_sems.at[k],
            device_id=peer,
            device_id_type=mesh_id,
        )
        c.start()
        copies.append(c)
        return c

    own_g = pltpu.make_async_copy(wg_ref, g_ref.at[z, y], local_sems.at[0])
    own_u = pltpu.make_async_copy(wu_ref, u_ref.at[z, y], local_sems.at[1])
    own_g.start()
    own_u.start()

    g_from_ym = send(wg_ref, g_ref.at[z, y], to(z, yp))
    g_from_yp = send(wg_ref, g_ref.at[z, y], to(z, ym))
    u_from_zm = send(wu_ref, u_ref.at[z, y], to(zp, y))
    u_from_zp = send(wu_ref, u_ref.at[z, y], to(zm, y))
    gz = {"y": (send(wg_ref, g_ref.at[z, y], to(zp, y)), send(wg_ref, g_ref.at[z, y], to(zm, y)))}
    uy = {"z": (send(wu_ref, u_ref.at[z, y], to(z, yp)), send(wu_ref, u_ref.at[z, y], to(z, ym)))}
    kv_copies = []
    own_kv = pltpu.make_async_copy(kv_ref.at[me], kv_out.at[me], local_sems.at[2])
    own_kv.start()
    for d in range(1, groups):
        dest = (me + d) % groups
        c = pltpu.make_async_remote_copy(
            src_ref=kv_ref.at[dest],
            dst_ref=kv_out.at[me],
            send_sem=send_sems.at[KV_SEMS + d - 1],
            recv_sem=recv_sems.at[KV_SEMS + d - 1],
            device_id=(dest, col),
            device_id_type=mesh_id,
        )
        c.start()
        kv_copies.append(c)

    chunk = prod_v.shape[2]

    def project(k, carry):
        rows = att_ref[pl.ds(pl.multiple_of(k * chunk, chunk), chunk), :]
        part = jnp.dot(rows, wout_ref[...], preferred_element_type=jnp.float32)
        prod_v[k // 2, k % 2] = part.astype(prod_v.dtype)
        return carry

    lax.fori_loop(0, 2 * xs, project, 0)
    ar_a = ar_copy(0, prod_v.at[:, 1 - cc], a_buf, core_peer)

    ar_a.wait_recv()

    def add_pair(i, carry):
        xi = i // tiles
        cols = pl.ds(pl.multiple_of((i % tiles) * width, width), width)
        b_src[xi, :, cols] = prod_v[xi, cc, :, cols].astype(jnp.float32) + a_buf[xi, :, cols].astype(
            jnp.float32
        )
        return carry

    lax.fori_loop(0, xs * tiles, add_pair, 0)
    ar_b = [
        ar_copy(d, b_src.at[(cx + d) % xs], b_buf.at[cx], x_peers[d - 1]) for d in range(1, xs)
    ]

    g_from_ym.wait_recv()
    g_far_a = send(g_ref.at[z, ym, low], g_ref.at[z, ym, low], to(z, yp))
    gz["ym"] = (send(g_ref.at[z, ym], g_ref.at[z, ym], to(zp, y)), send(g_ref.at[z, ym], g_ref.at[z, ym], to(zm, y)))
    u_from_zm.wait_recv()
    u_far_a = send(u_ref.at[zm, y, low], u_ref.at[zm, y, low], to(zp, y))
    uy["zm"] = (send(u_ref.at[zm, y], u_ref.at[zm, y], to(z, yp)), send(u_ref.at[zm, y], u_ref.at[zm, y], to(z, ym)))
    g_from_yp.wait_recv()
    g_far_b = send(g_ref.at[z, yp, high], g_ref.at[z, yp, high], to(z, ym))
    gz["yp"] = (send(g_ref.at[z, yp], g_ref.at[z, yp], to(zp, y)), send(g_ref.at[z, yp], g_ref.at[z, yp], to(zm, y)))
    u_from_zp.wait_recv()
    u_far_b = send(u_ref.at[zp, y, high], u_ref.at[zp, y, high], to(zm, y))
    uy["zp"] = (send(u_ref.at[zp, y], u_ref.at[zp, y], to(z, yp)), send(u_ref.at[zp, y], u_ref.at[zp, y], to(z, ym)))

    g_far_a.wait_recv()
    g_far_b.wait_recv()
    gz["y2"] = (send(g_ref.at[z, y2], g_ref.at[z, y2], to(zp, y)), send(g_ref.at[z, y2], g_ref.at[z, y2], to(zm, y)))
    u_far_a.wait_recv()
    u_far_b.wait_recv()
    uy["z2"] = (send(u_ref.at[z2, y], u_ref.at[z2, y], to(z, yp)), send(u_ref.at[z2, y], u_ref.at[z2, y], to(z, ym)))

    for c in ar_b:
        c.wait_recv()

    r_load.wait()
    g_load.wait()

    def add_chips(t, squares):
        cols = pl.ds(pl.multiple_of(t * width, width), width)
        acc = b_src[cx, :, cols]
        for d in range(1, xs):
            acc = acc + b_buf[(cx + d) % xs, :, cols]
        state = acc + r_buf[:, cols].astype(jnp.float32)
        b_src[cx, :, cols] = state
        return squares + jnp.sum(state * state, axis=1, keepdims=True)

    squares = lax.fori_loop(0, tiles, add_chips, jnp.zeros((m_buf.shape[0], 1), jnp.float32))
    scale = lax.rsqrt(squares / m_buf.shape[1] + EPS)

    def scale_rows(t, carry):
        cols = pl.ds(pl.multiple_of(t * width, width), width)
        normed = b_src[cx, :, cols] * scale * gain_buf[:, cols]
        m_buf[:, cols] = normed.astype(m_buf.dtype)
        return carry

    lax.fori_loop(0, tiles, scale_rows, 0)
    own_sum = pltpu.make_async_copy(m_buf, sum_ref.at[cx, cc], local_sems.at[4])
    own_sum.start()
    own_sum.wait()
    ar_c = [
        ar_copy(xs - 1 + d, sum_ref.at[cx, cc], sum_ref.at[cx, cc], x_peers[d - 1])
        for d in range(1, xs)
    ]

    for (gkey, yy), (ukey, zz) in zip(
        (("y", y), ("ym", ym), ("yp", yp), ("y2", y2)),
        (("z", z), ("zm", zm), ("zp", zp), ("z2", z2)),
    ):
        from_zm, from_zp = gz[gkey]
        from_ym, from_yp = uy[ukey]
        from_zm.wait_recv()
        send(g_ref.at[zm, yy, low], g_ref.at[zm, yy, low], to(zp, y))
        from_ym.wait_recv()
        send(u_ref.at[zz, ym, low], u_ref.at[zz, ym, low], to(z, yp))
        from_zp.wait_recv()
        send(g_ref.at[zp, yy, high], g_ref.at[zp, yy, high], to(zm, y))
        from_yp.wait_recv()
        send(u_ref.at[zz, yp, high], u_ref.at[zz, yp, high], to(z, ym))

    for c in ar_c:
        c.wait_recv()
    ar_d = ar_copy(2 * xs - 1, sum_ref.at[:, cc], sum_ref.at[:, cc], core_peer)
    ar_d.wait_recv()
    for c in [ar_a] + ar_b + ar_c + [ar_d]:
        c.wait_send()

    waited = [g_from_ym, g_from_yp, u_from_zm, u_from_zp, g_far_a, g_far_b, u_far_a, u_far_b]
    waited += list(gz["y"]) + list(gz["ym"]) + list(gz["yp"]) + list(gz["y2"])
    waited += list(uy["z"]) + list(uy["zm"]) + list(uy["zp"]) + list(uy["z2"])
    for c in copies:
        if not any(c is w for w in waited):
            c.wait_recv()
    for c in copies:
        c.wait_send()
    for c in kv_copies:
        c.wait_recv()
        c.wait_send()
    own_g.wait()
    own_u.wait()
    own_kv.wait()


def gather_weights(w_gate, w_up, kv_send, attended, w_out, residual, gain):
    rows, cols = w_gate.shape
    xs, _, chunk, width = residual.shape
    product = jax.ShapeDtypeStruct(residual.shape, jnp.bfloat16)
    any_spec = pl.BlockSpec(memory_space=pl.ANY)
    vmem_spec = pl.BlockSpec(memory_space=pltpu.VMEM)
    piece = jax.ShapeDtypeStruct((RING, RING, rows, cols), w_gate.dtype)
    slots = jax.ShapeDtypeStruct(kv_send.shape, kv_send.dtype)
    sums = jax.ShapeDtypeStruct(product.shape, product.dtype)
    sems = KV_SEMS + kv_send.shape[0] - 1
    return pl.pallas_call(
        gather_kernel,
        out_shape=(piece, piece, slots, sums),
        in_specs=[any_spec] * 3 + [vmem_spec] * 2 + [any_spec] * 2,
        out_specs=(any_spec, any_spec, any_spec, any_spec),
        scratch_shapes=[
            pltpu.SemaphoreType.DMA((sems,)),
            pltpu.SemaphoreType.DMA((sems,)),
            pltpu.SemaphoreType.DMA((7,)),
            pltpu.SemaphoreType.DMA((2 * xs,)),
            pltpu.SemaphoreType.DMA((2 * xs,)),
            pltpu.VMEM((xs, chunk, width), product.dtype),
            pltpu.VMEM(product.shape, product.dtype),
            pltpu.VMEM((xs, chunk, width), jnp.float32),
            pltpu.VMEM((xs, chunk, width), jnp.float32),
            pltpu.VMEM((chunk, width), product.dtype),
            pltpu.VMEM((chunk, width), residual.dtype),
            pltpu.VMEM((1, width), jnp.float32),
        ],
        compiler_params=pltpu.CompilerParams(
            collective_id=0, has_side_effects=True, vmem_limit_bytes=48 * 1024 * 1024
        ),
    )(w_gate, w_up, kv_send, attended, w_out, residual, gain)

def normalize(resid_rows, summed, gain_row):
    state = resid_rows.astype(jnp.float32) + summed
    scale_row = lax.rsqrt(jnp.mean(state * state, axis=-1, keepdims=True) + EPS)
    return (state * scale_row * gain_row).astype(jnp.bfloat16)


def shards(
    q_pre,
    k_pre,
    v_pre,
    q_bias,
    k_bias,
    v_bias,
    segment_ids,
    lengths,
    page_table,
    w_out,
    residual,
    norm_gain,
    w_gate,
    w_up,
):
    me_req = lax.axis_index("req")
    groups_all = lax.axis_size("req")
    block_rows = q_pre.shape[0]
    kv_heads = k_pre.shape[1] // HD
    q_heads = q_pre.shape[1] // HD
    group_size = q_heads // kv_heads


    own_lens = lax.dynamic_index_in_dim(lengths, me_req, 0, keepdims=False)
    own_pages = lax.dynamic_index_in_dim(page_table, me_req, 0, keepdims=False)
    own_owner = own_pages // REQS
    starts = jnp.cumsum(own_lens) - own_lens

    alive = segment_ids >= 0
    req_idx = jnp.clip(segment_ids - me_req * REQS, 0, REQS - 1)
    req_hit = req_idx[:, None] == jnp.arange(REQS)[None, :]
    row_start = jnp.sum(jnp.where(req_hit, starts[None, :], 0), axis=1)
    token = jnp.arange(block_rows, dtype=jnp.int32)
    positions = (token - row_start).astype(jnp.float32)
    keep = alive[:, None, None]

    queries = rotate(
        (q_pre.astype(jnp.float32) + q_bias).reshape(block_rows, q_heads, HD), positions
    )
    queries = jnp.where(keep, queries, 0.0).astype(jnp.bfloat16)
    keys = rotate((k_pre.astype(jnp.float32) + k_bias).reshape(block_rows, kv_heads, HD), positions)
    keys = jnp.where(keep, keys, 0.0).astype(jnp.bfloat16)
    values = (v_pre.astype(jnp.float32) + v_bias).reshape(block_rows, kv_heads, HD)
    values = jnp.where(keep, values, 0.0).astype(jnp.bfloat16)

    scale_factor = 1.0 / math.sqrt(HD)
    q_groups = queries.reshape(block_rows, kv_heads, group_size, HD)
    scores = (
        jnp.einsum("qhge,khe->hgqk", q_groups, keys, preferred_element_type=jnp.float32)
        * scale_factor
    )
    allowed = (
        (segment_ids[:, None] == segment_ids[None, :])
        & alive[None, :]
        & (token[None, :] <= token[:, None])
    )[None, None]
    row_max = jnp.max(jnp.where(allowed, scores, -1e30), axis=-1, keepdims=True)
    weights = jnp.where(allowed, jnp.exp(scores - row_max), 0.0)
    row_sum = jnp.sum(weights, axis=-1, keepdims=True)
    present = alive[None, None, :, None]
    probs = jnp.where(present, weights / jnp.where(present, row_sum, 1.0), 0.0).astype(
        jnp.bfloat16
    )
    attended = jnp.einsum("hgqk,khe->qhge", probs, values, preferred_element_type=jnp.float32)
    attended = attended.astype(jnp.bfloat16).reshape(block_rows, q_heads * HD)

    kv_rows = jnp.concatenate([keys, values], axis=-1).reshape(block_rows, -1)
    slot = jnp.arange(PAGE, dtype=jnp.int32)
    source = starts[:, None] + slot[None, :]
    live_slot = slot[None, :] < own_lens[:, None]
    select = (live_slot[:, :, None] & (source[:, :, None] == token[None, None, :])).astype(
        jnp.bfloat16
    )
    pages = jnp.einsum("jst,tc->jsc", select, kv_rows, preferred_element_type=jnp.float32)
    to_owner = (own_owner[None, :] == jnp.arange(groups_all)[:, None]).astype(jnp.bfloat16)
    kv_send = jnp.einsum(
        "gj,jsc->gsc", to_owner, pages.astype(jnp.bfloat16), preferred_element_type=jnp.float32
    ).astype(jnp.bfloat16)
    hits = (
        page_table[None, :, :] == (me_req * REQS + jnp.arange(REQS, dtype=jnp.int32))[:, None, None]
    )
    page_select = jnp.sum(hits.astype(jnp.int32), axis=2).astype(jnp.bfloat16)

    n_mp = lax.axis_size("mp")
    split_rows = (n_mp // 2, 2, block_rows // n_mp, residual.shape[-1])
    g_full, u_full, kv_in, normed = gather_weights(
        w_gate,
        w_up,
        kv_send,
        attended,
        w_out,
        residual.reshape(split_rows),
        norm_gain.reshape(1, -1).astype(jnp.float32),
    )
    normed = normed.reshape(block_rows, -1)
    kv_in = kv_in.reshape(groups_all, PAGE, kv_heads, 2 * HD)
    cache_out = jnp.einsum(
        "ls,sphc->lhpc", page_select, kv_in, preferred_element_type=jnp.float32
    ).astype(jnp.bfloat16)
    wg_full = g_full.reshape(-1, w_gate.shape[1])
    wu_full = u_full.reshape(-1, w_up.shape[1])
    gate_acc = jnp.dot(normed, wg_full, preferred_element_type=jnp.float32)
    up_acc = jnp.dot(normed, wu_full, preferred_element_type=jnp.float32)
    hidden = (jax.nn.silu(gate_acc) * up_acc).astype(jnp.bfloat16)
    return (hidden, cache_out)


def solution(mesh):
    in_specs = (
        P("req", "mp"),
        P("req", "mp"),
        P("req", "mp"),
        P("mp"),
        P("mp"),
        P("mp"),
        P("req"),
        P(),
        P(),
        P("mp", None),
        P("req", None),
        P(),
        P("req", "mp"),
        P("req", "mp"),
    )
    out_specs = (P("req", "mp"), P("req", "mp", None, None))
    return jax.shard_map(shards, mesh=mesh, in_specs=in_specs, out_specs=out_specs, check_vma=False)
```

```python
import math

import jax
import jax.numpy as jnp
from jax import lax
from jax.sharding import PartitionSpec as P
from jax.experimental import pallas as pl
from jax.experimental.pallas import tpu as pltpu

HD = 128
PAGE = 128
REQS = 4
RING = 4
KV_SEMS = 40
AR_TILE = 512


THETA = 1000000.0
EPS = 1e-06


def rotate(values, positions):
    half_dim = values.shape[-1] // 2
    frequencies = THETA ** (-jnp.arange(half_dim, dtype=jnp.float32) * (2.0 / values.shape[-1]))
    angles = positions[:, None] * frequencies[None, :]
    cosine = jnp.cos(angles)[:, None, :]
    sine_part = jnp.sin(angles)[:, None, :]
    first_half = values[..., :half_dim]
    second = values[..., half_dim:]
    return jnp.concatenate(
        [first_half * cosine - second * sine_part, second * cosine + first_half * sine_part],
        axis=-1,
    )


def gather_kernel(
    wg_ref, wu_ref, kv_ref, att_ref, wout_ref, res_ref, gain_ref, g_ref, u_ref, kv_out, sum_ref,
    send_sems, recv_sems, local_sems, ar_send, ar_recv, a_buf, prod_v, b_src, b_buf, m_buf,
    r_buf, gain_buf, s_buf,
):
    me = lax.axis_index("req")
    col = lax.axis_index("mp")
    z = me // RING
    y = me % RING
    yp = (y + 1) % RING
    ym = (y + RING - 1) % RING
    y2 = (y + 2) % RING
    zp = (z + 1) % RING
    zm = (z + RING - 1) % RING
    z2 = (z + 2) % RING
    rows = wg_ref.shape[0]
    low = pl.ds(0, rows // 2)
    high = pl.ds(rows // 2, rows - rows // 2)
    mesh_id = pl.DeviceIdType.MESH

    def to(zz, yy):
        return (zz * RING + yy, col)

    groups = kv_ref.shape[0]
    xs = prod_v.shape[0]
    cx = col // 2
    cc = col % 2
    core_peer = (me, cx * 2 + 1 - cc)
    x_peers = [(me, ((cx + d) % xs) * 2 + cc) for d in range(1, xs)]

    barrier = pltpu.get_barrier_semaphore()
    for d in range(1, groups):
        peer = ((me + d) % groups, col)
        pl.semaphore_signal(barrier, inc=1, device_id=peer, device_id_type=mesh_id)
    for peer in [core_peer] + x_peers:
        pl.semaphore_signal(barrier, inc=1, device_id=peer, device_id_type=mesh_id)
    pl.semaphore_wait(barrier, groups - 1 + xs)

    def ar_copy(k, src, dst, peer):
        c = pltpu.make_async_remote_copy(
            src_ref=src,
            dst_ref=dst,
            send_sem=ar_send.at[k],
            recv_sem=ar_recv.at[k],
            device_id=peer,
            device_id_type=mesh_id,
        )
        c.start()
        return c

    r_load = pltpu.make_async_copy(res_ref.at[cx, cc], r_buf, local_sems.at[5])
    r_load.start()
    g_load = pltpu.make_async_copy(gain_ref, gain_buf, local_sems.at[6])
    g_load.start()
    width = AR_TILE
    tiles = a_buf.shape[-1] // width

    copies = []

    def send(src, dst, peer):
        k = len(copies)
        c = pltpu.make_async_remote_copy(
            src_ref=src,
            dst_ref=dst,
            send_sem=send_sems.at[k],
            recv_sem=recv_sems.at[k],
            device_id=peer,
            device_id_type=mesh_id,
        )
        c.start()
        copies.append(c)
        return c

    own_g = pltpu.make_async_copy(wg_ref, g_ref.at[z, y], local_sems.at[0])
    own_u = pltpu.make_async_copy(wu_ref, u_ref.at[z, y], local_sems.at[1])
    own_g.start()
    own_u.start()

    g_from_ym = send(wg_ref, g_ref.at[z, y], to(z, yp))
    g_from_yp = send(wg_ref, g_ref.at[z, y], to(z, ym))
    u_from_zm = send(wu_ref, u_ref.at[z, y], to(zp, y))
    u_from_zp = send(wu_ref, u_ref.at[z, y], to(zm, y))
    gz = {"y": (send(wg_ref, g_ref.at[z, y], to(zp, y)), send(wg_ref, g_ref.at[z, y], to(zm, y)))}
    uy = {"z": (send(wu_ref, u_ref.at[z, y], to(z, yp)), send(wu_ref, u_ref.at[z, y], to(z, ym)))}
    kv_copies = []
    own_kv = pltpu.make_async_copy(kv_ref.at[me], kv_out.at[me], local_sems.at[2])
    own_kv.start()
    for d in range(1, groups):
        dest = (me + d) % groups
        c = pltpu.make_async_remote_copy(
            src_ref=kv_ref.at[dest],
            dst_ref=kv_out.at[me],
            send_sem=send_sems.at[KV_SEMS + d - 1],
            recv_sem=recv_sems.at[KV_SEMS + d - 1],
            device_id=(dest, col),
            device_id_type=mesh_id,
        )
        c.start()
        kv_copies.append(c)

    chunk = prod_v.shape[2]

    def project(k, carry):
        rows = att_ref[pl.ds(pl.multiple_of(k * chunk, chunk), chunk), :]
        part = jnp.dot(rows, wout_ref[...], preferred_element_type=jnp.float32)
        prod_v[k // 2, k % 2] = part.astype(prod_v.dtype)
        return carry

    lax.fori_loop(0, 2 * xs, project, 0)
    ar_a = ar_copy(0, prod_v.at[:, 1 - cc], a_buf, core_peer)

    ar_a.wait_recv()

    def add_pair(i, carry):
        xi = i // tiles
        cols = pl.ds(pl.multiple_of((i % tiles) * width, width), width)
        pair = prod_v[xi, cc, :, cols].astype(jnp.float32) + a_buf[xi, :, cols].astype(jnp.float32)
        b_src[xi, :, cols] = pair.astype(b_src.dtype)
        return carry

    lax.fori_loop(0, xs * tiles, add_pair, 0)
    ar_b = [
        ar_copy(d, b_src.at[(cx + d) % xs], b_buf.at[cx], x_peers[d - 1]) for d in range(1, xs)
    ]

    g_from_ym.wait_recv()
    g_far_a = send(g_ref.at[z, ym, low], g_ref.at[z, ym, low], to(z, yp))
    gz["ym"] = (send(g_ref.at[z, ym], g_ref.at[z, ym], to(zp, y)), send(g_ref.at[z, ym], g_ref.at[z, ym], to(zm, y)))
    u_from_zm.wait_recv()
    u_far_a = send(u_ref.at[zm, y, low], u_ref.at[zm, y, low], to(zp, y))
    uy["zm"] = (send(u_ref.at[zm, y], u_ref.at[zm, y], to(z, yp)), send(u_ref.at[zm, y], u_ref.at[zm, y], to(z, ym)))
    g_from_yp.wait_recv()
    g_far_b = send(g_ref.at[z, yp, high], g_ref.at[z, yp, high], to(z, ym))
    gz["yp"] = (send(g_ref.at[z, yp], g_ref.at[z, yp], to(zp, y)), send(g_ref.at[z, yp], g_ref.at[z, yp], to(zm, y)))
    u_from_zp.wait_recv()
    u_far_b = send(u_ref.at[zp, y, high], u_ref.at[zp, y, high], to(zm, y))
    uy["zp"] = (send(u_ref.at[zp, y], u_ref.at[zp, y], to(z, yp)), send(u_ref.at[zp, y], u_ref.at[zp, y], to(z, ym)))

    g_far_a.wait_recv()
    g_far_b.wait_recv()
    gz["y2"] = (send(g_ref.at[z, y2], g_ref.at[z, y2], to(zp, y)), send(g_ref.at[z, y2], g_ref.at[z, y2], to(zm, y)))
    u_far_a.wait_recv()
    u_far_b.wait_recv()
    uy["z2"] = (send(u_ref.at[z2, y], u_ref.at[z2, y], to(z, yp)), send(u_ref.at[z2, y], u_ref.at[z2, y], to(z, ym)))

    for c in ar_b:
        c.wait_recv()

    r_load.wait()
    g_load.wait()

    def add_chips(t, squares):
        cols = pl.ds(pl.multiple_of(t * width, width), width)
        acc = b_src[cx, :, cols].astype(jnp.float32)
        for d in range(1, xs):
            acc = acc + b_buf[(cx + d) % xs, :, cols].astype(jnp.float32)
        state = acc + r_buf[:, cols].astype(jnp.float32)
        s_buf[:, cols] = state
        return squares + jnp.sum(state * state, axis=1, keepdims=True)

    squares = lax.fori_loop(0, tiles, add_chips, jnp.zeros((m_buf.shape[0], 1), jnp.float32))
    scale = lax.rsqrt(squares / m_buf.shape[1] + EPS)

    def scale_rows(t, carry):
        cols = pl.ds(pl.multiple_of(t * width, width), width)
        normed = s_buf[:, cols] * scale * gain_buf[:, cols]
        m_buf[:, cols] = normed.astype(m_buf.dtype)
        return carry

    lax.fori_loop(0, tiles, scale_rows, 0)
    own_sum = pltpu.make_async_copy(m_buf, sum_ref.at[cx, cc], local_sems.at[4])
    own_sum.start()
    own_sum.wait()
    ar_c = [
        ar_copy(xs - 1 + d, sum_ref.at[cx, cc], sum_ref.at[cx, cc], x_peers[d - 1])
        for d in range(1, xs)
    ]

    for (gkey, yy), (ukey, zz) in zip(
        (("y", y), ("ym", ym), ("yp", yp), ("y2", y2)),
        (("z", z), ("zm", zm), ("zp", zp), ("z2", z2)),
    ):
        from_zm, from_zp = gz[gkey]
        from_ym, from_yp = uy[ukey]
        from_zm.wait_recv()
        send(g_ref.at[zm, yy, low], g_ref.at[zm, yy, low], to(zp, y))
        from_ym.wait_recv()
        send(u_ref.at[zz, ym, low], u_ref.at[zz, ym, low], to(z, yp))
        from_zp.wait_recv()
        send(g_ref.at[zp, yy, high], g_ref.at[zp, yy, high], to(zm, y))
        from_yp.wait_recv()
        send(u_ref.at[zz, yp, high], u_ref.at[zz, yp, high], to(z, ym))

    for c in ar_c:
        c.wait_recv()
    ar_d = ar_copy(2 * xs - 1, sum_ref.at[:, cc], sum_ref.at[:, cc], core_peer)
    ar_d.wait_recv()
    for c in [ar_a] + ar_b + ar_c + [ar_d]:
        c.wait_send()

    waited = [g_from_ym, g_from_yp, u_from_zm, u_from_zp, g_far_a, g_far_b, u_far_a, u_far_b]
    waited += list(gz["y"]) + list(gz["ym"]) + list(gz["yp"]) + list(gz["y2"])
    waited += list(uy["z"]) + list(uy["zm"]) + list(uy["zp"]) + list(uy["z2"])
    for c in copies:
        if not any(c is w for w in waited):
            c.wait_recv()
    for c in copies:
        c.wait_send()
    for c in kv_copies:
        c.wait_recv()
        c.wait_send()
    own_g.wait()
    own_u.wait()
    own_kv.wait()


def gather_weights(w_gate, w_up, kv_send, attended, w_out, residual, gain):
    rows, cols = w_gate.shape
    xs, _, chunk, width = residual.shape
    product = jax.ShapeDtypeStruct(residual.shape, jnp.bfloat16)
    any_spec = pl.BlockSpec(memory_space=pl.ANY)
    vmem_spec = pl.BlockSpec(memory_space=pltpu.VMEM)
    piece = jax.ShapeDtypeStruct((RING, RING, rows, cols), w_gate.dtype)
    slots = jax.ShapeDtypeStruct(kv_send.shape, kv_send.dtype)
    sums = jax.ShapeDtypeStruct(product.shape, product.dtype)
    sems = KV_SEMS + kv_send.shape[0] - 1
    return pl.pallas_call(
        gather_kernel,
        out_shape=(piece, piece, slots, sums),
        in_specs=[any_spec] * 3 + [vmem_spec] * 2 + [any_spec] * 2,
        out_specs=(any_spec, any_spec, any_spec, any_spec),
        scratch_shapes=[
            pltpu.SemaphoreType.DMA((sems,)),
            pltpu.SemaphoreType.DMA((sems,)),
            pltpu.SemaphoreType.DMA((7,)),
            pltpu.SemaphoreType.DMA((2 * xs,)),
            pltpu.SemaphoreType.DMA((2 * xs,)),
            pltpu.VMEM((xs, chunk, width), product.dtype),
            pltpu.VMEM(product.shape, product.dtype),
            pltpu.VMEM((xs, chunk, width), product.dtype),
            pltpu.VMEM((xs, chunk, width), product.dtype),
            pltpu.VMEM((chunk, width), product.dtype),
            pltpu.VMEM((chunk, width), residual.dtype),
            pltpu.VMEM((1, width), jnp.float32),
            pltpu.VMEM((chunk, width), jnp.float32),
        ],
        compiler_params=pltpu.CompilerParams(
            collective_id=0, has_side_effects=True, vmem_limit_bytes=48 * 1024 * 1024
        ),
    )(w_gate, w_up, kv_send, attended, w_out, residual, gain)

def normalize(resid_rows, summed, gain_row):
    state = resid_rows.astype(jnp.float32) + summed
    scale_row = lax.rsqrt(jnp.mean(state * state, axis=-1, keepdims=True) + EPS)
    return (state * scale_row * gain_row).astype(jnp.bfloat16)


def shards(
    q_pre,
    k_pre,
    v_pre,
    q_bias,
    k_bias,
    v_bias,
    segment_ids,
    lengths,
    page_table,
    w_out,
    residual,
    norm_gain,
    w_gate,
    w_up,
):
    me_req = lax.axis_index("req")
    groups_all = lax.axis_size("req")
    block_rows = q_pre.shape[0]
    kv_heads = k_pre.shape[1] // HD
    q_heads = q_pre.shape[1] // HD
    group_size = q_heads // kv_heads


    own_lens = lax.dynamic_index_in_dim(lengths, me_req, 0, keepdims=False)
    own_pages = lax.dynamic_index_in_dim(page_table, me_req, 0, keepdims=False)
    own_owner = own_pages // REQS
    starts = jnp.cumsum(own_lens) - own_lens

    alive = segment_ids >= 0
    req_idx = jnp.clip(segment_ids - me_req * REQS, 0, REQS - 1)
    req_hit = req_idx[:, None] == jnp.arange(REQS)[None, :]
    row_start = jnp.sum(jnp.where(req_hit, starts[None, :], 0), axis=1)
    token = jnp.arange(block_rows, dtype=jnp.int32)
    positions = (token - row_start).astype(jnp.float32)
    keep = alive[:, None, None]

    queries = rotate(
        (q_pre.astype(jnp.float32) + q_bias).reshape(block_rows, q_heads, HD), positions
    )
    queries = jnp.where(keep, queries, 0.0).astype(jnp.bfloat16)
    keys = rotate((k_pre.astype(jnp.float32) + k_bias).reshape(block_rows, kv_heads, HD), positions)
    keys = jnp.where(keep, keys, 0.0).astype(jnp.bfloat16)
    values = (v_pre.astype(jnp.float32) + v_bias).reshape(block_rows, kv_heads, HD)
    values = jnp.where(keep, values, 0.0).astype(jnp.bfloat16)

    scale_factor = 1.0 / math.sqrt(HD)
    q_groups = queries.reshape(block_rows, kv_heads, group_size, HD)
    scores = (
        jnp.einsum("qhge,khe->hgqk", q_groups, keys, preferred_element_type=jnp.float32)
        * scale_factor
    )
    allowed = (
        (segment_ids[:, None] == segment_ids[None, :])
        & alive[None, :]
        & (token[None, :] <= token[:, None])
    )[None, None]
    row_max = jnp.max(jnp.where(allowed, scores, -1e30), axis=-1, keepdims=True)
    weights = jnp.where(allowed, jnp.exp(scores - row_max), 0.0)
    row_sum = jnp.sum(weights, axis=-1, keepdims=True)
    present = alive[None, None, :, None]
    probs = jnp.where(present, weights / jnp.where(present, row_sum, 1.0), 0.0).astype(
        jnp.bfloat16
    )
    attended = jnp.einsum("hgqk,khe->qhge", probs, values, preferred_element_type=jnp.float32)
    attended = attended.astype(jnp.bfloat16).reshape(block_rows, q_heads * HD)

    kv_rows = jnp.concatenate([keys, values], axis=-1).reshape(block_rows, -1)
    slot = jnp.arange(PAGE, dtype=jnp.int32)
    source = starts[:, None] + slot[None, :]
    live_slot = slot[None, :] < own_lens[:, None]
    select = (live_slot[:, :, None] & (source[:, :, None] == token[None, None, :])).astype(
        jnp.bfloat16
    )
    pages = jnp.einsum("jst,tc->jsc", select, kv_rows, preferred_element_type=jnp.float32)
    to_owner = (own_owner[None, :] == jnp.arange(groups_all)[:, None]).astype(jnp.bfloat16)
    kv_send = jnp.einsum(
        "gj,jsc->gsc", to_owner, pages.astype(jnp.bfloat16), preferred_element_type=jnp.float32
    ).astype(jnp.bfloat16)
    hits = (
        page_table[None, :, :] == (me_req * REQS + jnp.arange(REQS, dtype=jnp.int32))[:, None, None]
    )
    page_select = jnp.sum(hits.astype(jnp.int32), axis=2).astype(jnp.bfloat16)

    n_mp = lax.axis_size("mp")
    split_rows = (n_mp // 2, 2, block_rows // n_mp, residual.shape[-1])
    g_full, u_full, kv_in, normed = gather_weights(
        w_gate,
        w_up,
        kv_send,
        attended,
        w_out,
        residual.reshape(split_rows),
        norm_gain.reshape(1, -1).astype(jnp.float32),
    )
    normed = normed.reshape(block_rows, -1)
    kv_in = kv_in.reshape(groups_all, PAGE, kv_heads, 2 * HD)
    cache_out = jnp.einsum(
        "ls,sphc->lhpc", page_select, kv_in, preferred_element_type=jnp.float32
    ).astype(jnp.bfloat16)
    wg_full = g_full.reshape(-1, w_gate.shape[1])
    wu_full = u_full.reshape(-1, w_up.shape[1])
    gate_acc = jnp.dot(normed, wg_full, preferred_element_type=jnp.float32)
    up_acc = jnp.dot(normed, wu_full, preferred_element_type=jnp.float32)
    hidden = (jax.nn.silu(gate_acc) * up_acc).astype(jnp.bfloat16)
    return (hidden, cache_out)


def solution(mesh):
    in_specs = (
        P("req", "mp"),
        P("req", "mp"),
        P("req", "mp"),
        P("mp"),
        P("mp"),
        P("mp"),
        P("req"),
        P(),
        P(),
        P("mp", None),
        P("req", None),
        P(),
        P("req", "mp"),
        P("req", "mp"),
    )
    out_specs = (P("req", "mp"), P("req", "mp", None, None))
    return jax.shard_map(shards, mesh=mesh, in_specs=in_specs, out_specs=out_specs, check_vma=False)
```

```python
import math

import jax
import jax.numpy as jnp
from jax import lax
from jax.sharding import PartitionSpec as P
from jax.experimental import pallas as pl
from jax.experimental.pallas import tpu as pltpu

HD = 128
PAGE = 128
REQS = 4
RING = 4
KV_SEMS = 40
AR_TILE = 512


THETA = 1000000.0
EPS = 1e-06


def rotate(values, positions):
    half_dim = values.shape[-1] // 2
    frequencies = THETA ** (-jnp.arange(half_dim, dtype=jnp.float32) * (2.0 / values.shape[-1]))
    angles = positions[:, None] * frequencies[None, :]
    cosine = jnp.cos(angles)[:, None, :]
    sine_part = jnp.sin(angles)[:, None, :]
    first_half = values[..., :half_dim]
    second = values[..., half_dim:]
    return jnp.concatenate(
        [first_half * cosine - second * sine_part, second * cosine + first_half * sine_part],
        axis=-1,
    )


def gather_kernel(
    wg_ref, wu_ref, kv_ref, att_ref, wout_ref, res_ref, gain_ref, src_ref, g_ref, u_ref, kv_out,
    sum_ref, send_sems, recv_sems, local_sems, ar_send, ar_recv, a_buf, prod_v, b_src, b_buf,
    m_buf, r_buf, gain_buf, s_buf, kv_land,
):
    me = lax.axis_index("req")
    col = lax.axis_index("mp")
    z = me // RING
    y = me % RING
    yp = (y + 1) % RING
    ym = (y + RING - 1) % RING
    y2 = (y + 2) % RING
    zp = (z + 1) % RING
    zm = (z + RING - 1) % RING
    z2 = (z + 2) % RING
    rows = wg_ref.shape[0]
    low = pl.ds(0, rows // 2)
    high = pl.ds(rows // 2, rows - rows // 2)
    mesh_id = pl.DeviceIdType.MESH

    def to(zz, yy):
        return (zz * RING + yy, col)

    groups = kv_ref.shape[0]
    xs = prod_v.shape[0]
    cx = col // 2
    cc = col % 2
    core_peer = (me, cx * 2 + 1 - cc)
    x_peers = [(me, ((cx + d) % xs) * 2 + cc) for d in range(1, xs)]

    barrier = pltpu.get_barrier_semaphore()
    for d in range(1, groups):
        peer = ((me + d) % groups, col)
        pl.semaphore_signal(barrier, inc=1, device_id=peer, device_id_type=mesh_id)
    for peer in [core_peer] + x_peers:
        pl.semaphore_signal(barrier, inc=1, device_id=peer, device_id_type=mesh_id)
    pl.semaphore_wait(barrier, groups - 1 + xs)

    def ar_copy(k, src, dst, peer):
        c = pltpu.make_async_remote_copy(
            src_ref=src,
            dst_ref=dst,
            send_sem=ar_send.at[k],
            recv_sem=ar_recv.at[k],
            device_id=peer,
            device_id_type=mesh_id,
        )
        c.start()
        return c

    r_load = pltpu.make_async_copy(res_ref.at[cx, cc], r_buf, local_sems.at[5])
    r_load.start()
    g_load = pltpu.make_async_copy(gain_ref, gain_buf, local_sems.at[6])
    g_load.start()
    width = AR_TILE
    tiles = a_buf.shape[-1] // width

    copies = []

    def send(src, dst, peer):
        k = len(copies)
        c = pltpu.make_async_remote_copy(
            src_ref=src,
            dst_ref=dst,
            send_sem=send_sems.at[k],
            recv_sem=recv_sems.at[k],
            device_id=peer,
            device_id_type=mesh_id,
        )
        c.start()
        copies.append(c)
        return c

    own_g = pltpu.make_async_copy(wg_ref, g_ref.at[z, y], local_sems.at[0])
    own_u = pltpu.make_async_copy(wu_ref, u_ref.at[z, y], local_sems.at[1])
    own_g.start()
    own_u.start()

    g_from_ym = send(wg_ref, g_ref.at[z, y], to(z, yp))
    g_from_yp = send(wg_ref, g_ref.at[z, y], to(z, ym))
    u_from_zm = send(wu_ref, u_ref.at[z, y], to(zp, y))
    u_from_zp = send(wu_ref, u_ref.at[z, y], to(zm, y))
    gz = {"y": (send(wg_ref, g_ref.at[z, y], to(zp, y)), send(wg_ref, g_ref.at[z, y], to(zm, y)))}
    uy = {"z": (send(wu_ref, u_ref.at[z, y], to(z, yp)), send(wu_ref, u_ref.at[z, y], to(z, ym)))}
    kv_copies = []
    own_kv = pltpu.make_async_copy(kv_ref.at[me], kv_land.at[me], local_sems.at[2])
    own_kv.start()
    for d in range(1, groups):
        dest = (me + d) % groups
        c = pltpu.make_async_remote_copy(
            src_ref=kv_ref.at[dest],
            dst_ref=kv_land.at[me],
            send_sem=send_sems.at[KV_SEMS + d - 1],
            recv_sem=recv_sems.at[KV_SEMS + d - 1],
            device_id=(dest, col),
            device_id_type=mesh_id,
        )
        c.start()
        kv_copies.append(c)

    chunk = prod_v.shape[2]

    def project(k, carry):
        rows = att_ref[pl.ds(pl.multiple_of(k * chunk, chunk), chunk), :]
        part = jnp.dot(rows, wout_ref[...], preferred_element_type=jnp.float32)
        prod_v[k // 2, k % 2] = part.astype(prod_v.dtype)
        return carry

    lax.fori_loop(0, 2 * xs, project, 0)
    ar_a = ar_copy(0, prod_v.at[:, 1 - cc], a_buf, core_peer)

    ar_a.wait_recv()

    def add_pair(i, carry):
        xi = i // tiles
        cols = pl.ds(pl.multiple_of((i % tiles) * width, width), width)
        pair = prod_v[xi, cc, :, cols].astype(jnp.float32) + a_buf[xi, :, cols].astype(jnp.float32)
        b_src[xi, :, cols] = pair.astype(b_src.dtype)
        return carry

    lax.fori_loop(0, xs * tiles, add_pair, 0)
    ar_b = [
        ar_copy(d, b_src.at[(cx + d) % xs], b_buf.at[cx], x_peers[d - 1]) for d in range(1, xs)
    ]

    g_from_ym.wait_recv()
    g_far_a = send(g_ref.at[z, ym, low], g_ref.at[z, ym, low], to(z, yp))
    gz["ym"] = (send(g_ref.at[z, ym], g_ref.at[z, ym], to(zp, y)), send(g_ref.at[z, ym], g_ref.at[z, ym], to(zm, y)))
    u_from_zm.wait_recv()
    u_far_a = send(u_ref.at[zm, y, low], u_ref.at[zm, y, low], to(zp, y))
    uy["zm"] = (send(u_ref.at[zm, y], u_ref.at[zm, y], to(z, yp)), send(u_ref.at[zm, y], u_ref.at[zm, y], to(z, ym)))
    g_from_yp.wait_recv()
    g_far_b = send(g_ref.at[z, yp, high], g_ref.at[z, yp, high], to(z, ym))
    gz["yp"] = (send(g_ref.at[z, yp], g_ref.at[z, yp], to(zp, y)), send(g_ref.at[z, yp], g_ref.at[z, yp], to(zm, y)))
    u_from_zp.wait_recv()
    u_far_b = send(u_ref.at[zp, y, high], u_ref.at[zp, y, high], to(zm, y))
    uy["zp"] = (send(u_ref.at[zp, y], u_ref.at[zp, y], to(z, yp)), send(u_ref.at[zp, y], u_ref.at[zp, y], to(z, ym)))

    g_far_a.wait_recv()
    g_far_b.wait_recv()
    gz["y2"] = (send(g_ref.at[z, y2], g_ref.at[z, y2], to(zp, y)), send(g_ref.at[z, y2], g_ref.at[z, y2], to(zm, y)))
    u_far_a.wait_recv()
    u_far_b.wait_recv()
    uy["z2"] = (send(u_ref.at[z2, y], u_ref.at[z2, y], to(z, yp)), send(u_ref.at[z2, y], u_ref.at[z2, y], to(z, ym)))

    for c in ar_b:
        c.wait_recv()

    r_load.wait()
    g_load.wait()

    def add_chips(t, squares):
        cols = pl.ds(pl.multiple_of(t * width, width), width)
        acc = b_src[cx, :, cols].astype(jnp.float32)
        for d in range(1, xs):
            acc = acc + b_buf[(cx + d) % xs, :, cols].astype(jnp.float32)
        state = acc + r_buf[:, cols].astype(jnp.float32)
        s_buf[:, cols] = state
        return squares + jnp.sum(state * state, axis=1, keepdims=True)

    squares = lax.fori_loop(0, tiles, add_chips, jnp.zeros((m_buf.shape[0], 1), jnp.float32))
    scale = lax.rsqrt(squares / m_buf.shape[1] + EPS)

    def scale_rows(t, carry):
        cols = pl.ds(pl.multiple_of(t * width, width), width)
        normed = s_buf[:, cols] * scale * gain_buf[:, cols]
        m_buf[:, cols] = normed.astype(m_buf.dtype)
        return carry

    lax.fori_loop(0, tiles, scale_rows, 0)
    own_sum = pltpu.make_async_copy(m_buf, sum_ref.at[cx, cc], local_sems.at[4])
    own_sum.start()
    own_sum.wait()
    ar_c = [
        ar_copy(xs - 1 + d, sum_ref.at[cx, cc], sum_ref.at[cx, cc], x_peers[d - 1])
        for d in range(1, xs)
    ]

    for (gkey, yy), (ukey, zz) in zip(
        (("y", y), ("ym", ym), ("yp", yp), ("y2", y2)),
        (("z", z), ("zm", zm), ("zp", zp), ("z2", z2)),
    ):
        from_zm, from_zp = gz[gkey]
        from_ym, from_yp = uy[ukey]
        from_zm.wait_recv()
        send(g_ref.at[zm, yy, low], g_ref.at[zm, yy, low], to(zp, y))
        from_ym.wait_recv()
        send(u_ref.at[zz, ym, low], u_ref.at[zz, ym, low], to(z, yp))
        from_zp.wait_recv()
        send(g_ref.at[zp, yy, high], g_ref.at[zp, yy, high], to(zm, y))
        from_yp.wait_recv()
        send(u_ref.at[zz, yp, high], u_ref.at[zz, yp, high], to(z, ym))

    for c in ar_c:
        c.wait_recv()
    ar_d = ar_copy(2 * xs - 1, sum_ref.at[:, cc], sum_ref.at[:, cc], core_peer)
    ar_d.wait_recv()
    for c in [ar_a] + ar_b + ar_c + [ar_d]:
        c.wait_send()

    waited = [g_from_ym, g_from_yp, u_from_zm, u_from_zp, g_far_a, g_far_b, u_far_a, u_far_b]
    waited += list(gz["y"]) + list(gz["ym"]) + list(gz["yp"]) + list(gz["y2"])
    waited += list(uy["z"]) + list(uy["zm"]) + list(uy["zp"]) + list(uy["z2"])
    for c in copies:
        if not any(c is w for w in waited):
            c.wait_recv()
    for c in copies:
        c.wait_send()
    for c in kv_copies:
        c.wait_recv()
        c.wait_send()
    own_g.wait()
    own_u.wait()
    own_kv.wait()
    for page in range(kv_out.shape[0]):
        kv_out[page] = kv_land[src_ref[page]]


def gather_weights(w_gate, w_up, kv_send, attended, w_out, residual, gain, page_src):
    rows, cols = w_gate.shape
    xs, _, chunk, width = residual.shape
    product = jax.ShapeDtypeStruct(residual.shape, jnp.bfloat16)
    any_spec = pl.BlockSpec(memory_space=pl.ANY)
    vmem_spec = pl.BlockSpec(memory_space=pltpu.VMEM)
    piece = jax.ShapeDtypeStruct((RING, RING, rows, cols), w_gate.dtype)
    slots = jax.ShapeDtypeStruct((page_src.shape[0],) + kv_send.shape[1:], kv_send.dtype)
    smem_spec = pl.BlockSpec(memory_space=pltpu.SMEM)
    sums = jax.ShapeDtypeStruct(product.shape, product.dtype)
    sems = KV_SEMS + kv_send.shape[0] - 1
    return pl.pallas_call(
        gather_kernel,
        out_shape=(piece, piece, slots, sums),
        in_specs=[any_spec] * 3 + [vmem_spec] * 2 + [any_spec] * 2 + [smem_spec],
        out_specs=(any_spec, any_spec, vmem_spec, any_spec),
        scratch_shapes=[
            pltpu.SemaphoreType.DMA((sems,)),
            pltpu.SemaphoreType.DMA((sems,)),
            pltpu.SemaphoreType.DMA((7,)),
            pltpu.SemaphoreType.DMA((2 * xs,)),
            pltpu.SemaphoreType.DMA((2 * xs,)),
            pltpu.VMEM((xs, chunk, width), product.dtype),
            pltpu.VMEM(product.shape, product.dtype),
            pltpu.VMEM((xs, chunk, width), product.dtype),
            pltpu.VMEM((xs, chunk, width), product.dtype),
            pltpu.VMEM((chunk, width), product.dtype),
            pltpu.VMEM((chunk, width), residual.dtype),
            pltpu.VMEM((1, width), jnp.float32),
            pltpu.VMEM((chunk, width), jnp.float32),
            pltpu.VMEM(kv_send.shape, kv_send.dtype),
        ],
        compiler_params=pltpu.CompilerParams(
            collective_id=0, has_side_effects=True, vmem_limit_bytes=48 * 1024 * 1024
        ),
    )(w_gate, w_up, kv_send, attended, w_out, residual, gain, page_src)

def normalize(resid_rows, summed, gain_row):
    state = resid_rows.astype(jnp.float32) + summed
    scale_row = lax.rsqrt(jnp.mean(state * state, axis=-1, keepdims=True) + EPS)
    return (state * scale_row * gain_row).astype(jnp.bfloat16)


def shards(
    q_pre,
    k_pre,
    v_pre,
    q_bias,
    k_bias,
    v_bias,
    segment_ids,
    lengths,
    page_table,
    w_out,
    residual,
    norm_gain,
    w_gate,
    w_up,
):
    me_req = lax.axis_index("req")
    groups_all = lax.axis_size("req")
    block_rows = q_pre.shape[0]
    kv_heads = k_pre.shape[1] // HD
    q_heads = q_pre.shape[1] // HD
    group_size = q_heads // kv_heads


    own_lens = lax.dynamic_index_in_dim(lengths, me_req, 0, keepdims=False)
    own_pages = lax.dynamic_index_in_dim(page_table, me_req, 0, keepdims=False)
    own_owner = own_pages // REQS
    starts = jnp.cumsum(own_lens) - own_lens

    alive = segment_ids >= 0
    req_idx = jnp.clip(segment_ids - me_req * REQS, 0, REQS - 1)
    req_hit = req_idx[:, None] == jnp.arange(REQS)[None, :]
    row_start = jnp.sum(jnp.where(req_hit, starts[None, :], 0), axis=1)
    token = jnp.arange(block_rows, dtype=jnp.int32)
    positions = (token - row_start).astype(jnp.float32)
    keep = alive[:, None, None]

    queries = rotate(
        (q_pre.astype(jnp.float32) + q_bias).reshape(block_rows, q_heads, HD), positions
    )
    queries = jnp.where(keep, queries, 0.0).astype(jnp.bfloat16)
    keys = rotate((k_pre.astype(jnp.float32) + k_bias).reshape(block_rows, kv_heads, HD), positions)
    keys = jnp.where(keep, keys, 0.0).astype(jnp.bfloat16)
    values = (v_pre.astype(jnp.float32) + v_bias).reshape(block_rows, kv_heads, HD)
    values = jnp.where(keep, values, 0.0).astype(jnp.bfloat16)

    scale_factor = 1.0 / math.sqrt(HD)
    q_groups = queries.reshape(block_rows, kv_heads, group_size, HD)
    scores = (
        jnp.einsum("qhge,khe->hgqk", q_groups, keys, preferred_element_type=jnp.float32)
        * scale_factor
    )
    allowed = (
        (segment_ids[:, None] == segment_ids[None, :])
        & alive[None, :]
        & (token[None, :] <= token[:, None])
    )[None, None]
    row_max = jnp.max(jnp.where(allowed, scores, -1e30), axis=-1, keepdims=True)
    weights = jnp.where(allowed, jnp.exp(scores - row_max), 0.0)
    row_sum = jnp.sum(weights, axis=-1, keepdims=True)
    present = alive[None, None, :, None]
    probs = jnp.where(present, weights / jnp.where(present, row_sum, 1.0), 0.0).astype(
        jnp.bfloat16
    )
    attended = jnp.einsum("hgqk,khe->qhge", probs, values, preferred_element_type=jnp.float32)
    attended = attended.astype(jnp.bfloat16).reshape(block_rows, q_heads * HD)

    kv_rows = jnp.concatenate([keys, values], axis=-1).reshape(block_rows, -1)
    slot = jnp.arange(PAGE, dtype=jnp.int32)
    source = starts[:, None] + slot[None, :]
    live_slot = slot[None, :] < own_lens[:, None]
    select = (live_slot[:, :, None] & (source[:, :, None] == token[None, None, :])).astype(
        jnp.bfloat16
    )
    pages = jnp.einsum("jst,tc->jsc", select, kv_rows, preferred_element_type=jnp.float32)
    to_owner = (own_owner[None, :] == jnp.arange(groups_all)[:, None]).astype(jnp.bfloat16)
    kv_send = jnp.einsum(
        "gj,jsc->gsc", to_owner, pages.astype(jnp.bfloat16), preferred_element_type=jnp.float32
    ).astype(jnp.bfloat16)
    hits = (
        page_table[None, :, :] == (me_req * REQS + jnp.arange(REQS, dtype=jnp.int32))[:, None, None]
    )
    page_src = jnp.argmax(jnp.any(hits, axis=2), axis=1).astype(jnp.int32)

    n_mp = lax.axis_size("mp")
    split_rows = (n_mp // 2, 2, block_rows // n_mp, residual.shape[-1])
    g_full, u_full, kv_in, normed = gather_weights(
        w_gate,
        w_up,
        kv_send,
        attended,
        w_out,
        residual.reshape(split_rows),
        norm_gain.reshape(1, -1).astype(jnp.float32),
        page_src,
    )
    normed = normed.reshape(block_rows, -1)
    assert kv_heads == 1
    cache_out = kv_in.reshape(REQS, kv_heads, PAGE, 2 * HD)
    wg_full = g_full.reshape(-1, w_gate.shape[1])
    wu_full = u_full.reshape(-1, w_up.shape[1])
    gate_acc = jnp.dot(normed, wg_full, preferred_element_type=jnp.float32)
    up_acc = jnp.dot(normed, wu_full, preferred_element_type=jnp.float32)
    hidden = (jax.nn.silu(gate_acc) * up_acc).astype(jnp.bfloat16)
    return (hidden, cache_out)


def solution(mesh):
    in_specs = (
        P("req", "mp"),
        P("req", "mp"),
        P("req", "mp"),
        P("mp"),
        P("mp"),
        P("mp"),
        P("req"),
        P(),
        P(),
        P("mp", None),
        P("req", None),
        P(),
        P("req", "mp"),
        P("req", "mp"),
    )
    out_specs = (P("req", "mp"), P("req", "mp", None, None))
    return jax.shard_map(shards, mesh=mesh, in_specs=in_specs, out_specs=out_specs, check_vma=False)
```

```python
import math

import jax
import jax.numpy as jnp
from jax import lax
from jax.sharding import PartitionSpec as P
from jax.experimental import pallas as pl
from jax.experimental.pallas import tpu as pltpu

HD = 128
PAGE = 128
REQS = 4
RING = 4
KV_SEMS = 40
AR_TILE = 512


THETA = 1000000.0
EPS = 1e-06


def rotate(values, positions):
    half_dim = values.shape[-1] // 2
    frequencies = THETA ** (-jnp.arange(half_dim, dtype=jnp.float32) * (2.0 / values.shape[-1]))
    angles = positions[:, None] * frequencies[None, :]
    cosine = jnp.cos(angles)[:, None, :]
    sine_part = jnp.sin(angles)[:, None, :]
    first_half = values[..., :half_dim]
    second = values[..., half_dim:]
    return jnp.concatenate(
        [first_half * cosine - second * sine_part, second * cosine + first_half * sine_part],
        axis=-1,
    )


def gather_kernel(
    wg_ref, wu_ref, kv_ref, att_ref, wout_ref, res_ref, gain_ref, g_ref, u_ref, kv_out, sum_ref,
    send_sems, recv_sems, local_sems, ar_send, ar_recv, a_buf, prod_v, b_src, b_buf, m_buf,
    r_buf, gain_buf, s_buf,
):
    me = lax.axis_index("req")
    col = lax.axis_index("mp")
    z = me // RING
    y = me % RING
    yp = (y + 1) % RING
    ym = (y + RING - 1) % RING
    y2 = (y + 2) % RING
    zp = (z + 1) % RING
    zm = (z + RING - 1) % RING
    z2 = (z + 2) % RING
    rows = wg_ref.shape[0]
    low = pl.ds(0, rows // 2)
    high = pl.ds(rows // 2, rows - rows // 2)
    mesh_id = pl.DeviceIdType.MESH

    def to(zz, yy):
        return (zz * RING + yy, col)

    groups = kv_ref.shape[0]
    xs = prod_v.shape[0]
    cx = col // 2
    cc = col % 2
    core_peer = (me, cx * 2 + 1 - cc)
    x_peers = [(me, ((cx + d) % xs) * 2 + cc) for d in range(1, xs)]

    barrier = pltpu.get_barrier_semaphore()
    for d in range(1, groups):
        peer = ((me + d) % groups, col)
        pl.semaphore_signal(barrier, inc=1, device_id=peer, device_id_type=mesh_id)
    for peer in [core_peer] + x_peers:
        pl.semaphore_signal(barrier, inc=1, device_id=peer, device_id_type=mesh_id)
    pl.semaphore_wait(barrier, groups - 1 + xs)

    def ar_copy(k, src, dst, peer):
        c = pltpu.make_async_remote_copy(
            src_ref=src,
            dst_ref=dst,
            send_sem=ar_send.at[k],
            recv_sem=ar_recv.at[k],
            device_id=peer,
            device_id_type=mesh_id,
        )
        c.start()
        return c

    r_load = pltpu.make_async_copy(res_ref.at[cx, cc], r_buf, local_sems.at[5])
    r_load.start()
    g_load = pltpu.make_async_copy(gain_ref, gain_buf, local_sems.at[6])
    g_load.start()
    width = AR_TILE
    tiles = a_buf.shape[-1] // width

    copies = []

    def send(src, dst, peer):
        k = len(copies)
        c = pltpu.make_async_remote_copy(
            src_ref=src,
            dst_ref=dst,
            send_sem=send_sems.at[k],
            recv_sem=recv_sems.at[k],
            device_id=peer,
            device_id_type=mesh_id,
        )
        c.start()
        copies.append(c)
        return c

    own_g = pltpu.make_async_copy(wg_ref, g_ref.at[z, y], local_sems.at[0])
    own_u = pltpu.make_async_copy(wu_ref, u_ref.at[z, y], local_sems.at[1])
    own_g.start()
    own_u.start()

    g_from_ym = send(wg_ref, g_ref.at[z, y], to(z, yp))
    g_from_yp = send(wg_ref, g_ref.at[z, y], to(z, ym))
    u_from_zm = send(wu_ref, u_ref.at[z, y], to(zp, y))
    u_from_zp = send(wu_ref, u_ref.at[z, y], to(zm, y))
    gz = {"y": (send(wg_ref, g_ref.at[z, y], to(zp, y)), send(wg_ref, g_ref.at[z, y], to(zm, y)))}
    uy = {"z": (send(wu_ref, u_ref.at[z, y], to(z, yp)), send(wu_ref, u_ref.at[z, y], to(z, ym)))}

    chunk = prod_v.shape[2]

    def project(k, carry):
        rows = att_ref[pl.ds(pl.multiple_of(k * chunk, chunk), chunk), :]
        part = jnp.dot(rows, wout_ref[...], preferred_element_type=jnp.float32)
        prod_v[k // 2, k % 2] = part.astype(prod_v.dtype)
        return carry

    lax.fori_loop(0, 2 * xs, project, 0)
    ar_a = ar_copy(0, prod_v.at[:, 1 - cc], a_buf, core_peer)

    ar_a.wait_recv()

    def add_pair(i, carry):
        xi = i // tiles
        cols = pl.ds(pl.multiple_of((i % tiles) * width, width), width)
        pair = prod_v[xi, cc, :, cols].astype(jnp.float32) + a_buf[xi, :, cols].astype(jnp.float32)
        b_src[xi, :, cols] = pair.astype(b_src.dtype)
        return carry

    lax.fori_loop(0, xs * tiles, add_pair, 0)
    ar_b = [
        ar_copy(d, b_src.at[(cx + d) % xs], b_buf.at[cx], x_peers[d - 1]) for d in range(1, xs)
    ]

    g_from_ym.wait_recv()
    g_far_a = send(g_ref.at[z, ym, low], g_ref.at[z, ym, low], to(z, yp))
    gz["ym"] = (send(g_ref.at[z, ym], g_ref.at[z, ym], to(zp, y)), send(g_ref.at[z, ym], g_ref.at[z, ym], to(zm, y)))
    u_from_zm.wait_recv()
    u_far_a = send(u_ref.at[zm, y, low], u_ref.at[zm, y, low], to(zp, y))
    uy["zm"] = (send(u_ref.at[zm, y], u_ref.at[zm, y], to(z, yp)), send(u_ref.at[zm, y], u_ref.at[zm, y], to(z, ym)))
    g_from_yp.wait_recv()
    g_far_b = send(g_ref.at[z, yp, high], g_ref.at[z, yp, high], to(z, ym))
    gz["yp"] = (send(g_ref.at[z, yp], g_ref.at[z, yp], to(zp, y)), send(g_ref.at[z, yp], g_ref.at[z, yp], to(zm, y)))
    u_from_zp.wait_recv()
    u_far_b = send(u_ref.at[zp, y, high], u_ref.at[zp, y, high], to(zm, y))
    uy["zp"] = (send(u_ref.at[zp, y], u_ref.at[zp, y], to(z, yp)), send(u_ref.at[zp, y], u_ref.at[zp, y], to(z, ym)))

    g_far_a.wait_recv()
    g_far_b.wait_recv()
    gz["y2"] = (send(g_ref.at[z, y2], g_ref.at[z, y2], to(zp, y)), send(g_ref.at[z, y2], g_ref.at[z, y2], to(zm, y)))
    u_far_a.wait_recv()
    u_far_b.wait_recv()
    uy["z2"] = (send(u_ref.at[z2, y], u_ref.at[z2, y], to(z, yp)), send(u_ref.at[z2, y], u_ref.at[z2, y], to(z, ym)))
    kv_copies = []
    own_kv = pltpu.make_async_copy(kv_ref.at[me], kv_out.at[me], local_sems.at[2])
    own_kv.start()
    for d in range(1, groups):
        dest = (me + d) % groups
        c = pltpu.make_async_remote_copy(
            src_ref=kv_ref.at[dest],
            dst_ref=kv_out.at[me],
            send_sem=send_sems.at[KV_SEMS + d - 1],
            recv_sem=recv_sems.at[KV_SEMS + d - 1],
            device_id=(dest, col),
            device_id_type=mesh_id,
        )
        c.start()
        kv_copies.append(c)

    for c in ar_b:
        c.wait_recv()

    r_load.wait()
    g_load.wait()

    def add_chips(t, squares):
        cols = pl.ds(pl.multiple_of(t * width, width), width)
        acc = b_src[cx, :, cols].astype(jnp.float32)
        for d in range(1, xs):
            acc = acc + b_buf[(cx + d) % xs, :, cols].astype(jnp.float32)
        state = acc + r_buf[:, cols].astype(jnp.float32)
        s_buf[:, cols] = state
        return squares + jnp.sum(state * state, axis=1, keepdims=True)

    squares = lax.fori_loop(0, tiles, add_chips, jnp.zeros((m_buf.shape[0], 1), jnp.float32))
    scale = lax.rsqrt(squares / m_buf.shape[1] + EPS)

    def scale_rows(t, carry):
        cols = pl.ds(pl.multiple_of(t * width, width), width)
        normed = s_buf[:, cols] * scale * gain_buf[:, cols]
        m_buf[:, cols] = normed.astype(m_buf.dtype)
        return carry

    lax.fori_loop(0, tiles, scale_rows, 0)
    own_sum = pltpu.make_async_copy(m_buf, sum_ref.at[cx, cc], local_sems.at[4])
    own_sum.start()
    own_sum.wait()
    ar_c = [
        ar_copy(xs - 1 + d, sum_ref.at[cx, cc], sum_ref.at[cx, cc], x_peers[d - 1])
        for d in range(1, xs)
    ]

    for (gkey, yy), (ukey, zz) in zip(
        (("y", y), ("ym", ym), ("yp", yp), ("y2", y2)),
        (("z", z), ("zm", zm), ("zp", zp), ("z2", z2)),
    ):
        from_zm, from_zp = gz[gkey]
        from_ym, from_yp = uy[ukey]
        from_zm.wait_recv()
        send(g_ref.at[zm, yy, low], g_ref.at[zm, yy, low], to(zp, y))
        from_ym.wait_recv()
        send(u_ref.at[zz, ym, low], u_ref.at[zz, ym, low], to(z, yp))
        from_zp.wait_recv()
        send(g_ref.at[zp, yy, high], g_ref.at[zp, yy, high], to(zm, y))
        from_yp.wait_recv()
        send(u_ref.at[zz, yp, high], u_ref.at[zz, yp, high], to(z, ym))

    for c in ar_c:
        c.wait_recv()
    ar_d = ar_copy(2 * xs - 1, sum_ref.at[:, cc], sum_ref.at[:, cc], core_peer)
    ar_d.wait_recv()
    for c in [ar_a] + ar_b + ar_c + [ar_d]:
        c.wait_send()

    waited = [g_from_ym, g_from_yp, u_from_zm, u_from_zp, g_far_a, g_far_b, u_far_a, u_far_b]
    waited += list(gz["y"]) + list(gz["ym"]) + list(gz["yp"]) + list(gz["y2"])
    waited += list(uy["z"]) + list(uy["zm"]) + list(uy["zp"]) + list(uy["z2"])
    for c in copies:
        if not any(c is w for w in waited):
            c.wait_recv()
    for c in copies:
        c.wait_send()
    for c in kv_copies:
        c.wait_recv()
        c.wait_send()
    own_g.wait()
    own_u.wait()
    own_kv.wait()


def gather_weights(w_gate, w_up, kv_send, attended, w_out, residual, gain):
    rows, cols = w_gate.shape
    xs, _, chunk, width = residual.shape
    product = jax.ShapeDtypeStruct(residual.shape, jnp.bfloat16)
    any_spec = pl.BlockSpec(memory_space=pl.ANY)
    vmem_spec = pl.BlockSpec(memory_space=pltpu.VMEM)
    piece = jax.ShapeDtypeStruct((RING, RING, rows, cols), w_gate.dtype)
    slots = jax.ShapeDtypeStruct(kv_send.shape, kv_send.dtype)
    sums = jax.ShapeDtypeStruct(product.shape, product.dtype)
    sems = KV_SEMS + kv_send.shape[0] - 1
    return pl.pallas_call(
        gather_kernel,
        out_shape=(piece, piece, slots, sums),
        in_specs=[any_spec] * 3 + [vmem_spec] * 2 + [any_spec] * 2,
        out_specs=(any_spec, any_spec, any_spec, any_spec),
        scratch_shapes=[
            pltpu.SemaphoreType.DMA((sems,)),
            pltpu.SemaphoreType.DMA((sems,)),
            pltpu.SemaphoreType.DMA((7,)),
            pltpu.SemaphoreType.DMA((2 * xs,)),
            pltpu.SemaphoreType.DMA((2 * xs,)),
            pltpu.VMEM((xs, chunk, width), product.dtype),
            pltpu.VMEM(product.shape, product.dtype),
            pltpu.VMEM((xs, chunk, width), product.dtype),
            pltpu.VMEM((xs, chunk, width), product.dtype),
            pltpu.VMEM((chunk, width), product.dtype),
            pltpu.VMEM((chunk, width), residual.dtype),
            pltpu.VMEM((1, width), jnp.float32),
            pltpu.VMEM((chunk, width), jnp.float32),
        ],
        compiler_params=pltpu.CompilerParams(
            collective_id=0, has_side_effects=True, vmem_limit_bytes=48 * 1024 * 1024
        ),
    )(w_gate, w_up, kv_send, attended, w_out, residual, gain)

def normalize(resid_rows, summed, gain_row):
    state = resid_rows.astype(jnp.float32) + summed
    scale_row = lax.rsqrt(jnp.mean(state * state, axis=-1, keepdims=True) + EPS)
    return (state * scale_row * gain_row).astype(jnp.bfloat16)


def shards(
    q_pre,
    k_pre,
    v_pre,
    q_bias,
    k_bias,
    v_bias,
    segment_ids,
    lengths,
    page_table,
    w_out,
    residual,
    norm_gain,
    w_gate,
    w_up,
):
    me_req = lax.axis_index("req")
    groups_all = lax.axis_size("req")
    block_rows = q_pre.shape[0]
    kv_heads = k_pre.shape[1] // HD
    q_heads = q_pre.shape[1] // HD
    group_size = q_heads // kv_heads


    own_lens = lax.dynamic_index_in_dim(lengths, me_req, 0, keepdims=False)
    own_pages = lax.dynamic_index_in_dim(page_table, me_req, 0, keepdims=False)
    own_owner = own_pages // REQS
    starts = jnp.cumsum(own_lens) - own_lens

    alive = segment_ids >= 0
    req_idx = jnp.clip(segment_ids - me_req * REQS, 0, REQS - 1)
    req_hit = req_idx[:, None] == jnp.arange(REQS)[None, :]
    row_start = jnp.sum(jnp.where(req_hit, starts[None, :], 0), axis=1)
    token = jnp.arange(block_rows, dtype=jnp.int32)
    positions = (token - row_start).astype(jnp.float32)
    keep = alive[:, None, None]

    queries = rotate(
        (q_pre.astype(jnp.float32) + q_bias).reshape(block_rows, q_heads, HD), positions
    )
    queries = jnp.where(keep, queries, 0.0).astype(jnp.bfloat16)
    keys = rotate((k_pre.astype(jnp.float32) + k_bias).reshape(block_rows, kv_heads, HD), positions)
    keys = jnp.where(keep, keys, 0.0).astype(jnp.bfloat16)
    values = (v_pre.astype(jnp.float32) + v_bias).reshape(block_rows, kv_heads, HD)
    values = jnp.where(keep, values, 0.0).astype(jnp.bfloat16)

    scale_factor = 1.0 / math.sqrt(HD)
    q_groups = queries.reshape(block_rows, kv_heads, group_size, HD)
    scores = (
        jnp.einsum("qhge,khe->hgqk", q_groups, keys, preferred_element_type=jnp.float32)
        * scale_factor
    )
    allowed = (
        (segment_ids[:, None] == segment_ids[None, :])
        & alive[None, :]
        & (token[None, :] <= token[:, None])
    )[None, None]
    row_max = jnp.max(jnp.where(allowed, scores, -1e30), axis=-1, keepdims=True)
    weights = jnp.where(allowed, jnp.exp(scores - row_max), 0.0)
    row_sum = jnp.sum(weights, axis=-1, keepdims=True)
    present = alive[None, None, :, None]
    probs = jnp.where(present, weights / jnp.where(present, row_sum, 1.0), 0.0).astype(
        jnp.bfloat16
    )
    attended = jnp.einsum("hgqk,khe->qhge", probs, values, preferred_element_type=jnp.float32)
    attended = attended.astype(jnp.bfloat16).reshape(block_rows, q_heads * HD)

    kv_rows = jnp.concatenate([keys, values], axis=-1).reshape(block_rows, -1)
    slot = jnp.arange(PAGE, dtype=jnp.int32)
    source = starts[:, None] + slot[None, :]
    live_slot = slot[None, :] < own_lens[:, None]
    select = (live_slot[:, :, None] & (source[:, :, None] == token[None, None, :])).astype(
        jnp.bfloat16
    )
    pages = jnp.einsum("jst,tc->jsc", select, kv_rows, preferred_element_type=jnp.float32)
    to_owner = (own_owner[None, :] == jnp.arange(groups_all)[:, None]).astype(jnp.bfloat16)
    kv_send = jnp.einsum(
        "gj,jsc->gsc", to_owner, pages.astype(jnp.bfloat16), preferred_element_type=jnp.float32
    ).astype(jnp.bfloat16)
    hits = (
        page_table[None, :, :] == (me_req * REQS + jnp.arange(REQS, dtype=jnp.int32))[:, None, None]
    )
    page_select = jnp.sum(hits.astype(jnp.int32), axis=2).astype(jnp.bfloat16)

    n_mp = lax.axis_size("mp")
    split_rows = (n_mp // 2, 2, block_rows // n_mp, residual.shape[-1])
    g_full, u_full, kv_in, normed = gather_weights(
        w_gate,
        w_up,
        kv_send,
        attended,
        w_out,
        residual.reshape(split_rows),
        norm_gain.reshape(1, -1).astype(jnp.float32),
    )
    normed = normed.reshape(block_rows, -1)
    kv_in = kv_in.reshape(groups_all, PAGE, kv_heads, 2 * HD)
    cache_out = jnp.einsum(
        "ls,sphc->lhpc", page_select, kv_in, preferred_element_type=jnp.float32
    ).astype(jnp.bfloat16)
    wg_full = g_full.reshape(-1, w_gate.shape[1])
    wu_full = u_full.reshape(-1, w_up.shape[1])
    gate_acc = jnp.dot(normed, wg_full, preferred_element_type=jnp.float32)
    up_acc = jnp.dot(normed, wu_full, preferred_element_type=jnp.float32)
    hidden = (jax.nn.silu(gate_acc) * up_acc).astype(jnp.bfloat16)
    return (hidden, cache_out)


def solution(mesh):
    in_specs = (
        P("req", "mp"),
        P("req", "mp"),
        P("req", "mp"),
        P("mp"),
        P("mp"),
        P("mp"),
        P("req"),
        P(),
        P(),
        P("mp", None),
        P("req", None),
        P(),
        P("req", "mp"),
        P("req", "mp"),
    )
    out_specs = (P("req", "mp"), P("req", "mp", None, None))
    return jax.shard_map(shards, mesh=mesh, in_specs=in_specs, out_specs=out_specs, check_vma=False)
```

```python
import math

import jax
import jax.numpy as jnp
from jax import lax
from jax.sharding import PartitionSpec as P
from jax.experimental import pallas as pl
from jax.experimental.pallas import tpu as pltpu

HD = 128
PAGE = 128
REQS = 4
RING = 4
KV_SEMS = 40
AR_TILE = 512


THETA = 1000000.0
EPS = 1e-06


def rotate(values, positions):
    half_dim = values.shape[-1] // 2
    frequencies = THETA ** (-jnp.arange(half_dim, dtype=jnp.float32) * (2.0 / values.shape[-1]))
    angles = positions[:, None] * frequencies[None, :]
    cosine = jnp.cos(angles)[:, None, :]
    sine_part = jnp.sin(angles)[:, None, :]
    first_half = values[..., :half_dim]
    second = values[..., half_dim:]
    return jnp.concatenate(
        [first_half * cosine - second * sine_part, second * cosine + first_half * sine_part],
        axis=-1,
    )


def gather_kernel(
    wg_ref, wu_ref, kv_ref, att_ref, wout_ref, res_ref, gain_ref, g_ref, u_ref, kv_out, sum_ref,
    send_sems, recv_sems, local_sems, ar_send, ar_recv, a_buf, prod_v, b_src, b_buf, m_buf,
    r_buf, gain_buf, s_buf,
):
    me = lax.axis_index("req")
    col = lax.axis_index("mp")
    z = me // RING
    y = me % RING
    yp = (y + 1) % RING
    ym = (y + RING - 1) % RING
    y2 = (y + 2) % RING
    zp = (z + 1) % RING
    zm = (z + RING - 1) % RING
    z2 = (z + 2) % RING
    rows = wg_ref.shape[0]
    low = pl.ds(0, rows // 2)
    high = pl.ds(rows // 2, rows - rows // 2)
    mesh_id = pl.DeviceIdType.MESH

    def to(zz, yy):
        return (zz * RING + yy, col)

    groups = kv_ref.shape[0]
    xs = prod_v.shape[0]
    cx = col // 2
    cc = col % 2
    core_peer = (me, cx * 2 + 1 - cc)
    x_peers = [(me, ((cx + d) % xs) * 2 + cc) for d in range(1, xs)]

    barrier = pltpu.get_barrier_semaphore()
    for d in range(1, groups):
        peer = ((me + d) % groups, col)
        pl.semaphore_signal(barrier, inc=1, device_id=peer, device_id_type=mesh_id)
    for peer in [core_peer] + x_peers:
        pl.semaphore_signal(barrier, inc=1, device_id=peer, device_id_type=mesh_id)
    pl.semaphore_wait(barrier, groups - 1 + xs)

    def ar_copy(k, src, dst, peer):
        c = pltpu.make_async_remote_copy(
            src_ref=src,
            dst_ref=dst,
            send_sem=ar_send.at[k],
            recv_sem=ar_recv.at[k],
            device_id=peer,
            device_id_type=mesh_id,
        )
        c.start()
        return c

    r_load = pltpu.make_async_copy(res_ref.at[cx, cc], r_buf, local_sems.at[5])
    r_load.start()
    g_load = pltpu.make_async_copy(gain_ref, gain_buf, local_sems.at[6])
    g_load.start()
    width = AR_TILE
    tiles = a_buf.shape[-1] // width

    copies = []

    def send(src, dst, peer):
        k = len(copies)
        c = pltpu.make_async_remote_copy(
            src_ref=src,
            dst_ref=dst,
            send_sem=send_sems.at[k],
            recv_sem=recv_sems.at[k],
            device_id=peer,
            device_id_type=mesh_id,
        )
        c.start()
        copies.append(c)
        return c

    own_g = pltpu.make_async_copy(wg_ref, g_ref.at[z, y], local_sems.at[0])
    own_u = pltpu.make_async_copy(wu_ref, u_ref.at[z, y], local_sems.at[1])
    own_g.start()
    own_u.start()

    g_from_ym = send(wg_ref, g_ref.at[z, y], to(z, yp))
    g_from_yp = send(wg_ref, g_ref.at[z, y], to(z, ym))
    u_from_zm = send(wu_ref, u_ref.at[z, y], to(zp, y))
    u_from_zp = send(wu_ref, u_ref.at[z, y], to(zm, y))
    gz = {"y": (send(wg_ref, g_ref.at[z, y], to(zp, y)), send(wg_ref, g_ref.at[z, y], to(zm, y)))}
    uy = {"z": (send(wu_ref, u_ref.at[z, y], to(z, yp)), send(wu_ref, u_ref.at[z, y], to(z, ym)))}

    chunk = prod_v.shape[2]

    def project(k, carry):
        rows = att_ref[pl.ds(pl.multiple_of(k * chunk, chunk), chunk), :]
        part = jnp.dot(rows, wout_ref[...], preferred_element_type=jnp.float32)
        prod_v[k // 2, k % 2] = part.astype(prod_v.dtype)
        return carry

    lax.fori_loop(0, 2 * xs, project, 0)
    ar_a = ar_copy(0, prod_v.at[:, 1 - cc], a_buf, core_peer)

    ar_a.wait_recv()

    def add_pair(i, carry):
        xi = i // tiles
        cols = pl.ds(pl.multiple_of((i % tiles) * width, width), width)
        pair = prod_v[xi, cc, :, cols].astype(jnp.float32) + a_buf[xi, :, cols].astype(jnp.float32)
        b_src[xi, :, cols] = pair.astype(b_src.dtype)
        return carry

    lax.fori_loop(0, xs * tiles, add_pair, 0)
    ar_b = [
        ar_copy(d, b_src.at[(cx + d) % xs], b_buf.at[cx], x_peers[d - 1]) for d in range(1, xs)
    ]

    g_from_ym.wait_recv()
    g_far_a = send(g_ref.at[z, ym, low], g_ref.at[z, ym, low], to(z, yp))
    gz["ym"] = (send(g_ref.at[z, ym], g_ref.at[z, ym], to(zp, y)), send(g_ref.at[z, ym], g_ref.at[z, ym], to(zm, y)))
    u_from_zm.wait_recv()
    u_far_a = send(u_ref.at[zm, y, low], u_ref.at[zm, y, low], to(zp, y))
    uy["zm"] = (send(u_ref.at[zm, y], u_ref.at[zm, y], to(z, yp)), send(u_ref.at[zm, y], u_ref.at[zm, y], to(z, ym)))
    g_from_yp.wait_recv()
    g_far_b = send(g_ref.at[z, yp, high], g_ref.at[z, yp, high], to(z, ym))
    gz["yp"] = (send(g_ref.at[z, yp], g_ref.at[z, yp], to(zp, y)), send(g_ref.at[z, yp], g_ref.at[z, yp], to(zm, y)))
    u_from_zp.wait_recv()
    u_far_b = send(u_ref.at[zp, y, high], u_ref.at[zp, y, high], to(zm, y))
    uy["zp"] = (send(u_ref.at[zp, y], u_ref.at[zp, y], to(z, yp)), send(u_ref.at[zp, y], u_ref.at[zp, y], to(z, ym)))

    g_far_a.wait_recv()
    g_far_b.wait_recv()
    gz["y2"] = (send(g_ref.at[z, y2], g_ref.at[z, y2], to(zp, y)), send(g_ref.at[z, y2], g_ref.at[z, y2], to(zm, y)))
    u_far_a.wait_recv()
    u_far_b.wait_recv()
    uy["z2"] = (send(u_ref.at[z2, y], u_ref.at[z2, y], to(z, yp)), send(u_ref.at[z2, y], u_ref.at[z2, y], to(z, ym)))

    for c in ar_b:
        c.wait_recv()

    r_load.wait()
    g_load.wait()

    def add_chips(t, squares):
        cols = pl.ds(pl.multiple_of(t * width, width), width)
        acc = b_src[cx, :, cols].astype(jnp.float32)
        for d in range(1, xs):
            acc = acc + b_buf[(cx + d) % xs, :, cols].astype(jnp.float32)
        state = acc + r_buf[:, cols].astype(jnp.float32)
        s_buf[:, cols] = state
        return squares + jnp.sum(state * state, axis=1, keepdims=True)

    squares = lax.fori_loop(0, tiles, add_chips, jnp.zeros((m_buf.shape[0], 1), jnp.float32))
    scale = lax.rsqrt(squares / m_buf.shape[1] + EPS)

    def scale_rows(t, carry):
        cols = pl.ds(pl.multiple_of(t * width, width), width)
        normed = s_buf[:, cols] * scale * gain_buf[:, cols]
        m_buf[:, cols] = normed.astype(m_buf.dtype)
        return carry

    lax.fori_loop(0, tiles, scale_rows, 0)
    own_sum = pltpu.make_async_copy(m_buf, sum_ref.at[cx, cc], local_sems.at[4])
    own_sum.start()
    own_sum.wait()
    ar_c = [
        ar_copy(xs - 1 + d, sum_ref.at[cx, cc], sum_ref.at[cx, cc], x_peers[d - 1])
        for d in range(1, xs)
    ]

    for (gkey, yy), (ukey, zz) in zip(
        (("y", y), ("ym", ym), ("yp", yp), ("y2", y2)),
        (("z", z), ("zm", zm), ("zp", zp), ("z2", z2)),
    ):
        from_zm, from_zp = gz[gkey]
        from_ym, from_yp = uy[ukey]
        from_zm.wait_recv()
        send(g_ref.at[zm, yy, low], g_ref.at[zm, yy, low], to(zp, y))
        from_ym.wait_recv()
        send(u_ref.at[zz, ym, low], u_ref.at[zz, ym, low], to(z, yp))
        from_zp.wait_recv()
        send(g_ref.at[zp, yy, high], g_ref.at[zp, yy, high], to(zm, y))
        from_yp.wait_recv()
        send(u_ref.at[zz, yp, high], u_ref.at[zz, yp, high], to(z, ym))

    kv_copies = []
    own_kv = pltpu.make_async_copy(kv_ref.at[me], kv_out.at[me], local_sems.at[2])
    own_kv.start()
    for d in range(1, groups):
        dest = (me + d) % groups
        c = pltpu.make_async_remote_copy(
            src_ref=kv_ref.at[dest],
            dst_ref=kv_out.at[me],
            send_sem=send_sems.at[KV_SEMS + d - 1],
            recv_sem=recv_sems.at[KV_SEMS + d - 1],
            device_id=(dest, col),
            device_id_type=mesh_id,
        )
        c.start()
        kv_copies.append(c)

    for c in ar_c:
        c.wait_recv()
    ar_d = ar_copy(2 * xs - 1, sum_ref.at[:, cc], sum_ref.at[:, cc], core_peer)
    ar_d.wait_recv()
    for c in [ar_a] + ar_b + ar_c + [ar_d]:
        c.wait_send()

    waited = [g_from_ym, g_from_yp, u_from_zm, u_from_zp, g_far_a, g_far_b, u_far_a, u_far_b]
    waited += list(gz["y"]) + list(gz["ym"]) + list(gz["yp"]) + list(gz["y2"])
    waited += list(uy["z"]) + list(uy["zm"]) + list(uy["zp"]) + list(uy["z2"])
    for c in copies:
        if not any(c is w for w in waited):
            c.wait_recv()
    for c in copies:
        c.wait_send()
    for c in kv_copies:
        c.wait_recv()
        c.wait_send()
    own_g.wait()
    own_u.wait()
    own_kv.wait()


def gather_weights(w_gate, w_up, kv_send, attended, w_out, residual, gain):
    rows, cols = w_gate.shape
    xs, _, chunk, width = residual.shape
    product = jax.ShapeDtypeStruct(residual.shape, jnp.bfloat16)
    any_spec = pl.BlockSpec(memory_space=pl.ANY)
    vmem_spec = pl.BlockSpec(memory_space=pltpu.VMEM)
    piece = jax.ShapeDtypeStruct((RING, RING, rows, cols), w_gate.dtype)
    slots = jax.ShapeDtypeStruct(kv_send.shape, kv_send.dtype)
    sums = jax.ShapeDtypeStruct(product.shape, product.dtype)
    sems = KV_SEMS + kv_send.shape[0] - 1
    return pl.pallas_call(
        gather_kernel,
        out_shape=(piece, piece, slots, sums),
        in_specs=[any_spec] * 3 + [vmem_spec] * 2 + [any_spec] * 2,
        out_specs=(any_spec, any_spec, any_spec, any_spec),
        scratch_shapes=[
            pltpu.SemaphoreType.DMA((sems,)),
            pltpu.SemaphoreType.DMA((sems,)),
            pltpu.SemaphoreType.DMA((7,)),
            pltpu.SemaphoreType.DMA((2 * xs,)),
            pltpu.SemaphoreType.DMA((2 * xs,)),
            pltpu.VMEM((xs, chunk, width), product.dtype),
            pltpu.VMEM(product.shape, product.dtype),
            pltpu.VMEM((xs, chunk, width), product.dtype),
            pltpu.VMEM((xs, chunk, width), product.dtype),
            pltpu.VMEM((chunk, width), product.dtype),
            pltpu.VMEM((chunk, width), residual.dtype),
            pltpu.VMEM((1, width), jnp.float32),
            pltpu.VMEM((chunk, width), jnp.float32),
        ],
        compiler_params=pltpu.CompilerParams(
            collective_id=0, has_side_effects=True, vmem_limit_bytes=48 * 1024 * 1024
        ),
    )(w_gate, w_up, kv_send, attended, w_out, residual, gain)

def normalize(resid_rows, summed, gain_row):
    state = resid_rows.astype(jnp.float32) + summed
    scale_row = lax.rsqrt(jnp.mean(state * state, axis=-1, keepdims=True) + EPS)
    return (state * scale_row * gain_row).astype(jnp.bfloat16)


def shards(
    q_pre,
    k_pre,
    v_pre,
    q_bias,
    k_bias,
    v_bias,
    segment_ids,
    lengths,
    page_table,
    w_out,
    residual,
    norm_gain,
    w_gate,
    w_up,
):
    me_req = lax.axis_index("req")
    groups_all = lax.axis_size("req")
    block_rows = q_pre.shape[0]
    kv_heads = k_pre.shape[1] // HD
    q_heads = q_pre.shape[1] // HD
    group_size = q_heads // kv_heads


    own_lens = lax.dynamic_index_in_dim(lengths, me_req, 0, keepdims=False)
    own_pages = lax.dynamic_index_in_dim(page_table, me_req, 0, keepdims=False)
    own_owner = own_pages // REQS
    starts = jnp.cumsum(own_lens) - own_lens

    alive = segment_ids >= 0
    req_idx = jnp.clip(segment_ids - me_req * REQS, 0, REQS - 1)
    req_hit = req_idx[:, None] == jnp.arange(REQS)[None, :]
    row_start = jnp.sum(jnp.where(req_hit, starts[None, :], 0), axis=1)
    token = jnp.arange(block_rows, dtype=jnp.int32)
    positions = (token - row_start).astype(jnp.float32)
    keep = alive[:, None, None]

    queries = rotate(
        (q_pre.astype(jnp.float32) + q_bias).reshape(block_rows, q_heads, HD), positions
    )
    queries = jnp.where(keep, queries, 0.0).astype(jnp.bfloat16)
    keys = rotate((k_pre.astype(jnp.float32) + k_bias).reshape(block_rows, kv_heads, HD), positions)
    keys = jnp.where(keep, keys, 0.0).astype(jnp.bfloat16)
    values = (v_pre.astype(jnp.float32) + v_bias).reshape(block_rows, kv_heads, HD)
    values = jnp.where(keep, values, 0.0).astype(jnp.bfloat16)

    scale_factor = 1.0 / math.sqrt(HD)
    q_groups = queries.reshape(block_rows, kv_heads, group_size, HD)
    scores = (
        jnp.einsum("qhge,khe->hgqk", q_groups, keys, preferred_element_type=jnp.float32)
        * scale_factor
    )
    allowed = (
        (segment_ids[:, None] == segment_ids[None, :])
        & alive[None, :]
        & (token[None, :] <= token[:, None])
    )[None, None]
    row_max = jnp.max(jnp.where(allowed, scores, -1e30), axis=-1, keepdims=True)
    weights = jnp.where(allowed, jnp.exp(scores - row_max), 0.0)
    row_sum = jnp.sum(weights, axis=-1, keepdims=True)
    present = alive[None, None, :, None]
    probs = jnp.where(present, weights / jnp.where(present, row_sum, 1.0), 0.0).astype(
        jnp.bfloat16
    )
    attended = jnp.einsum("hgqk,khe->qhge", probs, values, preferred_element_type=jnp.float32)
    attended = attended.astype(jnp.bfloat16).reshape(block_rows, q_heads * HD)

    kv_rows = jnp.concatenate([keys, values], axis=-1).reshape(block_rows, -1)
    slot = jnp.arange(PAGE, dtype=jnp.int32)
    source = starts[:, None] + slot[None, :]
    live_slot = slot[None, :] < own_lens[:, None]
    select = (live_slot[:, :, None] & (source[:, :, None] == token[None, None, :])).astype(
        jnp.bfloat16
    )
    pages = jnp.einsum("jst,tc->jsc", select, kv_rows, preferred_element_type=jnp.float32)
    to_owner = (own_owner[None, :] == jnp.arange(groups_all)[:, None]).astype(jnp.bfloat16)
    kv_send = jnp.einsum(
        "gj,jsc->gsc", to_owner, pages.astype(jnp.bfloat16), preferred_element_type=jnp.float32
    ).astype(jnp.bfloat16)
    hits = (
        page_table[None, :, :] == (me_req * REQS + jnp.arange(REQS, dtype=jnp.int32))[:, None, None]
    )
    page_select = jnp.sum(hits.astype(jnp.int32), axis=2).astype(jnp.bfloat16)

    n_mp = lax.axis_size("mp")
    split_rows = (n_mp // 2, 2, block_rows // n_mp, residual.shape[-1])
    g_full, u_full, kv_in, normed = gather_weights(
        w_gate,
        w_up,
        kv_send,
        attended,
        w_out,
        residual.reshape(split_rows),
        norm_gain.reshape(1, -1).astype(jnp.float32),
    )
    normed = normed.reshape(block_rows, -1)
    kv_in = kv_in.reshape(groups_all, PAGE, kv_heads, 2 * HD)
    cache_out = jnp.einsum(
        "ls,sphc->lhpc", page_select, kv_in, preferred_element_type=jnp.float32
    ).astype(jnp.bfloat16)
    wg_full = g_full.reshape(-1, w_gate.shape[1])
    wu_full = u_full.reshape(-1, w_up.shape[1])
    gate_acc = jnp.dot(normed, wg_full, preferred_element_type=jnp.float32)
    up_acc = jnp.dot(normed, wu_full, preferred_element_type=jnp.float32)
    hidden = (jax.nn.silu(gate_acc) * up_acc).astype(jnp.bfloat16)
    return (hidden, cache_out)


def solution(mesh):
    in_specs = (
        P("req", "mp"),
        P("req", "mp"),
        P("req", "mp"),
        P("mp"),
        P("mp"),
        P("mp"),
        P("req"),
        P(),
        P(),
        P("mp", None),
        P("req", None),
        P(),
        P("req", "mp"),
        P("req", "mp"),
    )
    out_specs = (P("req", "mp"), P("req", "mp", None, None))
    return jax.shard_map(shards, mesh=mesh, in_specs=in_specs, out_specs=out_specs, check_vma=False)
```

```python
import math

import jax
import jax.numpy as jnp
from jax import lax
from jax.sharding import PartitionSpec as P
from jax.experimental import pallas as pl
from jax.experimental.pallas import tpu as pltpu

HD = 128
PAGE = 128
REQS = 4
RING = 4
KV_SEMS = 40
AR_TILE = 512


THETA = 1000000.0
EPS = 1e-06


def rotate(values, positions):
    half_dim = values.shape[-1] // 2
    frequencies = THETA ** (-jnp.arange(half_dim, dtype=jnp.float32) * (2.0 / values.shape[-1]))
    angles = positions[:, None] * frequencies[None, :]
    cosine = jnp.cos(angles)[:, None, :]
    sine_part = jnp.sin(angles)[:, None, :]
    first_half = values[..., :half_dim]
    second = values[..., half_dim:]
    return jnp.concatenate(
        [first_half * cosine - second * sine_part, second * cosine + first_half * sine_part],
        axis=-1,
    )


def gather_kernel(
    wg_ref, wu_ref, kv_ref, att_ref, wout_ref, res_ref, gain_ref, g_ref, u_ref, kv_out, sum_ref,
    send_sems, recv_sems, local_sems, ar_send, ar_recv, a_buf, prod_v, b_src, b_buf, m_buf,
    r_buf, gain_buf, s_buf,
):
    me = lax.axis_index("req")
    col = lax.axis_index("mp")
    z = me // RING
    y = me % RING
    yp = (y + 1) % RING
    ym = (y + RING - 1) % RING
    y2 = (y + 2) % RING
    zp = (z + 1) % RING
    zm = (z + RING - 1) % RING
    z2 = (z + 2) % RING
    rows = wg_ref.shape[0]
    low = pl.ds(0, rows // 2)
    high = pl.ds(rows // 2, rows - rows // 2)
    mesh_id = pl.DeviceIdType.MESH

    def to(zz, yy):
        return (zz * RING + yy, col)

    groups = kv_ref.shape[0]
    xs = prod_v.shape[0]
    cx = col // 2
    cc = col % 2
    core_peer = (me, cx * 2 + 1 - cc)
    x_peers = [(me, ((cx + d) % xs) * 2 + cc) for d in range(1, xs)]

    barrier = pltpu.get_barrier_semaphore()
    for d in range(1, groups):
        peer = ((me + d) % groups, col)
        pl.semaphore_signal(barrier, inc=1, device_id=peer, device_id_type=mesh_id)
    for peer in [core_peer] + x_peers:
        pl.semaphore_signal(barrier, inc=1, device_id=peer, device_id_type=mesh_id)
    pl.semaphore_wait(barrier, groups - 1 + xs)

    def ar_copy(k, src, dst, peer):
        c = pltpu.make_async_remote_copy(
            src_ref=src,
            dst_ref=dst,
            send_sem=ar_send.at[k],
            recv_sem=ar_recv.at[k],
            device_id=peer,
            device_id_type=mesh_id,
        )
        c.start()
        return c

    r_load = pltpu.make_async_copy(res_ref.at[cx, cc], r_buf, local_sems.at[5])
    r_load.start()
    g_load = pltpu.make_async_copy(gain_ref, gain_buf, local_sems.at[6])
    g_load.start()
    width = AR_TILE
    tiles = a_buf.shape[-1] // width

    copies = []

    def send(src, dst, peer):
        k = len(copies)
        c = pltpu.make_async_remote_copy(
            src_ref=src,
            dst_ref=dst,
            send_sem=send_sems.at[k],
            recv_sem=recv_sems.at[k],
            device_id=peer,
            device_id_type=mesh_id,
        )
        c.start()
        copies.append(c)
        return c

    own_g = pltpu.make_async_copy(wg_ref, g_ref.at[z, y], local_sems.at[0])
    own_u = pltpu.make_async_copy(wu_ref, u_ref.at[z, y], local_sems.at[1])
    own_g.start()
    own_u.start()

    g_from_ym = send(wg_ref, g_ref.at[z, y], to(z, yp))
    g_from_yp = send(wg_ref, g_ref.at[z, y], to(z, ym))
    u_from_zm = send(wu_ref, u_ref.at[z, y], to(zp, y))
    u_from_zp = send(wu_ref, u_ref.at[z, y], to(zm, y))
    gz = {"y": (send(wg_ref, g_ref.at[z, y], to(zp, y)), send(wg_ref, g_ref.at[z, y], to(zm, y)))}
    uy = {"z": (send(wu_ref, u_ref.at[z, y], to(z, yp)), send(wu_ref, u_ref.at[z, y], to(z, ym)))}


    g_from_ym.wait_recv()
    g_far_a = send(g_ref.at[z, ym, low], g_ref.at[z, ym, low], to(z, yp))
    gz["ym"] = (send(g_ref.at[z, ym], g_ref.at[z, ym], to(zp, y)), send(g_ref.at[z, ym], g_ref.at[z, ym], to(zm, y)))
    u_from_zm.wait_recv()
    u_far_a = send(u_ref.at[zm, y, low], u_ref.at[zm, y, low], to(zp, y))
    uy["zm"] = (send(u_ref.at[zm, y], u_ref.at[zm, y], to(z, yp)), send(u_ref.at[zm, y], u_ref.at[zm, y], to(z, ym)))
    g_from_yp.wait_recv()
    g_far_b = send(g_ref.at[z, yp, high], g_ref.at[z, yp, high], to(z, ym))
    gz["yp"] = (send(g_ref.at[z, yp], g_ref.at[z, yp], to(zp, y)), send(g_ref.at[z, yp], g_ref.at[z, yp], to(zm, y)))
    u_from_zp.wait_recv()
    u_far_b = send(u_ref.at[zp, y, high], u_ref.at[zp, y, high], to(zm, y))
    uy["zp"] = (send(u_ref.at[zp, y], u_ref.at[zp, y], to(z, yp)), send(u_ref.at[zp, y], u_ref.at[zp, y], to(z, ym)))

    g_far_a.wait_recv()
    g_far_b.wait_recv()
    gz["y2"] = (send(g_ref.at[z, y2], g_ref.at[z, y2], to(zp, y)), send(g_ref.at[z, y2], g_ref.at[z, y2], to(zm, y)))
    u_far_a.wait_recv()
    u_far_b.wait_recv()
    uy["z2"] = (send(u_ref.at[z2, y], u_ref.at[z2, y], to(z, yp)), send(u_ref.at[z2, y], u_ref.at[z2, y], to(z, ym)))
    kv_copies = []
    own_kv = pltpu.make_async_copy(kv_ref.at[me], kv_out.at[me], local_sems.at[2])
    own_kv.start()
    for d in range(1, groups):
        dest = (me + d) % groups
        c = pltpu.make_async_remote_copy(
            src_ref=kv_ref.at[dest],
            dst_ref=kv_out.at[me],
            send_sem=send_sems.at[KV_SEMS + d - 1],
            recv_sem=recv_sems.at[KV_SEMS + d - 1],
            device_id=(dest, col),
            device_id_type=mesh_id,
        )
        c.start()
        kv_copies.append(c)

    chunk = prod_v.shape[2]

    def project(k, carry):
        rows = att_ref[pl.ds(pl.multiple_of(k * chunk, chunk), chunk), :]
        part = jnp.dot(rows, wout_ref[...], preferred_element_type=jnp.float32)
        prod_v[k // 2, k % 2] = part.astype(prod_v.dtype)
        return carry

    lax.fori_loop(0, 2 * xs, project, 0)
    ar_a = ar_copy(0, prod_v.at[:, 1 - cc], a_buf, core_peer)

    ar_a.wait_recv()

    def add_pair(i, carry):
        xi = i // tiles
        cols = pl.ds(pl.multiple_of((i % tiles) * width, width), width)
        pair = prod_v[xi, cc, :, cols].astype(jnp.float32) + a_buf[xi, :, cols].astype(jnp.float32)
        b_src[xi, :, cols] = pair.astype(b_src.dtype)
        return carry

    lax.fori_loop(0, xs * tiles, add_pair, 0)
    ar_b = [
        ar_copy(d, b_src.at[(cx + d) % xs], b_buf.at[cx], x_peers[d - 1]) for d in range(1, xs)
    ]

    for c in ar_b:
        c.wait_recv()

    r_load.wait()
    g_load.wait()

    def add_chips(t, squares):
        cols = pl.ds(pl.multiple_of(t * width, width), width)
        acc = b_src[cx, :, cols].astype(jnp.float32)
        for d in range(1, xs):
            acc = acc + b_buf[(cx + d) % xs, :, cols].astype(jnp.float32)
        state = acc + r_buf[:, cols].astype(jnp.float32)
        s_buf[:, cols] = state
        return squares + jnp.sum(state * state, axis=1, keepdims=True)

    squares = lax.fori_loop(0, tiles, add_chips, jnp.zeros((m_buf.shape[0], 1), jnp.float32))
    scale = lax.rsqrt(squares / m_buf.shape[1] + EPS)

    def scale_rows(t, carry):
        cols = pl.ds(pl.multiple_of(t * width, width), width)
        normed = s_buf[:, cols] * scale * gain_buf[:, cols]
        m_buf[:, cols] = normed.astype(m_buf.dtype)
        return carry

    lax.fori_loop(0, tiles, scale_rows, 0)
    own_sum = pltpu.make_async_copy(m_buf, sum_ref.at[cx, cc], local_sems.at[4])
    own_sum.start()
    own_sum.wait()
    ar_c = [
        ar_copy(xs - 1 + d, sum_ref.at[cx, cc], sum_ref.at[cx, cc], x_peers[d - 1])
        for d in range(1, xs)
    ]

    for (gkey, yy), (ukey, zz) in zip(
        (("y", y), ("ym", ym), ("yp", yp), ("y2", y2)),
        (("z", z), ("zm", zm), ("zp", zp), ("z2", z2)),
    ):
        from_zm, from_zp = gz[gkey]
        from_ym, from_yp = uy[ukey]
        from_zm.wait_recv()
        send(g_ref.at[zm, yy, low], g_ref.at[zm, yy, low], to(zp, y))
        from_ym.wait_recv()
        send(u_ref.at[zz, ym, low], u_ref.at[zz, ym, low], to(z, yp))
        from_zp.wait_recv()
        send(g_ref.at[zp, yy, high], g_ref.at[zp, yy, high], to(zm, y))
        from_yp.wait_recv()
        send(u_ref.at[zz, yp, high], u_ref.at[zz, yp, high], to(z, ym))

    for c in ar_c:
        c.wait_recv()
    ar_d = ar_copy(2 * xs - 1, sum_ref.at[:, cc], sum_ref.at[:, cc], core_peer)
    ar_d.wait_recv()
    for c in [ar_a] + ar_b + ar_c + [ar_d]:
        c.wait_send()

    waited = [g_from_ym, g_from_yp, u_from_zm, u_from_zp, g_far_a, g_far_b, u_far_a, u_far_b]
    waited += list(gz["y"]) + list(gz["ym"]) + list(gz["yp"]) + list(gz["y2"])
    waited += list(uy["z"]) + list(uy["zm"]) + list(uy["zp"]) + list(uy["z2"])
    for c in copies:
        if not any(c is w for w in waited):
            c.wait_recv()
    for c in copies:
        c.wait_send()
    for c in kv_copies:
        c.wait_recv()
        c.wait_send()
    own_g.wait()
    own_u.wait()
    own_kv.wait()


def gather_weights(w_gate, w_up, kv_send, attended, w_out, residual, gain):
    rows, cols = w_gate.shape
    xs, _, chunk, width = residual.shape
    product = jax.ShapeDtypeStruct(residual.shape, jnp.bfloat16)
    any_spec = pl.BlockSpec(memory_space=pl.ANY)
    vmem_spec = pl.BlockSpec(memory_space=pltpu.VMEM)
    piece = jax.ShapeDtypeStruct((RING, RING, rows, cols), w_gate.dtype)
    slots = jax.ShapeDtypeStruct(kv_send.shape, kv_send.dtype)
    sums = jax.ShapeDtypeStruct(product.shape, product.dtype)
    sems = KV_SEMS + kv_send.shape[0] - 1
    return pl.pallas_call(
        gather_kernel,
        out_shape=(piece, piece, slots, sums),
        in_specs=[any_spec] * 3 + [vmem_spec] * 2 + [any_spec] * 2,
        out_specs=(any_spec, any_spec, any_spec, any_spec),
        scratch_shapes=[
            pltpu.SemaphoreType.DMA((sems,)),
            pltpu.SemaphoreType.DMA((sems,)),
            pltpu.SemaphoreType.DMA((7,)),
            pltpu.SemaphoreType.DMA((2 * xs,)),
            pltpu.SemaphoreType.DMA((2 * xs,)),
            pltpu.VMEM((xs, chunk, width), product.dtype),
            pltpu.VMEM(product.shape, product.dtype),
            pltpu.VMEM((xs, chunk, width), product.dtype),
            pltpu.VMEM((xs, chunk, width), product.dtype),
            pltpu.VMEM((chunk, width), product.dtype),
            pltpu.VMEM((chunk, width), residual.dtype),
            pltpu.VMEM((1, width), jnp.float32),
            pltpu.VMEM((chunk, width), jnp.float32),
        ],
        compiler_params=pltpu.CompilerParams(
            collective_id=0, has_side_effects=True, vmem_limit_bytes=48 * 1024 * 1024
        ),
    )(w_gate, w_up, kv_send, attended, w_out, residual, gain)

def normalize(resid_rows, summed, gain_row):
    state = resid_rows.astype(jnp.float32) + summed
    scale_row = lax.rsqrt(jnp.mean(state * state, axis=-1, keepdims=True) + EPS)
    return (state * scale_row * gain_row).astype(jnp.bfloat16)


def shards(
    q_pre,
    k_pre,
    v_pre,
    q_bias,
    k_bias,
    v_bias,
    segment_ids,
    lengths,
    page_table,
    w_out,
    residual,
    norm_gain,
    w_gate,
    w_up,
):
    me_req = lax.axis_index("req")
    groups_all = lax.axis_size("req")
    block_rows = q_pre.shape[0]
    kv_heads = k_pre.shape[1] // HD
    q_heads = q_pre.shape[1] // HD
    group_size = q_heads // kv_heads


    own_lens = lax.dynamic_index_in_dim(lengths, me_req, 0, keepdims=False)
    own_pages = lax.dynamic_index_in_dim(page_table, me_req, 0, keepdims=False)
    own_owner = own_pages // REQS
    starts = jnp.cumsum(own_lens) - own_lens

    alive = segment_ids >= 0
    req_idx = jnp.clip(segment_ids - me_req * REQS, 0, REQS - 1)
    req_hit = req_idx[:, None] == jnp.arange(REQS)[None, :]
    row_start = jnp.sum(jnp.where(req_hit, starts[None, :], 0), axis=1)
    token = jnp.arange(block_rows, dtype=jnp.int32)
    positions = (token - row_start).astype(jnp.float32)
    keep = alive[:, None, None]

    queries = rotate(
        (q_pre.astype(jnp.float32) + q_bias).reshape(block_rows, q_heads, HD), positions
    )
    queries = jnp.where(keep, queries, 0.0).astype(jnp.bfloat16)
    keys = rotate((k_pre.astype(jnp.float32) + k_bias).reshape(block_rows, kv_heads, HD), positions)
    keys = jnp.where(keep, keys, 0.0).astype(jnp.bfloat16)
    values = (v_pre.astype(jnp.float32) + v_bias).reshape(block_rows, kv_heads, HD)
    values = jnp.where(keep, values, 0.0).astype(jnp.bfloat16)

    scale_factor = 1.0 / math.sqrt(HD)
    q_groups = queries.reshape(block_rows, kv_heads, group_size, HD)
    scores = (
        jnp.einsum("qhge,khe->hgqk", q_groups, keys, preferred_element_type=jnp.float32)
        * scale_factor
    )
    allowed = (
        (segment_ids[:, None] == segment_ids[None, :])
        & alive[None, :]
        & (token[None, :] <= token[:, None])
    )[None, None]
    row_max = jnp.max(jnp.where(allowed, scores, -1e30), axis=-1, keepdims=True)
    weights = jnp.where(allowed, jnp.exp(scores - row_max), 0.0)
    row_sum = jnp.sum(weights, axis=-1, keepdims=True)
    present = alive[None, None, :, None]
    probs = jnp.where(present, weights / jnp.where(present, row_sum, 1.0), 0.0).astype(
        jnp.bfloat16
    )
    attended = jnp.einsum("hgqk,khe->qhge", probs, values, preferred_element_type=jnp.float32)
    attended = attended.astype(jnp.bfloat16).reshape(block_rows, q_heads * HD)

    kv_rows = jnp.concatenate([keys, values], axis=-1).reshape(block_rows, -1)
    slot = jnp.arange(PAGE, dtype=jnp.int32)
    source = starts[:, None] + slot[None, :]
    live_slot = slot[None, :] < own_lens[:, None]
    select = (live_slot[:, :, None] & (source[:, :, None] == token[None, None, :])).astype(
        jnp.bfloat16
    )
    pages = jnp.einsum("jst,tc->jsc", select, kv_rows, preferred_element_type=jnp.float32)
    to_owner = (own_owner[None, :] == jnp.arange(groups_all)[:, None]).astype(jnp.bfloat16)
    kv_send = jnp.einsum(
        "gj,jsc->gsc", to_owner, pages.astype(jnp.bfloat16), preferred_element_type=jnp.float32
    ).astype(jnp.bfloat16)
    hits = (
        page_table[None, :, :] == (me_req * REQS + jnp.arange(REQS, dtype=jnp.int32))[:, None, None]
    )
    page_select = jnp.sum(hits.astype(jnp.int32), axis=2).astype(jnp.bfloat16)

    n_mp = lax.axis_size("mp")
    split_rows = (n_mp // 2, 2, block_rows // n_mp, residual.shape[-1])
    g_full, u_full, kv_in, normed = gather_weights(
        w_gate,
        w_up,
        kv_send,
        attended,
        w_out,
        residual.reshape(split_rows),
        norm_gain.reshape(1, -1).astype(jnp.float32),
    )
    normed = normed.reshape(block_rows, -1)
    kv_in = kv_in.reshape(groups_all, PAGE, kv_heads, 2 * HD)
    cache_out = jnp.einsum(
        "ls,sphc->lhpc", page_select, kv_in, preferred_element_type=jnp.float32
    ).astype(jnp.bfloat16)
    wg_full = g_full.reshape(-1, w_gate.shape[1])
    wu_full = u_full.reshape(-1, w_up.shape[1])
    gate_acc = jnp.dot(normed, wg_full, preferred_element_type=jnp.float32)
    up_acc = jnp.dot(normed, wu_full, preferred_element_type=jnp.float32)
    hidden = (jax.nn.silu(gate_acc) * up_acc).astype(jnp.bfloat16)
    return (hidden, cache_out)


def solution(mesh):
    in_specs = (
        P("req", "mp"),
        P("req", "mp"),
        P("req", "mp"),
        P("mp"),
        P("mp"),
        P("mp"),
        P("req"),
        P(),
        P(),
        P("mp", None),
        P("req", None),
        P(),
        P("req", "mp"),
        P("req", "mp"),
    )
    out_specs = (P("req", "mp"), P("req", "mp", None, None))
    return jax.shard_map(shards, mesh=mesh, in_specs=in_specs, out_specs=out_specs, check_vma=False)
```

```python
import math

import jax
import jax.numpy as jnp
from jax import lax
from jax.sharding import PartitionSpec as P
from jax.experimental import pallas as pl
from jax.experimental.pallas import tpu as pltpu

HD = 128
PAGE = 128
REQS = 4
RING = 4
KV_SEMS = 40
AR_TILE = 1024


THETA = 1000000.0
EPS = 1e-06


def rotate(values, positions):
    half_dim = values.shape[-1] // 2
    frequencies = THETA ** (-jnp.arange(half_dim, dtype=jnp.float32) * (2.0 / values.shape[-1]))
    angles = positions[:, None] * frequencies[None, :]
    cosine = jnp.cos(angles)[:, None, :]
    sine_part = jnp.sin(angles)[:, None, :]
    first_half = values[..., :half_dim]
    second = values[..., half_dim:]
    return jnp.concatenate(
        [first_half * cosine - second * sine_part, second * cosine + first_half * sine_part],
        axis=-1,
    )


def gather_kernel(
    wg_ref, wu_ref, kv_ref, att_ref, wout_ref, res_ref, gain_ref, g_ref, u_ref, kv_out, sum_ref,
    send_sems, recv_sems, local_sems, ar_send, ar_recv, a_buf, prod_v, b_src, b_buf, m_buf,
    r_buf, gain_buf, s_buf,
):
    me = lax.axis_index("req")
    col = lax.axis_index("mp")
    z = me // RING
    y = me % RING
    yp = (y + 1) % RING
    ym = (y + RING - 1) % RING
    y2 = (y + 2) % RING
    zp = (z + 1) % RING
    zm = (z + RING - 1) % RING
    z2 = (z + 2) % RING
    rows = wg_ref.shape[0]
    low = pl.ds(0, rows // 2)
    high = pl.ds(rows // 2, rows - rows // 2)
    mesh_id = pl.DeviceIdType.MESH

    def to(zz, yy):
        return (zz * RING + yy, col)

    groups = kv_ref.shape[0]
    xs = prod_v.shape[0]
    cx = col // 2
    cc = col % 2
    core_peer = (me, cx * 2 + 1 - cc)
    x_peers = [(me, ((cx + d) % xs) * 2 + cc) for d in range(1, xs)]

    barrier = pltpu.get_barrier_semaphore()
    for d in range(1, groups):
        peer = ((me + d) % groups, col)
        pl.semaphore_signal(barrier, inc=1, device_id=peer, device_id_type=mesh_id)
    for peer in [core_peer] + x_peers:
        pl.semaphore_signal(barrier, inc=1, device_id=peer, device_id_type=mesh_id)
    pl.semaphore_wait(barrier, groups - 1 + xs)

    def ar_copy(k, src, dst, peer):
        c = pltpu.make_async_remote_copy(
            src_ref=src,
            dst_ref=dst,
            send_sem=ar_send.at[k],
            recv_sem=ar_recv.at[k],
            device_id=peer,
            device_id_type=mesh_id,
        )
        c.start()
        return c

    r_load = pltpu.make_async_copy(res_ref.at[cx, cc], r_buf, local_sems.at[5])
    r_load.start()
    g_load = pltpu.make_async_copy(gain_ref, gain_buf, local_sems.at[6])
    g_load.start()
    width = AR_TILE
    tiles = a_buf.shape[-1] // width

    copies = []

    def send(src, dst, peer):
        k = len(copies)
        c = pltpu.make_async_remote_copy(
            src_ref=src,
            dst_ref=dst,
            send_sem=send_sems.at[k],
            recv_sem=recv_sems.at[k],
            device_id=peer,
            device_id_type=mesh_id,
        )
        c.start()
        copies.append(c)
        return c

    own_g = pltpu.make_async_copy(wg_ref, g_ref.at[z, y], local_sems.at[0])
    own_u = pltpu.make_async_copy(wu_ref, u_ref.at[z, y], local_sems.at[1])
    own_g.start()
    own_u.start()

    g_from_ym = send(wg_ref, g_ref.at[z, y], to(z, yp))
    g_from_yp = send(wg_ref, g_ref.at[z, y], to(z, ym))
    u_from_zm = send(wu_ref, u_ref.at[z, y], to(zp, y))
    u_from_zp = send(wu_ref, u_ref.at[z, y], to(zm, y))
    gz = {"y": (send(wg_ref, g_ref.at[z, y], to(zp, y)), send(wg_ref, g_ref.at[z, y], to(zm, y)))}
    uy = {"z": (send(wu_ref, u_ref.at[z, y], to(z, yp)), send(wu_ref, u_ref.at[z, y], to(z, ym)))}

    chunk = prod_v.shape[2]

    def project(k, carry):
        rows = att_ref[pl.ds(pl.multiple_of(k * chunk, chunk), chunk), :]
        part = jnp.dot(rows, wout_ref[...], preferred_element_type=jnp.float32)
        prod_v[k // 2, k % 2] = part.astype(prod_v.dtype)
        return carry

    lax.fori_loop(0, 2 * xs, project, 0)
    ar_a = ar_copy(0, prod_v.at[:, 1 - cc], a_buf, core_peer)

    ar_a.wait_recv()

    def add_pair(i, carry):
        xi = i // tiles
        cols = pl.ds(pl.multiple_of((i % tiles) * width, width), width)
        pair = prod_v[xi, cc, :, cols].astype(jnp.float32) + a_buf[xi, :, cols].astype(jnp.float32)
        b_src[xi, :, cols] = pair.astype(b_src.dtype)
        return carry

    lax.fori_loop(0, xs * tiles, add_pair, 0)
    ar_b = [
        ar_copy(d, b_src.at[(cx + d) % xs], b_buf.at[cx], x_peers[d - 1]) for d in range(1, xs)
    ]

    g_from_ym.wait_recv()
    g_far_a = send(g_ref.at[z, ym, low], g_ref.at[z, ym, low], to(z, yp))
    gz["ym"] = (send(g_ref.at[z, ym], g_ref.at[z, ym], to(zp, y)), send(g_ref.at[z, ym], g_ref.at[z, ym], to(zm, y)))
    u_from_zm.wait_recv()
    u_far_a = send(u_ref.at[zm, y, low], u_ref.at[zm, y, low], to(zp, y))
    uy["zm"] = (send(u_ref.at[zm, y], u_ref.at[zm, y], to(z, yp)), send(u_ref.at[zm, y], u_ref.at[zm, y], to(z, ym)))
    g_from_yp.wait_recv()
    g_far_b = send(g_ref.at[z, yp, high], g_ref.at[z, yp, high], to(z, ym))
    gz["yp"] = (send(g_ref.at[z, yp], g_ref.at[z, yp], to(zp, y)), send(g_ref.at[z, yp], g_ref.at[z, yp], to(zm, y)))
    u_from_zp.wait_recv()
    u_far_b = send(u_ref.at[zp, y, high], u_ref.at[zp, y, high], to(zm, y))
    uy["zp"] = (send(u_ref.at[zp, y], u_ref.at[zp, y], to(z, yp)), send(u_ref.at[zp, y], u_ref.at[zp, y], to(z, ym)))

    g_far_a.wait_recv()
    g_far_b.wait_recv()
    gz["y2"] = (send(g_ref.at[z, y2], g_ref.at[z, y2], to(zp, y)), send(g_ref.at[z, y2], g_ref.at[z, y2], to(zm, y)))
    u_far_a.wait_recv()
    u_far_b.wait_recv()
    uy["z2"] = (send(u_ref.at[z2, y], u_ref.at[z2, y], to(z, yp)), send(u_ref.at[z2, y], u_ref.at[z2, y], to(z, ym)))
    kv_copies = []
    own_kv = pltpu.make_async_copy(kv_ref.at[me], kv_out.at[me], local_sems.at[2])
    own_kv.start()
    for d in range(1, groups):
        dest = (me + d) % groups
        c = pltpu.make_async_remote_copy(
            src_ref=kv_ref.at[dest],
            dst_ref=kv_out.at[me],
            send_sem=send_sems.at[KV_SEMS + d - 1],
            recv_sem=recv_sems.at[KV_SEMS + d - 1],
            device_id=(dest, col),
            device_id_type=mesh_id,
        )
        c.start()
        kv_copies.append(c)

    for c in ar_b:
        c.wait_recv()

    r_load.wait()
    g_load.wait()

    def add_chips(t, squares):
        cols = pl.ds(pl.multiple_of(t * width, width), width)
        acc = b_src[cx, :, cols].astype(jnp.float32)
        for d in range(1, xs):
            acc = acc + b_buf[(cx + d) % xs, :, cols].astype(jnp.float32)
        state = acc + r_buf[:, cols].astype(jnp.float32)
        s_buf[:, cols] = state
        return squares + jnp.sum(state * state, axis=1, keepdims=True)

    squares = lax.fori_loop(0, tiles, add_chips, jnp.zeros((m_buf.shape[0], 1), jnp.float32))
    scale = lax.rsqrt(squares / m_buf.shape[1] + EPS)

    def scale_rows(t, carry):
        cols = pl.ds(pl.multiple_of(t * width, width), width)
        normed = s_buf[:, cols] * scale * gain_buf[:, cols]
        m_buf[:, cols] = normed.astype(m_buf.dtype)
        return carry

    lax.fori_loop(0, tiles, scale_rows, 0)
    own_sum = pltpu.make_async_copy(m_buf, sum_ref.at[cx, cc], local_sems.at[4])
    own_sum.start()
    own_sum.wait()
    ar_c = [
        ar_copy(xs - 1 + d, sum_ref.at[cx, cc], sum_ref.at[cx, cc], x_peers[d - 1])
        for d in range(1, xs)
    ]

    for (gkey, yy), (ukey, zz) in zip(
        (("y", y), ("ym", ym), ("yp", yp), ("y2", y2)),
        (("z", z), ("zm", zm), ("zp", zp), ("z2", z2)),
    ):
        from_zm, from_zp = gz[gkey]
        from_ym, from_yp = uy[ukey]
        from_zm.wait_recv()
        send(g_ref.at[zm, yy, low], g_ref.at[zm, yy, low], to(zp, y))
        from_ym.wait_recv()
        send(u_ref.at[zz, ym, low], u_ref.at[zz, ym, low], to(z, yp))
        from_zp.wait_recv()
        send(g_ref.at[zp, yy, high], g_ref.at[zp, yy, high], to(zm, y))
        from_yp.wait_recv()
        send(u_ref.at[zz, yp, high], u_ref.at[zz, yp, high], to(z, ym))

    for c in ar_c:
        c.wait_recv()
    ar_d = ar_copy(2 * xs - 1, sum_ref.at[:, cc], sum_ref.at[:, cc], core_peer)
    ar_d.wait_recv()
    for c in [ar_a] + ar_b + ar_c + [ar_d]:
        c.wait_send()

    waited = [g_from_ym, g_from_yp, u_from_zm, u_from_zp, g_far_a, g_far_b, u_far_a, u_far_b]
    waited += list(gz["y"]) + list(gz["ym"]) + list(gz["yp"]) + list(gz["y2"])
    waited += list(uy["z"]) + list(uy["zm"]) + list(uy["zp"]) + list(uy["z2"])
    for c in copies:
        if not any(c is w for w in waited):
            c.wait_recv()
    for c in copies:
        c.wait_send()
    for c in kv_copies:
        c.wait_recv()
        c.wait_send()
    own_g.wait()
    own_u.wait()
    own_kv.wait()


def gather_weights(w_gate, w_up, kv_send, attended, w_out, residual, gain):
    rows, cols = w_gate.shape
    xs, _, chunk, width = residual.shape
    product = jax.ShapeDtypeStruct(residual.shape, jnp.bfloat16)
    any_spec = pl.BlockSpec(memory_space=pl.ANY)
    vmem_spec = pl.BlockSpec(memory_space=pltpu.VMEM)
    piece = jax.ShapeDtypeStruct((RING, RING, rows, cols), w_gate.dtype)
    slots = jax.ShapeDtypeStruct(kv_send.shape, kv_send.dtype)
    sums = jax.ShapeDtypeStruct(product.shape, product.dtype)
    sems = KV_SEMS + kv_send.shape[0] - 1
    return pl.pallas_call(
        gather_kernel,
        out_shape=(piece, piece, slots, sums),
        in_specs=[any_spec] * 3 + [vmem_spec] * 2 + [any_spec] * 2,
        out_specs=(any_spec, any_spec, any_spec, any_spec),
        scratch_shapes=[
            pltpu.SemaphoreType.DMA((sems,)),
            pltpu.SemaphoreType.DMA((sems,)),
            pltpu.SemaphoreType.DMA((7,)),
            pltpu.SemaphoreType.DMA((2 * xs,)),
            pltpu.SemaphoreType.DMA((2 * xs,)),
            pltpu.VMEM((xs, chunk, width), product.dtype),
            pltpu.VMEM(product.shape, product.dtype),
            pltpu.VMEM((xs, chunk, width), product.dtype),
            pltpu.VMEM((xs, chunk, width), product.dtype),
            pltpu.VMEM((chunk, width), product.dtype),
            pltpu.VMEM((chunk, width), residual.dtype),
            pltpu.VMEM((1, width), jnp.float32),
            pltpu.VMEM((chunk, width), jnp.float32),
        ],
        compiler_params=pltpu.CompilerParams(
            collective_id=0, has_side_effects=True, vmem_limit_bytes=48 * 1024 * 1024
        ),
    )(w_gate, w_up, kv_send, attended, w_out, residual, gain)

def normalize(resid_rows, summed, gain_row):
    state = resid_rows.astype(jnp.float32) + summed
    scale_row = lax.rsqrt(jnp.mean(state * state, axis=-1, keepdims=True) + EPS)
    return (state * scale_row * gain_row).astype(jnp.bfloat16)


def shards(
    q_pre,
    k_pre,
    v_pre,
    q_bias,
    k_bias,
    v_bias,
    segment_ids,
    lengths,
    page_table,
    w_out,
    residual,
    norm_gain,
    w_gate,
    w_up,
):
    me_req = lax.axis_index("req")
    groups_all = lax.axis_size("req")
    block_rows = q_pre.shape[0]
    kv_heads = k_pre.shape[1] // HD
    q_heads = q_pre.shape[1] // HD
    group_size = q_heads // kv_heads


    own_lens = lax.dynamic_index_in_dim(lengths, me_req, 0, keepdims=False)
    own_pages = lax.dynamic_index_in_dim(page_table, me_req, 0, keepdims=False)
    own_owner = own_pages // REQS
    starts = jnp.cumsum(own_lens) - own_lens

    alive = segment_ids >= 0
    req_idx = jnp.clip(segment_ids - me_req * REQS, 0, REQS - 1)
    req_hit = req_idx[:, None] == jnp.arange(REQS)[None, :]
    row_start = jnp.sum(jnp.where(req_hit, starts[None, :], 0), axis=1)
    token = jnp.arange(block_rows, dtype=jnp.int32)
    positions = (token - row_start).astype(jnp.float32)
    keep = alive[:, None, None]

    queries = rotate(
        (q_pre.astype(jnp.float32) + q_bias).reshape(block_rows, q_heads, HD), positions
    )
    queries = jnp.where(keep, queries, 0.0).astype(jnp.bfloat16)
    keys = rotate((k_pre.astype(jnp.float32) + k_bias).reshape(block_rows, kv_heads, HD), positions)
    keys = jnp.where(keep, keys, 0.0).astype(jnp.bfloat16)
    values = (v_pre.astype(jnp.float32) + v_bias).reshape(block_rows, kv_heads, HD)
    values = jnp.where(keep, values, 0.0).astype(jnp.bfloat16)

    scale_factor = 1.0 / math.sqrt(HD)
    q_groups = queries.reshape(block_rows, kv_heads, group_size, HD)
    scores = (
        jnp.einsum("qhge,khe->hgqk", q_groups, keys, preferred_element_type=jnp.float32)
        * scale_factor
    )
    allowed = (
        (segment_ids[:, None] == segment_ids[None, :])
        & alive[None, :]
        & (token[None, :] <= token[:, None])
    )[None, None]
    row_max = jnp.max(jnp.where(allowed, scores, -1e30), axis=-1, keepdims=True)
    weights = jnp.where(allowed, jnp.exp(scores - row_max), 0.0)
    row_sum = jnp.sum(weights, axis=-1, keepdims=True)
    present = alive[None, None, :, None]
    probs = jnp.where(present, weights / jnp.where(present, row_sum, 1.0), 0.0).astype(
        jnp.bfloat16
    )
    attended = jnp.einsum("hgqk,khe->qhge", probs, values, preferred_element_type=jnp.float32)
    attended = attended.astype(jnp.bfloat16).reshape(block_rows, q_heads * HD)

    kv_rows = jnp.concatenate([keys, values], axis=-1).reshape(block_rows, -1)
    slot = jnp.arange(PAGE, dtype=jnp.int32)
    source = starts[:, None] + slot[None, :]
    live_slot = slot[None, :] < own_lens[:, None]
    select = (live_slot[:, :, None] & (source[:, :, None] == token[None, None, :])).astype(
        jnp.bfloat16
    )
    pages = jnp.einsum("jst,tc->jsc", select, kv_rows, preferred_element_type=jnp.float32)
    to_owner = (own_owner[None, :] == jnp.arange(groups_all)[:, None]).astype(jnp.bfloat16)
    kv_send = jnp.einsum(
        "gj,jsc->gsc", to_owner, pages.astype(jnp.bfloat16), preferred_element_type=jnp.float32
    ).astype(jnp.bfloat16)
    hits = (
        page_table[None, :, :] == (me_req * REQS + jnp.arange(REQS, dtype=jnp.int32))[:, None, None]
    )
    page_select = jnp.sum(hits.astype(jnp.int32), axis=2).astype(jnp.bfloat16)

    n_mp = lax.axis_size("mp")
    split_rows = (n_mp // 2, 2, block_rows // n_mp, residual.shape[-1])
    g_full, u_full, kv_in, normed = gather_weights(
        w_gate,
        w_up,
        kv_send,
        attended,
        w_out,
        residual.reshape(split_rows),
        norm_gain.reshape(1, -1).astype(jnp.float32),
    )
    normed = normed.reshape(block_rows, -1)
    kv_in = kv_in.reshape(groups_all, PAGE, kv_heads, 2 * HD)
    cache_out = jnp.einsum(
        "ls,sphc->lhpc", page_select, kv_in, preferred_element_type=jnp.float32
    ).astype(jnp.bfloat16)
    wg_full = g_full.reshape(-1, w_gate.shape[1])
    wu_full = u_full.reshape(-1, w_up.shape[1])
    gate_acc = jnp.dot(normed, wg_full, preferred_element_type=jnp.float32)
    up_acc = jnp.dot(normed, wu_full, preferred_element_type=jnp.float32)
    hidden = (jax.nn.silu(gate_acc) * up_acc).astype(jnp.bfloat16)
    return (hidden, cache_out)


def solution(mesh):
    in_specs = (
        P("req", "mp"),
        P("req", "mp"),
        P("req", "mp"),
        P("mp"),
        P("mp"),
        P("mp"),
        P("req"),
        P(),
        P(),
        P("mp", None),
        P("req", None),
        P(),
        P("req", "mp"),
        P("req", "mp"),
    )
    out_specs = (P("req", "mp"), P("req", "mp", None, None))
    return jax.shard_map(shards, mesh=mesh, in_specs=in_specs, out_specs=out_specs, check_vma=False)
```

```python
import math

import jax
import jax.numpy as jnp
from jax import lax
from jax.sharding import PartitionSpec as P
from jax.experimental import pallas as pl
from jax.experimental.pallas import tpu as pltpu

HD = 128
PAGE = 128
REQS = 4
RING = 4
KV_SEMS = 40
AR_TILE = 1280


THETA = 1000000.0
EPS = 1e-06


def rotate(values, positions):
    half_dim = values.shape[-1] // 2
    frequencies = THETA ** (-jnp.arange(half_dim, dtype=jnp.float32) * (2.0 / values.shape[-1]))
    angles = positions[:, None] * frequencies[None, :]
    cosine = jnp.cos(angles)[:, None, :]
    sine_part = jnp.sin(angles)[:, None, :]
    first_half = values[..., :half_dim]
    second = values[..., half_dim:]
    return jnp.concatenate(
        [first_half * cosine - second * sine_part, second * cosine + first_half * sine_part],
        axis=-1,
    )


def gather_kernel(
    wg_ref, wu_ref, kv_ref, att_ref, wout_ref, res_ref, gain_ref, g_ref, u_ref, kv_out, sum_ref,
    send_sems, recv_sems, local_sems, ar_send, ar_recv, a_buf, prod_v, b_src, b_buf, m_buf,
    r_buf, gain_buf, s_buf,
):
    me = lax.axis_index("req")
    col = lax.axis_index("mp")
    z = me // RING
    y = me % RING
    yp = (y + 1) % RING
    ym = (y + RING - 1) % RING
    y2 = (y + 2) % RING
    zp = (z + 1) % RING
    zm = (z + RING - 1) % RING
    z2 = (z + 2) % RING
    rows = wg_ref.shape[0]
    low = pl.ds(0, rows // 2)
    high = pl.ds(rows // 2, rows - rows // 2)
    mesh_id = pl.DeviceIdType.MESH

    def to(zz, yy):
        return (zz * RING + yy, col)

    groups = kv_ref.shape[0]
    xs = prod_v.shape[0]
    cx = col // 2
    cc = col % 2
    core_peer = (me, cx * 2 + 1 - cc)
    x_peers = [(me, ((cx + d) % xs) * 2 + cc) for d in range(1, xs)]

    barrier = pltpu.get_barrier_semaphore()
    for d in range(1, groups):
        peer = ((me + d) % groups, col)
        pl.semaphore_signal(barrier, inc=1, device_id=peer, device_id_type=mesh_id)
    for peer in [core_peer] + x_peers:
        pl.semaphore_signal(barrier, inc=1, device_id=peer, device_id_type=mesh_id)
    pl.semaphore_wait(barrier, groups - 1 + xs)

    def ar_copy(k, src, dst, peer):
        c = pltpu.make_async_remote_copy(
            src_ref=src,
            dst_ref=dst,
            send_sem=ar_send.at[k],
            recv_sem=ar_recv.at[k],
            device_id=peer,
            device_id_type=mesh_id,
        )
        c.start()
        return c

    r_load = pltpu.make_async_copy(res_ref.at[cx, cc], r_buf, local_sems.at[5])
    r_load.start()
    g_load = pltpu.make_async_copy(gain_ref, gain_buf, local_sems.at[6])
    g_load.start()
    width = AR_TILE
    tiles = a_buf.shape[-1] // width

    copies = []

    def send(src, dst, peer):
        k = len(copies)
        c = pltpu.make_async_remote_copy(
            src_ref=src,
            dst_ref=dst,
            send_sem=send_sems.at[k],
            recv_sem=recv_sems.at[k],
            device_id=peer,
            device_id_type=mesh_id,
        )
        c.start()
        copies.append(c)
        return c

    own_g = pltpu.make_async_copy(wg_ref, g_ref.at[z, y], local_sems.at[0])
    own_u = pltpu.make_async_copy(wu_ref, u_ref.at[z, y], local_sems.at[1])
    own_g.start()
    own_u.start()

    g_from_ym = send(wg_ref, g_ref.at[z, y], to(z, yp))
    g_from_yp = send(wg_ref, g_ref.at[z, y], to(z, ym))
    u_from_zm = send(wu_ref, u_ref.at[z, y], to(zp, y))
    u_from_zp = send(wu_ref, u_ref.at[z, y], to(zm, y))
    gz = {"y": (send(wg_ref, g_ref.at[z, y], to(zp, y)), send(wg_ref, g_ref.at[z, y], to(zm, y)))}
    uy = {"z": (send(wu_ref, u_ref.at[z, y], to(z, yp)), send(wu_ref, u_ref.at[z, y], to(z, ym)))}

    chunk = prod_v.shape[2]

    def project(k, carry):
        rows = att_ref[pl.ds(pl.multiple_of(k * chunk, chunk), chunk), :]
        part = jnp.dot(rows, wout_ref[...], preferred_element_type=jnp.float32)
        prod_v[k // 2, k % 2] = part.astype(prod_v.dtype)
        return carry

    lax.fori_loop(0, 2 * xs, project, 0)
    ar_a = ar_copy(0, prod_v.at[:, 1 - cc], a_buf, core_peer)

    ar_a.wait_recv()

    def add_pair(i, carry):
        xi = i // tiles
        cols = pl.ds(pl.multiple_of((i % tiles) * width, width), width)
        pair = prod_v[xi, cc, :, cols].astype(jnp.float32) + a_buf[xi, :, cols].astype(jnp.float32)
        b_src[xi, :, cols] = pair.astype(b_src.dtype)
        return carry

    lax.fori_loop(0, xs * tiles, add_pair, 0)
    ar_b = [
        ar_copy(d, b_src.at[(cx + d) % xs], b_buf.at[cx], x_peers[d - 1]) for d in range(1, xs)
    ]

    g_from_ym.wait_recv()
    g_far_a = send(g_ref.at[z, ym, low], g_ref.at[z, ym, low], to(z, yp))
    gz["ym"] = (send(g_ref.at[z, ym], g_ref.at[z, ym], to(zp, y)), send(g_ref.at[z, ym], g_ref.at[z, ym], to(zm, y)))
    u_from_zm.wait_recv()
    u_far_a = send(u_ref.at[zm, y, low], u_ref.at[zm, y, low], to(zp, y))
    uy["zm"] = (send(u_ref.at[zm, y], u_ref.at[zm, y], to(z, yp)), send(u_ref.at[zm, y], u_ref.at[zm, y], to(z, ym)))
    g_from_yp.wait_recv()
    g_far_b = send(g_ref.at[z, yp, high], g_ref.at[z, yp, high], to(z, ym))
    gz["yp"] = (send(g_ref.at[z, yp], g_ref.at[z, yp], to(zp, y)), send(g_ref.at[z, yp], g_ref.at[z, yp], to(zm, y)))
    u_from_zp.wait_recv()
    u_far_b = send(u_ref.at[zp, y, high], u_ref.at[zp, y, high], to(zm, y))
    uy["zp"] = (send(u_ref.at[zp, y], u_ref.at[zp, y], to(z, yp)), send(u_ref.at[zp, y], u_ref.at[zp, y], to(z, ym)))

    g_far_a.wait_recv()
    g_far_b.wait_recv()
    gz["y2"] = (send(g_ref.at[z, y2], g_ref.at[z, y2], to(zp, y)), send(g_ref.at[z, y2], g_ref.at[z, y2], to(zm, y)))
    u_far_a.wait_recv()
    u_far_b.wait_recv()
    uy["z2"] = (send(u_ref.at[z2, y], u_ref.at[z2, y], to(z, yp)), send(u_ref.at[z2, y], u_ref.at[z2, y], to(z, ym)))
    kv_copies = []
    own_kv = pltpu.make_async_copy(kv_ref.at[me], kv_out.at[me], local_sems.at[2])
    own_kv.start()
    for d in range(1, groups):
        dest = (me + d) % groups
        c = pltpu.make_async_remote_copy(
            src_ref=kv_ref.at[dest],
            dst_ref=kv_out.at[me],
            send_sem=send_sems.at[KV_SEMS + d - 1],
            recv_sem=recv_sems.at[KV_SEMS + d - 1],
            device_id=(dest, col),
            device_id_type=mesh_id,
        )
        c.start()
        kv_copies.append(c)

    for c in ar_b:
        c.wait_recv()

    r_load.wait()
    g_load.wait()

    def add_chips(t, squares):
        cols = pl.ds(pl.multiple_of(t * width, width), width)
        acc = b_src[cx, :, cols].astype(jnp.float32)
        for d in range(1, xs):
            acc = acc + b_buf[(cx + d) % xs, :, cols].astype(jnp.float32)
        state = acc + r_buf[:, cols].astype(jnp.float32)
        s_buf[:, cols] = state
        return squares + jnp.sum(state * state, axis=1, keepdims=True)

    squares = lax.fori_loop(0, tiles, add_chips, jnp.zeros((m_buf.shape[0], 1), jnp.float32))
    scale = lax.rsqrt(squares / m_buf.shape[1] + EPS)

    def scale_rows(t, carry):
        cols = pl.ds(pl.multiple_of(t * width, width), width)
        normed = s_buf[:, cols] * scale * gain_buf[:, cols]
        m_buf[:, cols] = normed.astype(m_buf.dtype)
        return carry

    lax.fori_loop(0, tiles, scale_rows, 0)
    own_sum = pltpu.make_async_copy(m_buf, sum_ref.at[cx, cc], local_sems.at[4])
    own_sum.start()
    own_sum.wait()
    ar_c = [
        ar_copy(xs - 1 + d, sum_ref.at[cx, cc], sum_ref.at[cx, cc], x_peers[d - 1])
        for d in range(1, xs)
    ]

    for (gkey, yy), (ukey, zz) in zip(
        (("y", y), ("ym", ym), ("yp", yp), ("y2", y2)),
        (("z", z), ("zm", zm), ("zp", zp), ("z2", z2)),
    ):
        from_zm, from_zp = gz[gkey]
        from_ym, from_yp = uy[ukey]
        from_zm.wait_recv()
        send(g_ref.at[zm, yy, low], g_ref.at[zm, yy, low], to(zp, y))
        from_ym.wait_recv()
        send(u_ref.at[zz, ym, low], u_ref.at[zz, ym, low], to(z, yp))
        from_zp.wait_recv()
        send(g_ref.at[zp, yy, high], g_ref.at[zp, yy, high], to(zm, y))
        from_yp.wait_recv()
        send(u_ref.at[zz, yp, high], u_ref.at[zz, yp, high], to(z, ym))

    for c in ar_c:
        c.wait_recv()
    ar_d = ar_copy(2 * xs - 1, sum_ref.at[:, cc], sum_ref.at[:, cc], core_peer)
    ar_d.wait_recv()
    for c in [ar_a] + ar_b + ar_c + [ar_d]:
        c.wait_send()

    waited = [g_from_ym, g_from_yp, u_from_zm, u_from_zp, g_far_a, g_far_b, u_far_a, u_far_b]
    waited += list(gz["y"]) + list(gz["ym"]) + list(gz["yp"]) + list(gz["y2"])
    waited += list(uy["z"]) + list(uy["zm"]) + list(uy["zp"]) + list(uy["z2"])
    for c in copies:
        if not any(c is w for w in waited):
            c.wait_recv()
    for c in copies:
        c.wait_send()
    for c in kv_copies:
        c.wait_recv()
        c.wait_send()
    own_g.wait()
    own_u.wait()
    own_kv.wait()


def gather_weights(w_gate, w_up, kv_send, attended, w_out, residual, gain):
    rows, cols = w_gate.shape
    xs, _, chunk, width = residual.shape
    product = jax.ShapeDtypeStruct(residual.shape, jnp.bfloat16)
    any_spec = pl.BlockSpec(memory_space=pl.ANY)
    vmem_spec = pl.BlockSpec(memory_space=pltpu.VMEM)
    piece = jax.ShapeDtypeStruct((RING, RING, rows, cols), w_gate.dtype)
    slots = jax.ShapeDtypeStruct(kv_send.shape, kv_send.dtype)
    sums = jax.ShapeDtypeStruct(product.shape, product.dtype)
    sems = KV_SEMS + kv_send.shape[0] - 1
    return pl.pallas_call(
        gather_kernel,
        out_shape=(piece, piece, slots, sums),
        in_specs=[any_spec] * 3 + [vmem_spec] * 2 + [any_spec] * 2,
        out_specs=(any_spec, any_spec, any_spec, any_spec),
        scratch_shapes=[
            pltpu.SemaphoreType.DMA((sems,)),
            pltpu.SemaphoreType.DMA((sems,)),
            pltpu.SemaphoreType.DMA((7,)),
            pltpu.SemaphoreType.DMA((2 * xs,)),
            pltpu.SemaphoreType.DMA((2 * xs,)),
            pltpu.VMEM((xs, chunk, width), product.dtype),
            pltpu.VMEM(product.shape, product.dtype),
            pltpu.VMEM((xs, chunk, width), product.dtype),
            pltpu.VMEM((xs, chunk, width), product.dtype),
            pltpu.VMEM((chunk, width), product.dtype),
            pltpu.VMEM((chunk, width), residual.dtype),
            pltpu.VMEM((1, width), jnp.float32),
            pltpu.VMEM((chunk, width), jnp.float32),
        ],
        compiler_params=pltpu.CompilerParams(
            collective_id=0, has_side_effects=True, vmem_limit_bytes=48 * 1024 * 1024
        ),
    )(w_gate, w_up, kv_send, attended, w_out, residual, gain)

def normalize(resid_rows, summed, gain_row):
    state = resid_rows.astype(jnp.float32) + summed
    scale_row = lax.rsqrt(jnp.mean(state * state, axis=-1, keepdims=True) + EPS)
    return (state * scale_row * gain_row).astype(jnp.bfloat16)


def shards(
    q_pre,
    k_pre,
    v_pre,
    q_bias,
    k_bias,
    v_bias,
    segment_ids,
    lengths,
    page_table,
    w_out,
    residual,
    norm_gain,
    w_gate,
    w_up,
):
    me_req = lax.axis_index("req")
    groups_all = lax.axis_size("req")
    block_rows = q_pre.shape[0]
    kv_heads = k_pre.shape[1] // HD
    q_heads = q_pre.shape[1] // HD
    group_size = q_heads // kv_heads


    own_lens = lax.dynamic_index_in_dim(lengths, me_req, 0, keepdims=False)
    own_pages = lax.dynamic_index_in_dim(page_table, me_req, 0, keepdims=False)
    own_owner = own_pages // REQS
    starts = jnp.cumsum(own_lens) - own_lens

    alive = segment_ids >= 0
    req_idx = jnp.clip(segment_ids - me_req * REQS, 0, REQS - 1)
    req_hit = req_idx[:, None] == jnp.arange(REQS)[None, :]
    row_start = jnp.sum(jnp.where(req_hit, starts[None, :], 0), axis=1)
    token = jnp.arange(block_rows, dtype=jnp.int32)
    positions = (token - row_start).astype(jnp.float32)
    keep = alive[:, None, None]

    queries = rotate(
        (q_pre.astype(jnp.float32) + q_bias).reshape(block_rows, q_heads, HD), positions
    )
    queries = jnp.where(keep, queries, 0.0).astype(jnp.bfloat16)
    keys = rotate((k_pre.astype(jnp.float32) + k_bias).reshape(block_rows, kv_heads, HD), positions)
    keys = jnp.where(keep, keys, 0.0).astype(jnp.bfloat16)
    values = (v_pre.astype(jnp.float32) + v_bias).reshape(block_rows, kv_heads, HD)
    values = jnp.where(keep, values, 0.0).astype(jnp.bfloat16)

    scale_factor = 1.0 / math.sqrt(HD)
    q_groups = queries.reshape(block_rows, kv_heads, group_size, HD)
    scores = (
        jnp.einsum("qhge,khe->hgqk", q_groups, keys, preferred_element_type=jnp.float32)
        * scale_factor
    )
    allowed = (
        (segment_ids[:, None] == segment_ids[None, :])
        & alive[None, :]
        & (token[None, :] <= token[:, None])
    )[None, None]
    row_max = jnp.max(jnp.where(allowed, scores, -1e30), axis=-1, keepdims=True)
    weights = jnp.where(allowed, jnp.exp(scores - row_max), 0.0)
    row_sum = jnp.sum(weights, axis=-1, keepdims=True)
    present = alive[None, None, :, None]
    probs = jnp.where(present, weights / jnp.where(present, row_sum, 1.0), 0.0).astype(
        jnp.bfloat16
    )
    attended = jnp.einsum("hgqk,khe->qhge", probs, values, preferred_element_type=jnp.float32)
    attended = attended.astype(jnp.bfloat16).reshape(block_rows, q_heads * HD)

    kv_rows = jnp.concatenate([keys, values], axis=-1).reshape(block_rows, -1)
    slot = jnp.arange(PAGE, dtype=jnp.int32)
    source = starts[:, None] + slot[None, :]
    live_slot = slot[None, :] < own_lens[:, None]
    select = (live_slot[:, :, None] & (source[:, :, None] == token[None, None, :])).astype(
        jnp.bfloat16
    )
    pages = jnp.einsum("jst,tc->jsc", select, kv_rows, preferred_element_type=jnp.float32)
    to_owner = (own_owner[None, :] == jnp.arange(groups_all)[:, None]).astype(jnp.bfloat16)
    kv_send = jnp.einsum(
        "gj,jsc->gsc", to_owner, pages.astype(jnp.bfloat16), preferred_element_type=jnp.float32
    ).astype(jnp.bfloat16)
    hits = (
        page_table[None, :, :] == (me_req * REQS + jnp.arange(REQS, dtype=jnp.int32))[:, None, None]
    )
    page_select = jnp.sum(hits.astype(jnp.int32), axis=2).astype(jnp.bfloat16)

    n_mp = lax.axis_size("mp")
    split_rows = (n_mp // 2, 2, block_rows // n_mp, residual.shape[-1])
    g_full, u_full, kv_in, normed = gather_weights(
        w_gate,
        w_up,
        kv_send,
        attended,
        w_out,
        residual.reshape(split_rows),
        norm_gain.reshape(1, -1).astype(jnp.float32),
    )
    normed = normed.reshape(block_rows, -1)
    kv_in = kv_in.reshape(groups_all, PAGE, kv_heads, 2 * HD)
    cache_out = jnp.einsum(
        "ls,sphc->lhpc", page_select, kv_in, preferred_element_type=jnp.float32
    ).astype(jnp.bfloat16)
    wg_full = g_full.reshape(-1, w_gate.shape[1])
    wu_full = u_full.reshape(-1, w_up.shape[1])
    gate_acc = jnp.dot(normed, wg_full, preferred_element_type=jnp.float32)
    up_acc = jnp.dot(normed, wu_full, preferred_element_type=jnp.float32)
    hidden = (jax.nn.silu(gate_acc) * up_acc).astype(jnp.bfloat16)
    return (hidden, cache_out)


def solution(mesh):
    in_specs = (
        P("req", "mp"),
        P("req", "mp"),
        P("req", "mp"),
        P("mp"),
        P("mp"),
        P("mp"),
        P("req"),
        P(),
        P(),
        P("mp", None),
        P("req", None),
        P(),
        P("req", "mp"),
        P("req", "mp"),
    )
    out_specs = (P("req", "mp"), P("req", "mp", None, None))
    return jax.shard_map(shards, mesh=mesh, in_specs=in_specs, out_specs=out_specs, check_vma=False)
```
